32 devices in a mesh: groups: 2 (over y), seq: 4 (over z), mp: 2 (over x), section: 2 (over core).
Axes of the slice: x: 2, y: 2, z: 4, core: 2. Of those that a mesh axis runs over, the one named last changes fastest.
Arguments:
- readout: bfloat16 [8, 64, 32, 1024], P(('groups', 'mp', 'section'), None, 'seq'), parts along dimension 0, may hold values from -6 to 6
- first_kernel: bfloat16 [3, 3, 64, 128], replicated, may hold values from -0.25 to 0.25
- second_kernel: bfloat16 [3, 3, 128, 256], replicated, may hold values from -0.1875 to 0.1875
- embed_weight: bfloat16 [1024, 768], P(('mp', 'section')), may hold values from -0.1875 to 0.1875
- project_weight: bfloat16 [768, 2304], P(('mp', 'section'))
- output_weight: bfloat16 [768, 768], P(('mp', 'section')), may hold values from -0.4375 to 0.4375
- order: int32 [8, 512], P(('groups', 'mp', 'section')), parts along dimension 0, may hold values from 0 to 511, as said below
- active: int32 [8, 512], P(('groups', 'mp', 'section'), 'seq'), parts along dimension 0, may hold values 0 or 1
Outputs:
- encoded: bfloat16 [8, 512, 768], P(('groups', 'mp', 'section'), 'seq'), parts along dimension 0
The draws below stay inside these ranges and needn't reach their ends.
There are 2 independent parts, one for each index of `groups`. The reference program is written for one: setup_inputs(seed, part) draws one part's arguments, and reference() takes and returns one part's arrays. A program takes and returns all parts, laid end to end along the dimension named above; an argument that names none is the same for every part. Nothing has to cross between parts.
Inputs may be any that keep to these rules, and one draw needn't show every extreme that they name: Each row of order lists each of the 512 patches of its region once. Patch i comes from the wire tile i // 128; each block of 128 positions k * 128 to (k + 1) * 128 - 1 holds exactly 32 patches of every wire tile.
All inputs are finite; a program needn't handle non-finite values. No bound on the sum of `active` on one device may be relied on, other than what follows from the above.
Results may differ from the reference program's by a relative error of at most 0.017.
Values may be sent and summed in bfloat16 or wider, within the bound.
No kernel may reach another device: no remote copies, remote signals or barrier semaphores. Data moves between devices by JAX's collectives and lax.ppermute only.
A program may use at most 64 MiB of HBM per device.

```python
import jax
import jax.numpy as jnp
from jax import lax

D = 768
HEADS = 12
C_IN = 64
C_MID = 128
C_OUT = 256
TICKS = 1024
HEAD_DIM = 64
PATCH_DIM = 1024
TOK_DEV = 128
SEQ_LEN = 512
GROUP = 32
REGIONS = 4
WIRES = 32
N_SEQ = 4


def draw_project_weight(key, part):
    first_key = jax.random.fold_in(key, 11)
    result = jax.random.normal(first_key, (D, 3 * D), jnp.float32) * (2.0 / D) ** 0.5
    return result.astype(jnp.bfloat16)


def draw_order(key, part):
    sources = SEQ_LEN // TOK_DEV
    first_key = jax.random.fold_in(key, 21)
    second_key = jax.random.fold_in(key, 22)
    local = jnp.broadcast_to(jnp.arange(TOK_DEV, dtype=jnp.int32), (REGIONS, sources, TOK_DEV))
    shuffled = jax.random.permutation(first_key, local, axis=2, independent=True)
    labels = shuffled + (jnp.arange(sources, dtype=jnp.int32) * TOK_DEV)[None, :, None]
    labels = labels.reshape(REGIONS, sources, sources, GROUP).transpose(0, 2, 1, 3).reshape(REGIONS, sources, TOK_DEV)
    labels = jax.random.permutation(second_key, labels, axis=2, independent=True)
    return labels.reshape(REGIONS, SEQ_LEN).astype(jnp.int32)


def set_ends(values, own_key, smallest, top_value):
    extent = values.shape
    index_at = [jax.random.randint(jax.random.fold_in(own_key, axis), (), 0, extent[axis]) for axis in range(len(extent))]
    values = values.at[tuple(index_at)].set(smallest)
    longest = extent.index(max(extent))
    index_at[longest] = (index_at[longest] + 1) % extent[longest]
    return values.at[tuple(index_at)].set(top_value)


def block_levels(stream_key, extent, pieces, low, largest):
    def one(dim, blocks):
        draws = jax.random.uniform(jax.random.fold_in(jax.random.fold_in(stream_key, 6), dim), (blocks,), jnp.float32, low / len(pieces), largest / len(pieces))
        return jnp.repeat(jnp.exp(draws), extent[dim] // blocks).reshape((-1,) + (1,) * (len(extent) - dim - 1))

    factor_of = one(*pieces[0])
    for cut in pieces[1:]:
        factor_of = factor_of * one(*cut)
    return factor_of


def bell_draw(stream_key, dims, scale, reach, split=(), held_as=jnp.bfloat16):
    values = jax.random.normal(stream_key, dims, jnp.float32) * scale
    if len(split) > 0:
        values = block_levels(stream_key, dims, split, -0.22, 0.18) * values
    return jnp.clip(values, min=-reach, max=reach).astype(held_as)


def setup_inputs(seed: int = 0, part: int = 0) -> dict:
    splits = jax.random.split(jax.random.key(seed), 9)
    part_keys = jax.random.split(jax.random.fold_in(splits[8], part), 9)
    return {
        "readout": bell_draw(part_keys[0], (REGIONS, C_IN, WIRES, TICKS), 1.0, 6.0, ((0, 4), (2, 4))),
        "first_kernel": bell_draw(splits[1], (3, 3, C_IN, C_MID), (9 * C_IN) ** -0.5, 0.25),
        "second_kernel": bell_draw(splits[2], (3, 3, C_MID, C_OUT), (9 * C_MID) ** -0.5, 0.1875),
        "embed_weight": bell_draw(splits[3], (PATCH_DIM, D), PATCH_DIM ** -0.5, 0.1875, ((0, 4),)),
        "project_weight": draw_project_weight(jax.random.fold_in(splits[8], 71), part),
        "output_weight": bell_draw(splits[5], (D, D), (D // 4) ** -0.5, 0.4375, ((0, 4),)),
        "order": draw_order(jax.random.fold_in(jax.random.fold_in(splits[8], part), 71), part),
        "active": set_ends((jax.random.randint(part_keys[7], (REGIONS, SEQ_LEN), 0, 4) < 3).astype(jnp.int32), jax.random.fold_in(part_keys[7], 1), 0, 1),
    }


masked_score = -1e+30
epsilon = 1e-05

def strided_conv(picture, kernel):
    result = lax.conv_general_dilated(picture[None], kernel, (2, 2), ((1, 1), (1, 1)), dimension_numbers=('NCHW', 'HWIO', 'NCHW'), preferred_element_type=jnp.float32)[0]
    return jax.nn.silu(result).astype(jnp.bfloat16)

def normalize(tokens):
    values = tokens.astype(jnp.float32)
    center = lax.optimization_barrier(jnp.mean(values, axis=-1, keepdims=True))
    spread = lax.optimization_barrier(jnp.mean(jnp.square(values - center), axis=-1, keepdims=True))
    return ((values - center) * lax.rsqrt(spread + epsilon)).astype(jnp.bfloat16)

def reference(readout, first_kernel, second_kernel, embed_weight, project_weight, output_weight, order, active):

    def region(inputs):
        picture, sequence, flags = inputs
        first = strided_conv(picture, first_kernel)
        second = strided_conv(first, second_kernel)
        grid = second.reshape(C_OUT, WIRES // 8, 2, TICKS // 8, 2)
        patches = grid.transpose(1, 3, 0, 2, 4).reshape(SEQ_LEN, PATCH_DIM)
        placed = jnp.take(patches, sequence, axis=0)
        tokens = jnp.dot(placed, embed_weight, preferred_element_type=jnp.float32).astype(jnp.bfloat16)
        normed = normalize(tokens)
        projected = jnp.dot(normed, project_weight, preferred_element_type=jnp.float32)
        queries = (projected[:, :D] * HEAD_DIM ** (-0.5)).astype(jnp.bfloat16)
        keys_all = projected[:, D:2 * D].astype(jnp.bfloat16).reshape(SEQ_LEN, HEADS, HEAD_DIM).astype(jnp.float32)
        values_all = projected[:, 2 * D:].astype(jnp.bfloat16).reshape(SEQ_LEN, HEADS, HEAD_DIM).astype(jnp.float32)
        keep = flags > 0
        positions = jnp.arange(SEQ_LEN, dtype=jnp.int32)

        def attend(block):
            query_block, query_pos = block
            scores = jnp.einsum('qhd,khd->qhk', query_block.astype(jnp.float32), keys_all)
            allowed = (keep[None, :] | (positions[None, :] == query_pos[:, None]))[:, None, :]
            scores = jnp.where(allowed, scores, masked_score)
            rowmax = lax.optimization_barrier(jnp.max(scores, axis=-1))
            weights = jnp.where(allowed, jnp.exp(scores - rowmax[..., None]), 0.0)
            total = lax.optimization_barrier(jnp.sum(weights, axis=-1))
            rounded = lax.optimization_barrier(weights.astype(jnp.bfloat16)).astype(jnp.float32)
            mixed = jnp.einsum('qhk,khd->qhd', rounded, values_all) / total[..., None]
            return mixed.astype(jnp.bfloat16).reshape(TOK_DEV, D)
        query_blocks = queries.reshape(N_SEQ, TOK_DEV, HEADS, HEAD_DIM)
        mixed = lax.map(attend, (query_blocks, positions.reshape(N_SEQ, TOK_DEV))).reshape(SEQ_LEN, D)
        result = tokens.astype(jnp.float32) + jnp.dot(mixed, output_weight, preferred_element_type=jnp.float32)
        return result.astype(jnp.bfloat16)
    return lax.map(region, (readout, order, active))
```

```python
import functools

import jax
import jax.numpy as jnp
from jax import lax
from jax.experimental import pallas as pl
from jax.experimental.pallas import tpu as pltpu
from jax.sharding import PartitionSpec as P

HEADS = 12
masked_score = -1e30
epsilon = 1e-05
BF = jnp.bfloat16
F32 = jnp.float32
EXTRA = 8


def dot(a, b, ca=1, cb=0):
    return lax.dot_general(a, b, (((ca,), (cb,)), ((), ())), preferred_element_type=F32)


def iota(shape, axis):
    return lax.broadcasted_iota(jnp.int32, shape, axis)


def one_hot(mask):
    return jnp.where(mask, 1.0, 0.0).astype(BF)


def silu(v):
    half = 0.5 * v
    return half + half * jnp.tanh(half)


def split_matrix():
    row, col = iota((256, 256), 0), iota((256, 256), 1)
    return one_hot(row == jnp.where(col < 128, 2 * col, 2 * col - 255))


def split_time(rows, splitter):
    even, odd = [], []
    for start in range(0, rows.shape[1], 256):
        both = dot(rows[:, start : start + 256], splitter)
        even.append(both[:, :128])
        odd.append(both[:, 128:])
    if len(even) == 1:
        return even[0], odd[0]
    return jnp.concatenate(even, axis=1), jnp.concatenate(odd, axis=1)


def later(odd):
    moved = pltpu.roll(odd, 1, 1)
    return jnp.where(iota(odd.shape, 1) == 0, 0.0, moved)


def store_taps(taps, base, even, odd):
    height = even.shape[0]
    taps[base : base + height, :] = later(odd).astype(BF)
    taps[base + height : base + 2 * height, :] = even.astype(BF)
    taps[base + 2 * height : base + 3 * height, :] = odd.astype(BF)


def front_kernel(x_ref, k1_ref, msg_ref, taps1_ref, taps2_ref, all1, *, wires, channels, middle):
    splitter = split_matrix()
    row, col = iota((256, 256), 0), iota((256, 256), 1)
    part = 256 // wires
    mixer = one_hot(col == (row % part) * wires + row // part)
    for block in range(channels // part):
        rows = dot(mixer, x_ref[block * 256 : (block + 1) * 256, :]).astype(BF)
        even, odd = split_time(rows, splitter)
        lagged = later(odd)
        for wire in range(wires):
            here = slice(wire * part, (wire + 1) * part)
            base = wire * 3 * channels + block * part
            all1[base : base + part, :] = lagged[here].astype(BF)
            all1[base + channels : base + channels + part, :] = even[here].astype(BF)
            all1[base + 2 * channels : base + 2 * channels + part, :] = odd[here].astype(BF)
    taps1_ref[...] = all1[: 6 * channels, :]
    last = (wires - 1) * 3 * channels
    msg_ref[: 2 * channels, :] = all1[last + channels : last + 3 * channels, :]
    k1 = k1_ref[...]
    for level in range(1, wires // 2):
        start = (2 * level - 1) * 3 * channels
        out = silu(dot(k1, all1[start : start + 9 * channels, :], 0, 0)).astype(BF)
        if level == wires // 2 - 1:
            msg_ref[2 * channels :, :] = out
        even, odd = split_time(out, splitter)
        store_taps(taps2_ref, (level - 1) * 3 * middle, even, odd)


def back_kernel(
    block_ref, got_ref, taps1_ref, taps2_ref, k1_ref, k2_ref, active_ref, *refs, channels, middle, pieces
):
    embed_refs = refs[:pieces]
    out_ref, all1, all2, patch = refs[pieces:]
    splitter = split_matrix()
    length = got_ref.shape[1]
    odd = got_ref[channels : 2 * channels, :].astype(F32)
    all1[:channels, :] = later(odd).astype(BF)
    all1[channels : 3 * channels, :] = got_ref[: 2 * channels, :]
    all1[3 * channels :, :] = taps1_ref[...]
    first = silu(dot(k1_ref[...], all1[...], 0, 0)).astype(BF)
    even, odd = split_time(got_ref[2 * channels :, :], splitter)
    store_taps(all2, 0, even, odd)
    even, odd = split_time(first, splitter)
    store_taps(all2, 3 * middle, even, odd)
    rest = taps2_ref.shape[0]
    all2[6 * middle : 6 * middle + rest, :] = taps2_ref[...]
    k2 = k2_ref[...]
    outer = k2.shape[1]
    halves = []
    for level in range(2):
        start = level * 6 * middle
        out = silu(dot(k2, all2[start : start + 9 * middle, :], 0, 0)).astype(BF)
        even, odd = split_time(out, splitter)
        halves += [even.astype(BF), odd.astype(BF)]
    row, col = iota((256, 256), 0), iota((256, 256), 1)
    mixer = one_hot(col == (row % 4) * 64 + row // 4)
    for block in range(outer // 64):
        rows = jnp.concatenate([h[block * 64 : (block + 1) * 64] for h in halves], axis=0)
        patch[block * 256 : (block + 1) * 256, :] = dot(mixer, rows).astype(BF)
    total = None
    for piece, ref in enumerate(embed_refs):
        depth = ref.shape[0]
        base = pl.multiple_of(block_ref[piece] * depth, depth)
        term = dot(patch[pl.ds(base, depth), :], ref[...], 0, 0)
        total = term if total is None else total + term
    count, width = total.shape
    out_ref[:count, :] = total.astype(BF)
    tail = jnp.broadcast_to(active_ref[...].astype(F32), (EXTRA, count))
    tail = jnp.concatenate([tail, jnp.zeros((EXTRA, width - count), F32)], axis=1)
    out_ref[count:, :] = tail.astype(BF)


def attend_kernel(block_ref, got_ref, order_ref, *refs, pieces, shards, count):
    project_refs = refs[:pieces]
    output_refs = refs[pieces : 2 * pieces]
    out_ref, project, output, normed, tokens, keys, values, mixed, keep, sems = refs[2 * pieces :]
    copies = []
    for kind, (pieces_refs, target) in enumerate(((project_refs, project), (output_refs, output))):
        for piece, ref in enumerate(pieces_refs):
            depth = ref.shape[0]
            base = pl.multiple_of(block_ref[piece] * depth, depth)
            copy = pltpu.make_async_copy(ref, target.at[pl.ds(base, depth), :], sems.at[kind, piece])
            copy.start()
            copies.append(copy)
    width = got_ref.shape[1]
    size = shards * count
    stride = count + EXTRA
    for shard in range(shards):
        piece = got_ref[shard * stride : shard * stride + count, :]
        here = slice(shard * count, (shard + 1) * count)
        tokens[here, :] = piece
        value = piece.astype(F32)
        center = jnp.mean(value, axis=-1, keepdims=True)
        value = value - center
        spread = jnp.mean(value * value, axis=-1, keepdims=True)
        normed[here, :] = (value * lax.rsqrt(spread + epsilon)).astype(BF)
    square = iota((count, count), 0) == iota((count, count), 1)
    labels = iota((count, size), 1).astype(F32)

    def placed(row):
        across = jnp.broadcast_to(row.astype(F32), (count, count))
        down = jnp.sum(jnp.where(square, across, 0.0), axis=1, keepdims=True)
        return labels == down

    on = jnp.zeros((EXTRA, size), F32)
    for shard in range(shards):
        flags = got_ref[shard * stride + count : (shard + 1) * stride, :count]
        on += dot(flags, one_hot(placed(order_ref[shard : shard + 1, :])))
    position = block_ref[pieces]
    own = placed(order_ref[pl.ds(position, 1), :])
    select = one_hot(own)
    keep[...] = jnp.where(own | jnp.broadcast_to(on[:1] > 0.5, (count, size)), 1.0, 0.0)
    token_own = dot(select, tokens[...])
    normed_own = dot(select, normed[...]).astype(BF)
    for copy in copies[:pieces]:
        copy.wait()
    head = width // HEADS
    queries = (dot(normed_own, project[:, :width]) * head ** (-0.5)).astype(BF)
    keys[...] = dot(normed[...], project[:, width : 2 * width]).astype(BF)
    values[...] = dot(normed[...], project[:, 2 * width :]).astype(BF)
    for index in range(HEADS):
        here = slice(index * head, (index + 1) * head)
        scores = dot(queries[:, here], keys[:, here], 1, 1)
        allowed = keep[...] > 0.5
        scores = jnp.where(allowed, scores, masked_score)
        top = jnp.max(scores, axis=-1, keepdims=True)
        weights = jnp.exp(scores - top)
        total = jnp.sum(weights, axis=-1, keepdims=True)
        part = dot(weights.astype(BF), values[:, here]) / total
        mixed[:, here] = part.astype(BF)
    for copy in copies[pieces:]:
        copy.wait()
    out_ref[...] = (token_own + dot(mixed[...], output[...])).astype(BF)


def vmem():
    return pl.BlockSpec(memory_space=pltpu.VMEM)


def smem():
    return pl.BlockSpec(memory_space=pltpu.SMEM)


def hbm():
    return pl.BlockSpec(memory_space=pl.ANY)


def params():
    return pltpu.CompilerParams(vmem_limit_bytes=48 * 1024 * 1024)


def front(rows, k1, wires):
    channels = rows.shape[0] // wires
    middle = k1.shape[1]
    length = rows.shape[1] // 2
    return pl.pallas_call(
        functools.partial(front_kernel, wires=wires, channels=channels, middle=middle),
        out_shape=(
            jax.ShapeDtypeStruct((2 * channels + middle, length), BF),
            jax.ShapeDtypeStruct((6 * channels, length), BF),
            jax.ShapeDtypeStruct(((wires // 2 - 1) * 3 * middle, length // 2), BF),
        ),
        in_specs=[vmem()] * 2,
        out_specs=[vmem()] * 3,
        scratch_shapes=[pltpu.VMEM((wires * 3 * channels, length), BF)],
        compiler_params=params(),
        name="front",
    )(rows, k1)


def back(blocks, got, taps1, taps2, k1, k2, active, embeds):
    middle = k1.shape[1]
    channels = k1.shape[0] // 9
    length = got.shape[1]
    count = active.shape[1]
    width = embeds[0].shape[1]
    return pl.pallas_call(
        functools.partial(back_kernel, channels=channels, middle=middle, pieces=len(embeds)),
        out_shape=jax.ShapeDtypeStruct((count + EXTRA, width), BF),
        in_specs=[smem()] + [vmem()] * (6 + len(embeds)),
        out_specs=vmem(),
        scratch_shapes=[
            pltpu.VMEM((9 * channels, length), BF),
            pltpu.VMEM((15 * middle, length // 2), BF),
            pltpu.VMEM((4 * k2.shape[1], count), BF),
        ],
        compiler_params=params(),
        name="back",
    )(blocks, got, taps1, taps2, k1, k2, active, *embeds)


def attend(blocks, got, order, projects, outputs):
    shards, count = order.shape
    width = got.shape[1]
    size = shards * count
    pieces = len(projects)
    return pl.pallas_call(
        functools.partial(attend_kernel, pieces=pieces, shards=shards, count=count),
        out_shape=jax.ShapeDtypeStruct((count, width), BF),
        in_specs=[smem(), vmem(), vmem()] + [hbm()] * (2 * pieces),
        out_specs=vmem(),
        scratch_shapes=[
            pltpu.VMEM((width, 3 * width), BF),
            pltpu.VMEM((width, width), BF),
            pltpu.VMEM((size, width), BF),
            pltpu.VMEM((size, width), BF),
            pltpu.VMEM((size, width), BF),
            pltpu.VMEM((size, width), BF),
            pltpu.VMEM((count, width), BF),
            pltpu.VMEM((count, size), F32),
            pltpu.SemaphoreType.DMA((2, pieces)),
        ],
        compiler_params=params(),
        name="attend",
    )(blocks, got, order, *projects, *outputs)


def swapped(value, axis):
    return lax.ppermute(value, axis, [(0, 1), (1, 0)])


def gathered(weight):
    if lax.axis_size("mp") == 2 and lax.axis_size("section") == 2:
        across = swapped(weight, "mp")
        return [weight, swapped(weight, "section"), across, swapped(across, "section")]
    return [lax.all_gather(weight, ("mp", "section"), axis=0, tiled=True)]


def body(
    readout, first_kernel, second_kernel, embed_weight, project_weight, output_weight, order, active
):
    shards = lax.axis_size("seq")
    position = lax.axis_index("seq")
    embeds, projects, outputs = gathered(embed_weight), gathered(project_weight), gathered(output_weight)
    pieces = len(embeds)
    own = lax.axis_index("mp") * 2 + lax.axis_index("section") if pieces > 1 else 0
    blocks = jnp.concatenate(
        [jnp.arange(pieces, dtype=jnp.int32) ^ own, jnp.reshape(position, (1,)).astype(jnp.int32)]
    )
    channels, wires, ticks = readout.shape[1:]
    k1 = first_kernel.reshape(-1, first_kernel.shape[-1])
    k2 = second_kernel.reshape(-1, second_kernel.shape[-1])
    msg, taps1, taps2 = front(readout.reshape(channels * wires, ticks), k1, wires)
    got = lax.ppermute(msg, "seq", [(i, i + 1) for i in range(shards - 1)])
    tokens = back(blocks, got, taps1, taps2, k1, k2, active, embeds)
    everyone = lax.all_gather(tokens, "seq", axis=0, tiled=True)
    result = attend(blocks, everyone, order.reshape(shards, -1), projects, outputs)
    return result[None]


def solution(mesh):
    in_specs = (
        P(("groups", "mp", "section"), None, "seq", None),
        P(),
        P(),
        P(("mp", "section"), None),
        P(("mp", "section"), None),
        P(("mp", "section"), None),
        P(("groups", "mp", "section"), None),
        P(("groups", "mp", "section"), "seq"),
    )
    out_specs = P(("groups", "mp", "section"), "seq", None)
    return jax.shard_map(body, mesh=mesh, in_specs=in_specs, out_specs=out_specs, check_vma=False)
```

```python
import functools

import jax
import jax.numpy as jnp
from jax import lax
from jax.experimental import pallas as pl
from jax.experimental.pallas import tpu as pltpu
from jax.sharding import PartitionSpec as P


HEADS = 12
masked_score = -1e30
largest = 3e38
epsilon = 1e-05
BF = jnp.bfloat16
F32 = jnp.float32
EXTRA = 8


def dot(a, b, ca=1, cb=0):
    return lax.dot_general(a, b, (((ca,), (cb,)), ((), ())), preferred_element_type=F32)


def iota(shape, axis):
    return lax.broadcasted_iota(jnp.int32, shape, axis)


def one_hot(mask):
    return jnp.where(mask, 1.0, 0.0).astype(BF)


def silu(v):
    half = 0.5 * v
    return half + half * jnp.tanh(half)


def split_matrix():
    row, col = iota((256, 256), 0), iota((256, 256), 1)
    return one_hot(row == jnp.where(col < 128, 2 * col, 2 * col - 255))


def split_time(rows, splitter):
    even, odd = [], []
    for start in range(0, rows.shape[1], 256):
        both = dot(rows[:, start : start + 256], splitter)
        even.append(both[:, :128])
        odd.append(both[:, 128:])
    if len(even) == 1:
        return even[0], odd[0]
    return jnp.concatenate(even, axis=1), jnp.concatenate(odd, axis=1)


def later(odd):
    moved = pltpu.roll(odd, 1, 1)
    return jnp.where(iota(odd.shape, 1) == 0, 0.0, moved)


def store_taps(taps, base, even, odd):
    height = even.shape[0]
    taps[base : base + height, :] = later(odd).astype(BF)
    taps[base + height : base + 2 * height, :] = even.astype(BF)
    taps[base + 2 * height : base + 3 * height, :] = odd.astype(BF)


def front_kernel(x_ref, k1_ref, msg_ref, taps1_ref, taps2_ref, all1, *, wires, channels, middle):
    splitter = split_matrix()
    row, col = iota((256, 256), 0), iota((256, 256), 1)
    part = 256 // wires
    mixer = one_hot(col == (row % part) * wires + row // part)
    for block in range(channels // part):
        rows = dot(mixer, x_ref[block * 256 : (block + 1) * 256, :]).astype(BF)
        even, odd = split_time(rows, splitter)
        lagged = later(odd)
        for wire in range(wires):
            here = slice(wire * part, (wire + 1) * part)
            base = wire * 3 * channels + block * part
            all1[base : base + part, :] = lagged[here].astype(BF)
            all1[base + channels : base + channels + part, :] = even[here].astype(BF)
            all1[base + 2 * channels : base + 2 * channels + part, :] = odd[here].astype(BF)
    taps1_ref[...] = all1[: 6 * channels, :]
    last = (wires - 1) * 3 * channels
    msg_ref[: 2 * channels, :] = all1[last + channels : last + 3 * channels, :]
    k1 = k1_ref[...]
    for level in range(1, wires // 2):
        start = (2 * level - 1) * 3 * channels
        out = silu(dot(k1, all1[start : start + 9 * channels, :], 0, 0)).astype(BF)
        if level == wires // 2 - 1:
            msg_ref[2 * channels :, :] = out
        even, odd = split_time(out, splitter)
        store_taps(taps2_ref, (level - 1) * 3 * middle, even, odd)


def middle_kernel(
    block_ref, taps1_ref, taps2_ref, k1_ref, k2_ref, *refs, channels, middle, pieces
):
    embed_refs = refs[:pieces]
    first_ref, second_ref, token_ref, low_ref, high, patch = refs[pieces:]
    splitter = split_matrix()
    first_ref[...] = dot(k1_ref[3 * channels :, :], taps1_ref[...], 0, 0)
    second_ref[...] = dot(k2_ref[6 * middle :, :], taps2_ref[: 3 * middle, :], 0, 0)
    out = silu(dot(k2_ref[...], taps2_ref[...], 0, 0)).astype(BF)
    store_patch(patch, out, splitter)
    row, col = iota((256, 256), 0), iota((256, 256), 1)
    mixer = one_hot(col == (row % 64) * 4 + row // 64)
    for piece, ref in enumerate(embed_refs):
        parts = ref.shape[0] // 256
        for part in range(parts):
            rows = dot(mixer, ref[part * 256 : (part + 1) * 256, :]).astype(BF)
            base = pl.multiple_of((block_ref[piece] * parts + part) * 128, 128)
            low_ref[pl.ds(base, 128), :] = rows[:128]
            high[pl.ds(base, 128), :] = rows[128:]
    token_ref[...] = dot(patch[...], high[...], 0, 0)


def store_patch(patch, out, splitter):
    even, odd = split_time(out, splitter)
    even, odd = even.astype(BF), odd.astype(BF)
    for block in range(out.shape[0] // 64):
        here = slice(block * 64, (block + 1) * 64)
        patch[block * 128 : block * 128 + 64, :] = even[here]
        patch[block * 128 + 64 : (block + 1) * 128, :] = odd[here]


def back_kernel(
    got_ref, first_ref, second_ref, token_ref, low_ref, k1_ref, k2_ref, active_ref,
    out_ref, all1, all2, patch, *, channels, middle
):
    splitter = split_matrix()
    odd = got_ref[channels : 2 * channels, :].astype(F32)
    all1[:channels, :] = later(odd).astype(BF)
    all1[channels:, :] = got_ref[: 2 * channels, :]
    even, odd = split_time(got_ref[2 * channels :, :], splitter)
    store_taps(all2, 0, even, odd)
    first = silu(first_ref[...] + dot(k1_ref[: 3 * channels, :], all1[...], 0, 0)).astype(BF)
    even, odd = split_time(first, splitter)
    store_taps(all2, 3 * middle, even, odd)
    out = silu(second_ref[...] + dot(k2_ref[: 6 * middle, :], all2[...], 0, 0)).astype(BF)
    store_patch(patch, out, splitter)
    total = token_ref[...] + dot(patch[...], low_ref[...], 0, 0)
    count, width = total.shape
    out_ref[:count, :] = total.astype(BF)
    tail = jnp.broadcast_to(active_ref[...].astype(F32), (EXTRA, count))
    tail = jnp.concatenate([tail, jnp.zeros((EXTRA, width - count), F32)], axis=1)
    out_ref[count:, :] = tail.astype(BF)


def normal(tokens):
    value = tokens.astype(F32)
    value = value - jnp.mean(value, axis=-1, keepdims=True)
    spread = jnp.mean(value * value, axis=-1, keepdims=True)
    return (value * lax.rsqrt(spread + epsilon)).astype(BF)


def lift(chunk_refs, project, normed, keys, values):
    width = project.shape[0]
    for slot, ref in enumerate(chunk_refs):
        count = ref.shape[0] - EXTRA
        normed[slot * count : (slot + 1) * count, :] = normal(ref[:count, :])
    rows = normed[...]
    keys[...] = dot(rows, project[:, width : 2 * width]).astype(BF)
    values[...] = dot(rows, project[:, 2 * width :]).astype(BF)


def collect(block_ref, pieces_refs, target, sems):
    copies = []
    for piece, ref in enumerate(pieces_refs):
        depth = ref.shape[0]
        base = pl.multiple_of(block_ref[piece] * depth, depth)
        copies.append(pltpu.make_async_copy(ref, target.at[pl.ds(base, depth), :], sems.at[piece]))
        copies[-1].start()
    return copies


def prepare_kernel(block_ref, place_ref, order_ref, *refs, pieces, chunks, count):
    project_refs = refs[:pieces]
    chunk_refs = refs[pieces : pieces + chunks]
    project, normed, keys, values, perm_ref, sems = refs[pieces + chunks :]
    copies = collect(block_ref, project_refs, project, sems)
    shards = order_ref.shape[0]
    square = iota((count, count), 0) == iota((count, count), 1)
    lane = iota((1, count), 1)
    labels = jnp.concatenate([lane + place_ref[slot] * count for slot in range(shards)], axis=1)
    labels = labels.astype(F32)
    for slot in range(shards):
        row = order_ref[pl.ds(place_ref[slot], 1), :].astype(F32)
        across = jnp.broadcast_to(row, (count, count))
        down = jnp.sum(jnp.where(square, across, 0.0), axis=1, keepdims=True)
        perm_ref[slot * count : (slot + 1) * count, :] = one_hot(labels == down)
    for copy in copies:
        copy.wait()
    lift(chunk_refs, project, normed, keys, values)


def finish_kernel(block_ref, place_ref, perm_ref, project, normed0, keys0, values0, *refs, pieces, chunks, early, count):
    chunk_refs = refs[:chunks]
    output_refs = refs[chunks : chunks + pieces]
    out_ref, output, normed1, keys1, values1, cap, mixed, sems = refs[chunks + pieces :]
    copies = collect(block_ref, output_refs, output, sems)
    width = project.shape[0]
    lift(chunk_refs[early:], project, normed1, keys1, values1)
    near = early * count
    own = perm_ref[pl.ds(pl.multiple_of(place_ref[chunks] * count, count), count), :]
    picked = (dot(own[:, :near], normed0[...]) + dot(own[:, near:], normed1[...])).astype(BF)
    head = width // HEADS
    queries = (dot(picked, project[:, :width]) * head ** (-0.5)).astype(BF)
    on = None
    token = None
    for slot, ref in enumerate(chunk_refs):
        here = slice(slot * count, (slot + 1) * count)
        term = dot(ref[count:, :count], perm_ref[here, :])
        on = term if on is None else on + term
        term = dot(own[:, here], ref[:count, :])
        token = term if token is None else token + term
    allowed = (own.astype(F32) + jnp.broadcast_to(on[:1], own.shape)) > 0.5
    cap[...] = jnp.where(allowed, largest, masked_score)
    low = iota((count, 2 * head), 1) < head
    for pair in range(HEADS // 2):
        here = slice(pair * 2 * head, (pair + 1) * 2 * head)
        query = queries[:, here]
        zero = jnp.zeros_like(query)
        both = jnp.concatenate([jnp.where(low, query, zero), jnp.where(low, zero, query)], axis=0)
        scores = jnp.concatenate([dot(both, keys0[:, here], 1, 1), dot(both, keys1[:, here], 1, 1)], axis=1)
        weights, scale = [], []
        for half in range(2):
            score = jnp.minimum(scores[half * count : (half + 1) * count], cap[...])
            weight = jnp.exp(score - jnp.max(score, axis=-1, keepdims=True))
            scale.append(1.0 / jnp.sum(weight, axis=-1, keepdims=True))
            weights.append(weight.astype(BF))
        weights = jnp.concatenate(weights, axis=0)
        part = dot(weights[:, :near], values0[:, here]) + dot(weights[:, near:], values1[:, here])
        mixed[:, here] = jnp.where(low, part[:count] * scale[0], part[count:] * scale[1]).astype(BF)
    for copy in copies:
        copy.wait()
    out_ref[...] = (token + dot(mixed[...], output[...])).astype(BF)


def vmem():
    return pl.BlockSpec(memory_space=pltpu.VMEM)


def smem():
    return pl.BlockSpec(memory_space=pltpu.SMEM)


def hbm():
    return pl.BlockSpec(memory_space=pl.ANY)


def params(mib):
    return pltpu.CompilerParams(vmem_limit_bytes=mib * 1024 * 1024)


def array(shape, dtype=BF):
    return jax.ShapeDtypeStruct(shape, dtype)


def front(rows, k1, wires):
    channels = rows.shape[0] // wires
    middle = k1.shape[1]
    length = rows.shape[1] // 2
    return pl.pallas_call(
        functools.partial(front_kernel, wires=wires, channels=channels, middle=middle),
        out_shape=(
            array((2 * channels + middle, length)),
            array((6 * channels, length)),
            array(((wires // 2 - 1) * 3 * middle, length // 2)),
        ),
        in_specs=[vmem()] * 2,
        out_specs=[vmem()] * 3,
        scratch_shapes=[pltpu.VMEM((wires * 3 * channels, length), BF)],
        compiler_params=params(12),
        name="front",
    )(rows, k1)


def central(blocks, taps1, taps2, k1, k2, embeds, count):
    middle, outer = k1.shape[1], k2.shape[1]
    channels = k1.shape[0] // 9
    width = embeds[0].shape[1]
    return pl.pallas_call(
        functools.partial(middle_kernel, channels=channels, middle=middle, pieces=len(embeds)),
        out_shape=(
            array((middle, taps1.shape[1]), F32),
            array((outer, taps2.shape[1]), F32),
            array((count, width), F32),
            array((2 * outer, width)),
        ),
        in_specs=[smem()] + [vmem()] * (4 + len(embeds)),
        out_specs=[vmem()] * 4,
        scratch_shapes=[pltpu.VMEM((2 * outer, width), BF), pltpu.VMEM((2 * outer, count), BF)],
        compiler_params=params(12),
        name="central",
    )(blocks, taps1, taps2, k1, k2, *embeds)


def back(got, parts, k1, k2, active):
    middle = k1.shape[1]
    channels = k1.shape[0] // 9
    length = got.shape[1]
    count = active.shape[1]
    width = parts[-1].shape[1]
    return pl.pallas_call(
        functools.partial(back_kernel, channels=channels, middle=middle),
        out_shape=array((count + EXTRA, width)),
        in_specs=[vmem()] * (4 + len(parts)),
        out_specs=vmem(),
        scratch_shapes=[
            pltpu.VMEM((3 * channels, length), BF),
            pltpu.VMEM((6 * middle, length // 2), BF),
            pltpu.VMEM((2 * k2.shape[1], count), BF),
        ],
        compiler_params=params(12),
        name="back",
    )(got, *parts, k1, k2, active)


def prepare(blocks, places, order, projects, chunks):
    shards, count = order.shape
    width = chunks[0].shape[1]
    size, near = shards * count, len(chunks) * count
    return pl.pallas_call(
        functools.partial(prepare_kernel, pieces=len(projects), chunks=len(chunks), count=count),
        out_shape=(array((width, 3 * width)),) + (array((near, width)),) * 3 + (array((size, size)),),
        in_specs=[smem()] * 2 + [vmem()] + [hbm()] * len(projects) + [vmem()] * len(chunks),
        out_specs=[vmem()] * 5,
        scratch_shapes=[pltpu.SemaphoreType.DMA((len(projects),))],
        compiler_params=params(8 + size // 128),
        name="prepare",
    )(blocks, places, order, *projects, *chunks)


def finish(blocks, places, ready, chunks, outputs, early):
    project, normed, keys, values, perm = ready
    width = project.shape[0]
    size = perm.shape[0]
    count = size // len(chunks)
    far = size - early * count
    return pl.pallas_call(
        functools.partial(finish_kernel, pieces=len(outputs), chunks=len(chunks), early=early, count=count),
        out_shape=array((count, width)),
        in_specs=[smem()] * 2 + [vmem()] * (5 + len(chunks)) + [hbm()] * len(outputs),
        out_specs=vmem(),
        scratch_shapes=[
            pltpu.VMEM((width, width), BF),
            pltpu.VMEM((far, width), BF),
            pltpu.VMEM((far, width), BF),
            pltpu.VMEM((far, width), BF),
            pltpu.VMEM((count, size), F32),
            pltpu.VMEM((count, width), BF),
            pltpu.SemaphoreType.DMA((len(outputs),)),
        ],
        compiler_params=params(8 + size // 64),
        name="finish",
    )(blocks, places, perm, project, normed, keys, values, *chunks, *outputs)


def exchanged(value, axis, flip):
    count = lax.axis_size(axis)
    return lax.ppermute(value, axis, [(i, i ^ flip) for i in range(count)])


def paired():
    return lax.axis_size("mp") == 2 and lax.axis_size("section") == 2


def gathered(weight):
    if paired():
        across = exchanged(weight, "mp", 1)
        beside = exchanged(weight, "section", 1)
        return [weight, beside, across, exchanged(across, "section", 1)]
    return [lax.all_gather(weight, ("mp", "section"), axis=0, tiled=True)]


def layer(
    readout, first_kernel, second_kernel, embed_weight, project_weight, output_weight, order, active
):
    shards = lax.axis_size("seq")
    position = lax.axis_index("seq").astype(jnp.int32)
    embeds = gathered(embed_weight)
    projects = gathered(project_weight)
    outputs = gathered(output_weight)
    pieces = len(embeds)
    own = lax.axis_index("mp") * 2 + lax.axis_index("section") if pieces > 1 else 0
    blocks = jnp.arange(pieces, dtype=jnp.int32) ^ own
    channels, wires, ticks = readout.shape[1:]
    k1 = first_kernel.reshape(-1, first_kernel.shape[-1])
    k2 = second_kernel.reshape(-1, second_kernel.shape[-1])
    order = order.reshape(shards, -1)
    count = order.shape[1]
    slots = jnp.arange(shards, dtype=jnp.int32)
    msg, taps1, taps2 = front(readout.reshape(channels * wires, ticks), k1, wires)
    got = lax.ppermute(msg, "seq", [(i, i + 1) for i in range(shards - 1)])
    parts = central(blocks, taps1, taps2, k1, k2, embeds, count)
    tokens = back(got, parts, k1, k2, active)
    if shards == 4:
        slot = jnp.zeros((1,), jnp.int32)
        places = slots ^ position
        chunks = [tokens] + [exchanged(tokens, "seq", flip) for flip in (1, 2, 3)]
    else:
        slot = position.reshape(1)
        places = slots
        everyone = lax.all_gather(tokens, "seq", axis=0, tiled=True)
        chunks = [everyone[i * (count + EXTRA) : (i + 1) * (count + EXTRA)] for i in range(shards)]
    early = shards // 2
    places = jnp.concatenate([places, slot])
    ready = prepare(blocks, places, order, projects, chunks[:early])
    result = finish(blocks, places, ready, chunks, outputs, early)
    return result[None]


def solution(mesh):
    in_specs = (
        P(("groups", "mp", "section"), None, "seq", None),
        P(),
        P(),
        P(("mp", "section"), None),
        P(("mp", "section"), None),
        P(("mp", "section"), None),
        P(("groups", "mp", "section"), None),
        P(("groups", "mp", "section"), "seq"),
    )
    out_specs = P(("groups", "mp", "section"), "seq", None)
    return jax.shard_map(layer, mesh=mesh, in_specs=in_specs, out_specs=out_specs, check_vma=False)
```

```python
import functools

import jax
import jax.numpy as jnp
from jax import lax
from jax.experimental import pallas as pl
from jax.experimental.pallas import tpu as pltpu
from jax.sharding import PartitionSpec as P


HEADS = 12
masked_score = -1e30
largest = 3e38
epsilon = 1e-05
BF = jnp.bfloat16
F32 = jnp.float32
EXTRA = 8


def dot(a, b, ca=1, cb=0):
    return lax.dot_general(a, b, (((ca,), (cb,)), ((), ())), preferred_element_type=F32)


def iota(shape, axis):
    return lax.broadcasted_iota(jnp.int32, shape, axis)


def one_hot(mask):
    return jnp.where(mask, 1.0, 0.0).astype(BF)


def silu(v):
    half = 0.5 * v
    return half + half * jnp.tanh(half)


def split_matrix():
    row, col = iota((256, 256), 0), iota((256, 256), 1)
    return one_hot(row == jnp.where(col < 128, 2 * col, 2 * col - 255))


def split_time(rows, splitter):
    even, odd = [], []
    for start in range(0, rows.shape[1], 256):
        both = dot(rows[:, start : start + 256], splitter)
        even.append(both[:, :128])
        odd.append(both[:, 128:])
    if len(even) == 1:
        return even[0], odd[0]
    return jnp.concatenate(even, axis=1), jnp.concatenate(odd, axis=1)


def later(odd):
    moved = pltpu.roll(odd, 1, 1)
    return jnp.where(iota(odd.shape, 1) == 0, 0.0, moved)


def store_taps(taps, base, even, odd):
    height = even.shape[0]
    taps[base : base + height, :] = later(odd).astype(BF)
    taps[base + height : base + 2 * height, :] = even.astype(BF)
    taps[base + 2 * height : base + 3 * height, :] = odd.astype(BF)


def block_of(paired, flip=0):
    if not paired:
        return 0
    return (lax.axis_index("mp") * 2 + lax.axis_index("section")) ^ flip


def front_kernel(x_hbm, k1_hbm, k2_hbm, *refs, wires, channels, middle, paired):
    if paired:
        project_hbm, output_hbm = refs[:2]
        refs = refs[2:]
    msg_ref, taps1_ref, taps2_ref, k1_ref, k2_ref = refs[:5]
    all1, x_ref, sems = refs[-3:]
    part = 256 // wires
    blocks = channels // part
    loads = []
    for block in range(blocks):
        here = pl.ds(block * 256, 256)
        loads.append(pltpu.make_async_copy(x_hbm.at[here, :], x_ref.at[here, :], sems.at[block]))
    loads.append(pltpu.make_async_copy(k1_hbm, k1_ref, sems.at[blocks]))
    others = [pltpu.make_async_copy(k2_hbm, k2_ref, sems.at[blocks + 1])]
    if paired:
        near_ref, query_ref = refs[5:7]
        depth, width = output_hbm.shape
        half = depth // 2
        rows = pl.ds(pl.multiple_of(lax.axis_index("groups") * half, half), half)
        others.append(
            pltpu.make_async_copy(
                project_hbm.at[rows, pl.ds(width, 2 * width)], near_ref, sems.at[blocks + 2]
            )
        )
        others.append(
            pltpu.make_async_copy(
                project_hbm.at[:, pl.ds(0, width)], query_ref.at[:, pl.ds(0, width)], sems.at[blocks + 3]
            )
        )
        others.append(
            pltpu.make_async_copy(output_hbm, query_ref.at[:, pl.ds(width, width)], sems.at[blocks + 4])
        )
    for copy in loads + others:
        copy.start()
    splitter = split_matrix()
    row, col = iota((256, 256), 0), iota((256, 256), 1)
    mixer = one_hot(col == (row % part) * wires + row // part)
    for block in range(blocks):
        loads[block].wait()
        rows = dot(mixer, x_ref[block * 256 : (block + 1) * 256, :]).astype(BF)
        even, odd = split_time(rows, splitter)
        lagged = later(odd)
        for wire in range(wires):
            here = slice(wire * part, (wire + 1) * part)
            base = wire * 3 * channels + block * part
            all1[base : base + part, :] = lagged[here].astype(BF)
            all1[base + channels : base + channels + part, :] = even[here].astype(BF)
            all1[base + 2 * channels : base + 2 * channels + part, :] = odd[here].astype(BF)
    taps1_ref[...] = all1[: 6 * channels, :]
    last = (wires - 1) * 3 * channels
    msg_ref[: 2 * channels, :] = all1[last + channels : last + 3 * channels, :]
    loads[blocks].wait()
    k1 = k1_ref[...]
    for level in range(1, wires // 2):
        start = (2 * level - 1) * 3 * channels
        out = silu(dot(k1, all1[start : start + 9 * channels, :], 0, 0)).astype(BF)
        if level == wires // 2 - 1:
            msg_ref[2 * channels :, :] = out
        even, odd = split_time(out, splitter)
        store_taps(taps2_ref, (level - 1) * 3 * middle, even, odd)
    for copy in others:
        copy.wait()


def central_kernel(taps1_ref, taps2_ref, k1_ref, k2_ref, first_ref, second_ref, patch, *, channels, middle):
    splitter = split_matrix()
    first_ref[...] = dot(k1_ref[3 * channels :, :], taps1_ref[...], 0, 0)
    second_ref[...] = dot(k2_ref[6 * middle :, :], taps2_ref[: 3 * middle, :], 0, 0)
    out = silu(dot(k2_ref[...], taps2_ref[...], 0, 0)).astype(BF)
    store_patch(patch, out, splitter)


def mix_kernel(patch, *refs, pieces):
    embed_refs = refs[:pieces]
    token_ref, low_ref, high, own, sem = refs[pieces:]
    copy = pltpu.make_async_copy(embed_refs[0], own, sem)
    copy.start()
    row, col = iota((256, 256), 0), iota((256, 256), 1)
    mixer = one_hot(col == (row % 64) * 4 + row // 64)
    for piece in list(range(1, pieces)) + [0]:
        ref = embed_refs[piece]
        if piece == 0:
            copy.wait()
            ref = own
        parts = ref.shape[0] // 256
        for part in range(parts):
            rows = dot(mixer, ref[part * 256 : (part + 1) * 256, :]).astype(BF)
            base = pl.multiple_of((block_of(pieces > 1, piece) * parts + part) * 128, 128)
            low_ref[pl.ds(base, 128), :] = rows[:128]
            high[pl.ds(base, 128), :] = rows[128:]
    token_ref[...] = dot(patch[...], high[...], 0, 0)


def store_patch(patch, out, splitter):
    even, odd = split_time(out, splitter)
    even, odd = even.astype(BF), odd.astype(BF)
    for block in range(out.shape[0] // 64):
        here = slice(block * 64, (block + 1) * 64)
        patch[block * 128 : block * 128 + 64, :] = even[here]
        patch[block * 128 + 64 : (block + 1) * 128, :] = odd[here]


def back_kernel(
    got_ref, first_ref, second_ref, token_ref, low_ref, k1_ref, k2_ref, active_ref,
    out_ref, all1, all2, patch, *, channels, middle
):
    splitter = split_matrix()
    odd = got_ref[channels : 2 * channels, :].astype(F32)
    all1[:channels, :] = later(odd).astype(BF)
    all1[channels:, :] = got_ref[: 2 * channels, :]
    even, odd = split_time(got_ref[2 * channels :, :], splitter)
    store_taps(all2, 0, even, odd)
    first = silu(first_ref[...] + dot(k1_ref[: 3 * channels, :], all1[...], 0, 0)).astype(BF)
    even, odd = split_time(first, splitter)
    store_taps(all2, 3 * middle, even, odd)
    out = silu(second_ref[...] + dot(k2_ref[: 6 * middle, :], all2[...], 0, 0)).astype(BF)
    store_patch(patch, out, splitter)
    total = token_ref[...] + dot(patch[...], low_ref[...], 0, 0)
    count, width = total.shape
    out_ref[:count, :] = total.astype(BF)
    tail = jnp.broadcast_to(active_ref[...].astype(F32), (EXTRA, count))
    tail = jnp.concatenate([tail, jnp.zeros((EXTRA, width - count), F32)], axis=1)
    out_ref[count:, :] = tail.astype(BF)


def normal(tokens):
    value = tokens.astype(F32)
    value = value - jnp.mean(value, axis=-1, keepdims=True)
    spread = jnp.mean(value * value, axis=-1, keepdims=True)
    return (value * lax.rsqrt(spread + epsilon)).astype(BF)


def lift(joined, normed, keys, values):
    width = joined.shape[0]
    rows = normed[...]
    keys[...] = dot(rows, joined[:, :width]).astype(BF)
    values[...] = dot(rows, joined[:, width:]).astype(BF)


def collect(sources, target, sems):
    copies = []
    for index, (ref, base, column, align) in enumerate(sources):
        if not isinstance(base, int):
            base = pl.multiple_of(base, align)
        copies.append(
            pltpu.make_async_copy(
                ref.at[:, pl.ds(column, target.shape[1])],
                target.at[pl.ds(base, ref.shape[0]), :],
                sems.at[index],
            )
        )
        copies[-1].start()
    return copies


def place_of(slot, swap):
    position = lax.axis_index("seq")
    return position ^ slot if swap else slot


def prepare_kernel(order_ref, *refs, pieces, chunks, swap):
    kv_refs = refs[:pieces]
    chunk_refs = refs[pieces : pieces + chunks]
    joined, normed, keys, values, perm_ref, sems = refs[pieces + chunks :]
    width = joined.shape[0]
    if pieces > 1:
        own, beside, near, far, near_corner, far_corner = kv_refs
        depth, half = own.shape[0], near.shape[0]
        group = lax.axis_index("groups")
        sources = [
            (own, block_of(True, 0) * depth, width, depth),
            (beside, block_of(True, 1) * depth, width, depth),
        ]
        for flip, first, second in ((2, near, far), (3, near_corner, far_corner)):
            base = block_of(True, flip) * depth
            sources.append((first, base + group * half, 0, half))
            sources.append((second, base + (group ^ 1) * half, 0, half))
    else:
        sources = [(kv_refs[0], 0, width, 1)]
    copies = collect(sources, joined, sems)
    shards, count = order_ref.shape
    square = iota((count, count), 0) == iota((count, count), 1)
    lane = iota((1, count), 1)
    labels = jnp.concatenate([lane + place_of(slot, swap) * count for slot in range(shards)], axis=1)
    labels = labels.astype(F32)
    for slot in range(shards):
        row = order_ref[pl.ds(place_of(slot, swap), 1), :].astype(F32)
        across = jnp.broadcast_to(row, (count, count))
        down = jnp.sum(jnp.where(square, across, 0.0), axis=1, keepdims=True)
        perm_ref[slot * count : (slot + 1) * count, :] = one_hot(labels == down)
    for slot, ref in enumerate(chunk_refs):
        normed[slot * count : (slot + 1) * count, :] = normal(ref[:count, :])
    for copy in copies:
        copy.wait()
    lift(joined, normed, keys, values)


def finish_kernel(perm_ref, joined, normed0, keys0, values0, *refs, pieces, chunks, early, count, swap):
    chunk_refs = refs[:chunks]
    weight_refs = refs[chunks : chunks + 2 * pieces]
    out_ref, query, output, normed1, keys1, values1, cap, mixed, sems = refs[chunks + 2 * pieces :]
    width = joined.shape[0]
    sources = [[], []]
    for kind in range(2):
        for piece in range(pieces):
            ref = weight_refs[kind * pieces + piece]
            depth = ref.shape[0]
            column = width if kind and piece > 1 else 0
            sources[kind].append((ref, block_of(pieces > 1, piece) * depth, column, depth))
    wait_query = collect(sources[0], query, sems.at[0])
    wait_output = collect(sources[1], output, sems.at[1])
    for slot, ref in enumerate(chunk_refs[early:]):
        normed1[slot * count : (slot + 1) * count, :] = normal(ref[:count, :])
    lift(joined, normed1, keys1, values1)
    near = early * count
    slot = 0 if swap else lax.axis_index("seq")
    own = perm_ref[pl.ds(pl.multiple_of(slot * count, count), count), :]
    picked = (dot(own[:, :near], normed0[...]) + dot(own[:, near:], normed1[...])).astype(BF)
    head = width // HEADS
    for copy in wait_query:
        copy.wait()
    queries = (dot(picked, query[...]) * head ** (-0.5)).astype(BF)
    on = None
    token = None
    for slot, ref in enumerate(chunk_refs):
        here = slice(slot * count, (slot + 1) * count)
        term = dot(ref[count:, :count], perm_ref[here, :])
        on = term if on is None else on + term
        term = dot(own[:, here], ref[:count, :])
        token = term if token is None else token + term
    allowed = (own.astype(F32) + jnp.broadcast_to(on[:1], own.shape)) > 0.5
    cap[...] = jnp.where(allowed, largest, masked_score)
    low = iota((count, 2 * head), 1) < head
    for pair in range(HEADS // 2):
        here = slice(pair * 2 * head, (pair + 1) * 2 * head)
        query = queries[:, here]
        zero = jnp.zeros_like(query)
        both = jnp.concatenate([jnp.where(low, query, zero), jnp.where(low, zero, query)], axis=0)
        scores = jnp.concatenate([dot(both, keys0[:, here], 1, 1), dot(both, keys1[:, here], 1, 1)], axis=1)
        weights, scale = [], []
        for half in range(2):
            score = jnp.minimum(scores[half * count : (half + 1) * count], cap[...])
            weight = jnp.exp(score - jnp.max(score, axis=-1, keepdims=True))
            scale.append(1.0 / jnp.sum(weight, axis=-1, keepdims=True))
            weights.append(weight.astype(BF))
        weights = jnp.concatenate(weights, axis=0)
        part = dot(weights[:, :near], values0[:, here]) + dot(weights[:, near:], values1[:, here])
        mixed[:, here] = jnp.where(low, part[:count] * scale[0], part[count:] * scale[1]).astype(BF)
    for copy in wait_output:
        copy.wait()
    out_ref[...] = (token + dot(mixed[...], output[...])).astype(BF)


def vmem():
    return pl.BlockSpec(memory_space=pltpu.VMEM)


def hbm():
    return pl.BlockSpec(memory_space=pl.ANY)


def fixed():
    return pl.BlockSpec(memory_space=pltpu.HBM)


def params(mib):
    return pltpu.CompilerParams(vmem_limit_bytes=mib * 1024 * 1024)


def array(shape, dtype=BF):
    return jax.ShapeDtypeStruct(shape, dtype)


def front(rows, k1, k2, wires, weights):
    channels = rows.shape[0] // wires
    middle = k1.shape[1]
    length = rows.shape[1] // 2
    outs = [
        array((2 * channels + middle, length)),
        array((6 * channels, length)),
        array(((wires // 2 - 1) * 3 * middle, length // 2)),
        array(k1.shape),
        array(k2.shape),
    ]
    if weights:
        depth, width = weights[1].shape
        outs += [array((depth // 2, 2 * width)), array((depth, 2 * width))]
    return pl.pallas_call(
        functools.partial(
            front_kernel, wires=wires, channels=channels, middle=middle, paired=len(weights) > 0
        ),
        out_shape=outs,
        in_specs=[fixed()] * (3 + len(weights)),
        out_specs=[vmem()] * len(outs),
        scratch_shapes=[
            pltpu.VMEM((wires * 3 * channels, length), BF),
            pltpu.VMEM(rows.shape, BF),
            pltpu.SemaphoreType.DMA((channels * wires // 256 + 5,)),
        ],
        compiler_params=params(12),
        name="front",
    )(*[pltpu.with_memory_space_constraint(v, pltpu.HBM) for v in (rows, k1, k2, *weights)])


def central(taps1, taps2, k1, k2, count):
    middle, outer = k1.shape[1], k2.shape[1]
    channels = k1.shape[0] // 9
    return pl.pallas_call(
        functools.partial(central_kernel, channels=channels, middle=middle),
        out_shape=(
            array((middle, taps1.shape[1]), F32),
            array((outer, taps2.shape[1]), F32),
            array((2 * outer, count)),
        ),
        in_specs=[vmem()] * 4,
        out_specs=[vmem()] * 3,
        compiler_params=params(8),
        name="central",
    )(taps1, taps2, k1, k2)


def mix(patch, embeds):
    width = embeds[0].shape[1]
    return pl.pallas_call(
        functools.partial(mix_kernel, pieces=len(embeds)),
        out_shape=(array((patch.shape[1], width), F32), array((patch.shape[0], width))),
        in_specs=[vmem()] + [fixed()] + [vmem()] * (len(embeds) - 1),
        out_specs=[vmem()] * 2,
        scratch_shapes=[
            pltpu.VMEM((patch.shape[0], width), BF),
            pltpu.VMEM(embeds[0].shape, BF),
            pltpu.SemaphoreType.DMA,
        ],
        compiler_params=params(8),
        name="mix",
    )(patch, *embeds)


def back(got, parts, k1, k2, active):
    middle = k1.shape[1]
    channels = k1.shape[0] // 9
    length = got.shape[1]
    count = active.shape[1]
    width = parts[-1].shape[1]
    return pl.pallas_call(
        functools.partial(back_kernel, channels=channels, middle=middle),
        out_shape=array((count + EXTRA, width)),
        in_specs=[vmem()] * (4 + len(parts)),
        out_specs=vmem(),
        scratch_shapes=[
            pltpu.VMEM((3 * channels, length), BF),
            pltpu.VMEM((6 * middle, length // 2), BF),
            pltpu.VMEM((2 * k2.shape[1], count), BF),
        ],
        compiler_params=params(8),
        name="back",
    )(got, *parts, k1, k2, active)


def prepare(order, weights, chunks, swap):
    shards, count = order.shape
    width = chunks[0].shape[1]
    size, near = shards * count, len(chunks) * count
    return pl.pallas_call(
        functools.partial(prepare_kernel, pieces=len(weights), chunks=len(chunks), swap=swap),
        out_shape=(array((width, 2 * width)),) + (array((near, width)),) * 3 + (array((size, size)),),
        in_specs=[vmem()] + [fixed()] + [hbm()] * (len(weights) - 1) + [vmem()] * len(chunks),
        out_specs=[vmem()] * 5,
        scratch_shapes=[pltpu.SemaphoreType.DMA((len(weights),))],
        compiler_params=params(8 + size // 128),
        name="prepare",
    )(order, *weights, *chunks)


def finish(ready, chunks, weights, early, swap):
    joined, normed, keys, values, perm = ready
    width = joined.shape[0]
    size = perm.shape[0]
    count = size // len(chunks)
    far = size - early * count
    pieces = len(weights) // 2
    return pl.pallas_call(
        functools.partial(
            finish_kernel, pieces=pieces, chunks=len(chunks), early=early, count=count, swap=swap
        ),
        out_shape=array((count, width)),
        in_specs=[vmem()] * (5 + len(chunks))
        + ([fixed()] + [hbm()] * (pieces - 1)) * 2,
        out_specs=vmem(),
        scratch_shapes=[
            pltpu.VMEM((width, width), BF),
            pltpu.VMEM((width, width), BF),
            pltpu.VMEM((far, width), BF),
            pltpu.VMEM((far, width), BF),
            pltpu.VMEM((far, width), BF),
            pltpu.VMEM((count, size), F32),
            pltpu.VMEM((count, width), BF),
            pltpu.SemaphoreType.DMA((2, pieces)),
        ],
        compiler_params=params(8 + size // 64),
        name="finish",
    )(perm, joined, normed, keys, values, *chunks, *weights)


def exchanged(value, axis, flip):
    count = lax.axis_size(axis)
    return lax.ppermute(value, axis, [(i, i ^ flip) for i in range(count)])


def layer(
    readout, first_kernel, second_kernel, embed_weight, project_weight, output_weight, order, active
):
    shards = lax.axis_size("seq")
    paired = lax.axis_size("mp") == 2 and lax.axis_size("section") == 2 and lax.axis_size("groups") == 2
    swap = shards == 4
    channels, wires, ticks = readout.shape[1:]
    k1 = first_kernel.reshape(-1, first_kernel.shape[-1])
    k2 = second_kernel.reshape(-1, second_kernel.shape[-1])
    order = order.reshape(shards, -1)
    count = order.shape[1]
    rows = readout.reshape(channels * wires, ticks)
    weights = (project_weight, output_weight)
    if paired:
        embed_across = exchanged(embed_weight, "mp", 1)
        embed_beside = exchanged(embed_weight, "section", 1)
        embeds = [embed_weight, embed_beside, embed_across]
        embeds.append(exchanged(embed_across, "section", 1))
        front_out = front(rows, k1, k2, wires, weights)
        msg, taps1, taps2, k1, k2, near, packed = front_out
    else:
        embeds = [lax.all_gather(embed_weight, ("mp", "section"), axis=0, tiled=True)]
        msg, taps1, taps2, k1, k2 = front(rows, k1, k2, wires, ())
    got = lax.ppermute(msg, "seq", [(i, i + 1) for i in range(shards - 1)])
    first, second, patch = central(taps1, taps2, k1, k2, count)
    token, low = mix(patch, embeds)
    tokens = back(got, (first, second, token, low), k1, k2, active)
    if swap:
        chunks = [tokens] + [exchanged(tokens, "seq", flip) for flip in (1, 2, 3)]
    else:
        everyone = lax.all_gather(tokens, "seq", axis=0, tiled=True)
        chunks = [everyone[i * (count + EXTRA) : (i + 1) * (count + EXTRA)] for i in range(shards)]
    if paired:
        project_beside = exchanged(project_weight, "section", 1)
        output_beside = exchanged(output_weight, "section", 1)
        near = exchanged(near, "mp", 1)
        far = exchanged(near, "groups", 1)
        packed = exchanged(packed, "mp", 1)
        kv_weights = [project_weight, project_beside, near, far]
        kv_weights.append(exchanged(near, "section", 1))
        kv_weights.append(exchanged(far, "section", 1))
        corner = exchanged(packed, "section", 1)
        last_weights = [project_weight, project_beside, packed, corner]
        last_weights += [output_weight, output_beside, packed, corner]
    else:
        kv_weights = [lax.all_gather(project_weight, ("mp", "section"), axis=0, tiled=True)]
        last_weights = kv_weights + [lax.all_gather(output_weight, ("mp", "section"), axis=0, tiled=True)]
    early = shards // 2
    ready = prepare(order, kv_weights, chunks[:early], swap)
    result = finish(ready, chunks, last_weights, early, swap)
    return result[None]


def solution(mesh):
    in_specs = (
        P(("groups", "mp", "section"), None, "seq", None),
        P(),
        P(),
        P(("mp", "section"), None),
        P(("mp", "section"), None),
        P(("mp", "section"), None),
        P(("groups", "mp", "section"), None),
        P(("groups", "mp", "section"), "seq"),
    )
    out_specs = P(("groups", "mp", "section"), "seq", None)
    return jax.shard_map(layer, mesh=mesh, in_specs=in_specs, out_specs=out_specs, check_vma=False)
```

```python
import functools

import jax
import jax.numpy as jnp
from jax import lax
from jax.experimental import pallas as pl
from jax.experimental.pallas import tpu as pltpu
from jax.sharding import PartitionSpec as P


HEADS = 12
masked_score = -1e30
largest = 3e38
epsilon = 1e-05
BF = jnp.bfloat16
F32 = jnp.float32
EXTRA = 8


def dot(a, b, ca=1, cb=0):
    return lax.dot_general(a, b, (((ca,), (cb,)), ((), ())), preferred_element_type=F32)


def iota(shape, axis):
    return lax.broadcasted_iota(jnp.int32, shape, axis)


def one_hot(mask):
    return jnp.where(mask, 1.0, 0.0).astype(BF)


def silu(v):
    half = 0.5 * v
    return half + half * jnp.tanh(half)


def split_matrix():
    row, col = iota((256, 256), 0), iota((256, 256), 1)
    return one_hot(row == jnp.where(col < 128, 2 * col, 2 * col - 255))


def split_time(rows, splitter):
    even, odd = [], []
    for start in range(0, rows.shape[1], 256):
        both = dot(rows[:, start : start + 256], splitter)
        even.append(both[:, :128])
        odd.append(both[:, 128:])
    if len(even) == 1:
        return even[0], odd[0]
    return jnp.concatenate(even, axis=1), jnp.concatenate(odd, axis=1)


def later(odd):
    moved = pltpu.roll(odd, 1, 1)
    return jnp.where(iota(odd.shape, 1) == 0, 0.0, moved)


def store_taps(taps, base, even, odd):
    height = even.shape[0]
    taps[base : base + height, :] = later(odd).astype(BF)
    taps[base + height : base + 2 * height, :] = even.astype(BF)
    taps[base + 2 * height : base + 3 * height, :] = odd.astype(BF)


def block_of(paired, flip=0):
    if not paired:
        return 0
    return (lax.axis_index("mp") * 2 + lax.axis_index("section")) ^ flip


def front_kernel(x_hbm, k1_hbm, k2_hbm, *refs, wires, channels, middle, paired):
    if paired:
        project_hbm, output_hbm = refs[:2]
        refs = refs[2:]
    msg_ref, taps1_ref, taps2_ref, k1_ref, k2_ref = refs[:5]
    all1, x_ref, sems = refs[-3:]
    part = 256 // wires
    blocks = channels // part
    loads = []
    for block in range(blocks):
        here = pl.ds(block * 256, 256)
        loads.append(pltpu.make_async_copy(x_hbm.at[here, :], x_ref.at[here, :], sems.at[block]))
    loads.append(pltpu.make_async_copy(k1_hbm, k1_ref, sems.at[blocks]))
    others = [pltpu.make_async_copy(k2_hbm, k2_ref, sems.at[blocks + 1])]
    if paired:
        near_ref, query_ref = refs[5:7]
        depth, width = output_hbm.shape
        half = depth // 2
        rows = pl.ds(pl.multiple_of(lax.axis_index("groups") * half, half), half)
        others.append(
            pltpu.make_async_copy(
                project_hbm.at[rows, pl.ds(width, 2 * width)], near_ref, sems.at[blocks + 2]
            )
        )
        others.append(
            pltpu.make_async_copy(
                project_hbm.at[:, pl.ds(0, width)], query_ref.at[:, pl.ds(0, width)], sems.at[blocks + 3]
            )
        )
        others.append(
            pltpu.make_async_copy(output_hbm, query_ref.at[:, pl.ds(width, width)], sems.at[blocks + 4])
        )
    for copy in loads + others:
        copy.start()
    splitter = split_matrix()
    row, col = iota((256, 256), 0), iota((256, 256), 1)
    mixer = one_hot(col == (row % part) * wires + row // part)
    for block in range(blocks):
        loads[block].wait()
        rows = dot(mixer, x_ref[block * 256 : (block + 1) * 256, :]).astype(BF)
        even, odd = split_time(rows, splitter)
        lagged = later(odd)
        for wire in range(wires):
            here = slice(wire * part, (wire + 1) * part)
            base = wire * 3 * channels + block * part
            all1[base : base + part, :] = lagged[here].astype(BF)
            all1[base + channels : base + channels + part, :] = even[here].astype(BF)
            all1[base + 2 * channels : base + 2 * channels + part, :] = odd[here].astype(BF)
    taps1_ref[...] = all1[: 6 * channels, :]
    last = (wires - 1) * 3 * channels
    msg_ref[: 2 * channels, :] = all1[last + channels : last + 3 * channels, :]
    loads[blocks].wait()
    k1 = k1_ref[...]
    for level in range(1, wires // 2):
        start = (2 * level - 1) * 3 * channels
        out = silu(dot(k1, all1[start : start + 9 * channels, :], 0, 0)).astype(BF)
        if level == wires // 2 - 1:
            msg_ref[2 * channels :, :] = out
        even, odd = split_time(out, splitter)
        store_taps(taps2_ref, (level - 1) * 3 * middle, even, odd)
    for copy in others:
        copy.wait()


def central_kernel(taps1_ref, taps2_ref, k1_ref, k2_ref, first_ref, second_ref, patch, *, channels, middle):
    splitter = split_matrix()
    first_ref[...] = dot(k1_ref[3 * channels :, :], taps1_ref[...], 0, 0)
    second_ref[...] = dot(k2_ref[6 * middle :, :], taps2_ref[: 3 * middle, :], 0, 0)
    out = silu(dot(k2_ref[...], taps2_ref[...], 0, 0)).astype(BF)
    store_patch(patch, out, splitter)


def mix_kernel(patch, *refs, pieces):
    embed_refs = refs[:pieces]
    token_ref, low_ref, high, own, sem = refs[pieces:]
    copy = pltpu.make_async_copy(embed_refs[0], own, sem)
    copy.start()
    row, col = iota((256, 256), 0), iota((256, 256), 1)
    mixer = one_hot(col == (row % 64) * 4 + row // 64)
    for piece in list(range(1, pieces)) + [0]:
        ref = embed_refs[piece]
        if piece == 0:
            copy.wait()
            ref = own
        parts = ref.shape[0] // 256
        for part in range(parts):
            rows = dot(mixer, ref[part * 256 : (part + 1) * 256, :]).astype(BF)
            base = pl.multiple_of((block_of(pieces > 1, piece) * parts + part) * 128, 128)
            low_ref[pl.ds(base, 128), :] = rows[:128]
            high[pl.ds(base, 128), :] = rows[128:]
    token_ref[...] = dot(patch[...], high[...], 0, 0)


def store_patch(patch, out, splitter):
    even, odd = split_time(out, splitter)
    even, odd = even.astype(BF), odd.astype(BF)
    for block in range(out.shape[0] // 64):
        here = slice(block * 64, (block + 1) * 64)
        patch[block * 128 : block * 128 + 64, :] = even[here]
        patch[block * 128 + 64 : (block + 1) * 128, :] = odd[here]


def back_kernel(
    got_ref, first_ref, second_ref, token_ref, low_ref, k1_ref, k2_ref, active_ref,
    out_ref, all1, all2, patch, *, channels, middle
):
    splitter = split_matrix()
    odd = got_ref[channels : 2 * channels, :].astype(F32)
    all1[:channels, :] = later(odd).astype(BF)
    all1[channels:, :] = got_ref[: 2 * channels, :]
    even, odd = split_time(got_ref[2 * channels :, :], splitter)
    store_taps(all2, 0, even, odd)
    first = silu(first_ref[...] + dot(k1_ref[: 3 * channels, :], all1[...], 0, 0)).astype(BF)
    even, odd = split_time(first, splitter)
    store_taps(all2, 3 * middle, even, odd)
    out = silu(second_ref[...] + dot(k2_ref[: 6 * middle, :], all2[...], 0, 0)).astype(BF)
    store_patch(patch, out, splitter)
    total = token_ref[...] + dot(patch[...], low_ref[...], 0, 0)
    count, width = total.shape
    out_ref[:count, :] = total.astype(BF)
    tail = jnp.broadcast_to(active_ref[...].astype(F32), (EXTRA, count))
    tail = jnp.concatenate([tail, jnp.zeros((EXTRA, width - count), F32)], axis=1)
    out_ref[count:, :] = tail.astype(BF)


def normal(tokens):
    value = tokens.astype(F32)
    value = value - jnp.mean(value, axis=-1, keepdims=True)
    spread = jnp.mean(value * value, axis=-1, keepdims=True)
    return (value * lax.rsqrt(spread + epsilon)).astype(BF)


def lift(joined, normed, keys, values):
    width = joined.shape[0]
    rows = normed[...]
    keys[...] = dot(rows, joined[:, :width]).astype(BF)
    values[...] = dot(rows, joined[:, width:]).astype(BF)


def collect(sources, target, sems):
    copies = []
    for index, (ref, base, column, align) in enumerate(sources):
        if not isinstance(base, int):
            base = pl.multiple_of(base, align)
        copies.append(
            pltpu.make_async_copy(
                ref.at[:, pl.ds(column, target.shape[1])],
                target.at[pl.ds(base, ref.shape[0]), :],
                sems.at[index],
            )
        )
        copies[-1].start()
    return copies


def place_of(slot, swap):
    position = lax.axis_index("seq")
    return position ^ slot if swap else slot


def prepare_kernel(order_ref, *refs, pieces, chunks, swap):
    kv_refs = refs[:pieces]
    chunk_refs = refs[pieces : pieces + chunks]
    joined, normed, keys, values, perm_ref, sems = refs[pieces + chunks :]
    width = joined.shape[0]
    if pieces > 1:
        own, beside, near, far, near_corner, far_corner = kv_refs
        depth, half = own.shape[0], near.shape[0]
        group = lax.axis_index("groups")
        sources = [
            (own, block_of(True, 0) * depth, width, depth),
            (beside, block_of(True, 1) * depth, width, depth),
        ]
        for flip, first, second in ((2, near, far), (3, near_corner, far_corner)):
            base = block_of(True, flip) * depth
            sources.append((first, base + group * half, 0, half))
            sources.append((second, base + (group ^ 1) * half, 0, half))
    else:
        sources = [(kv_refs[0], 0, width, 1)]
    copies = collect(sources, joined, sems)
    shards, count = order_ref.shape
    square = iota((count, count), 0) == iota((count, count), 1)
    lane = iota((1, count), 1)
    labels = jnp.concatenate([lane + place_of(slot, swap) * count for slot in range(shards)], axis=1)
    labels = labels.astype(F32)
    for slot in range(shards):
        row = order_ref[pl.ds(place_of(slot, swap), 1), :].astype(F32)
        across = jnp.broadcast_to(row, (count, count))
        down = jnp.sum(jnp.where(square, across, 0.0), axis=1, keepdims=True)
        perm_ref[slot * count : (slot + 1) * count, :] = one_hot(labels == down)
    for slot, ref in enumerate(chunk_refs):
        normed[slot * count : (slot + 1) * count, :] = normal(ref[:count, :])
    for copy in copies:
        copy.wait()
    lift(joined, normed, keys, values)


def extend_kernel(perm_ref, joined, normed0, *refs, pieces, chunks, early, swap):
    chunk_refs = refs[:chunks]
    weight_refs = refs[chunks : chunks + 2 * pieces]
    refs = refs[chunks + 2 * pieces :]
    query, output, keys1, values1, token_ref, picked_ref, on_ref, normed1, sems = refs
    width = joined.shape[0]
    count = token_ref.shape[0]
    copies = []
    for kind, target in enumerate((query, output)):
        sources = []
        for piece in range(pieces):
            ref = weight_refs[kind * pieces + piece]
            depth = ref.shape[0]
            column = width if kind and piece > 1 else 0
            sources.append((ref, block_of(pieces > 1, piece) * depth, column, depth))
        copies += collect(sources, target, sems.at[kind])
    for slot, ref in enumerate(chunk_refs[early:]):
        normed1[slot * count : (slot + 1) * count, :] = normal(ref[:count, :])
    lift(joined, normed1, keys1, values1)
    own = own_rows(perm_ref, count, swap)
    near = early * count
    picked_ref[...] = dot(own[:, :near], normed0[...]) + dot(own[:, near : chunks * count], normed1[...])
    on, token = flags_and_tokens(perm_ref, own, chunk_refs, 0)
    on_ref[...] = on
    token_ref[...] = token
    for copy in copies:
        copy.wait()


def own_rows(perm_ref, count, swap):
    slot = 0 if swap else lax.axis_index("seq")
    return perm_ref[pl.ds(pl.multiple_of(slot * count, count), count), :]


def flags_and_tokens(perm_ref, own, chunk_refs, first):
    count = own.shape[0]
    on = token = 0.0
    for slot, ref in enumerate(chunk_refs):
        here = slice((first + slot) * count, (first + slot + 1) * count)
        on += dot(ref[count:, :count], perm_ref[here, :])
        token += dot(own[:, here], ref[:count, :])
    return on, token


def finish_kernel(
    perm_ref, joined, keys0, values0, keys1, values1, query, output, token_ref, picked_ref, on_ref, *refs,
    chunks, swap
):
    chunk_refs = refs[:chunks]
    out_ref, normed2, keys2, values2, cap, mixed = refs[chunks:]
    count, width = token_ref.shape
    first = perm_ref.shape[0] // count - chunks
    for slot, ref in enumerate(chunk_refs):
        normed2[slot * count : (slot + 1) * count, :] = normal(ref[:count, :])
    lift(joined, normed2, keys2, values2)
    own = own_rows(perm_ref, count, swap)
    picked = (picked_ref[...] + dot(own[:, first * count :], normed2[...])).astype(BF)
    head = width // HEADS
    queries = (dot(picked, query[...]) * head ** (-0.5)).astype(BF)
    on, token = flags_and_tokens(perm_ref, own, chunk_refs, first)
    on += on_ref[...]
    token += token_ref[...]
    allowed = (own.astype(F32) + jnp.broadcast_to(on[:1], own.shape)) > 0.5
    cap[...] = jnp.where(allowed, largest, masked_score)
    low = iota((count, 2 * head), 1) < head
    groups = ((keys0, values0), (keys1, values1), (keys2, values2))
    for pair in range(HEADS // 2):
        here = slice(pair * 2 * head, (pair + 1) * 2 * head)
        part_query = queries[:, here]
        zero = jnp.zeros_like(part_query)
        both = [jnp.where(low, part_query, zero), jnp.where(low, zero, part_query)]
        both = jnp.concatenate(both, axis=0)
        scores = jnp.concatenate([dot(both, keys[:, here], 1, 1) for keys, _ in groups], axis=1)
        weights, scale = [], []
        for half in range(2):
            score = jnp.minimum(scores[half * count : (half + 1) * count], cap[...])
            weight = jnp.exp(score - jnp.max(score, axis=-1, keepdims=True))
            scale.append(1.0 / jnp.sum(weight, axis=-1, keepdims=True))
            weights.append(weight.astype(BF))
        weights = jnp.concatenate(weights, axis=0)
        part, start = 0.0, 0
        for keys, values in groups:
            part += dot(weights[:, start : start + keys.shape[0]], values[:, here])
            start += keys.shape[0]
        mixed[:, here] = jnp.where(low, part[:count] * scale[0], part[count:] * scale[1]).astype(BF)
    out_ref[...] = (token + dot(mixed[...], output[...])).astype(BF)


def vmem():
    return pl.BlockSpec(memory_space=pltpu.VMEM)


def hbm():
    return pl.BlockSpec(memory_space=pl.ANY)


def fixed():
    return pl.BlockSpec(memory_space=pltpu.HBM)


def params(mib):
    return pltpu.CompilerParams(vmem_limit_bytes=mib * 1024 * 1024)


def array(shape, dtype=BF):
    return jax.ShapeDtypeStruct(shape, dtype)


def front(rows, k1, k2, wires, weights):
    channels = rows.shape[0] // wires
    middle = k1.shape[1]
    length = rows.shape[1] // 2
    outs = [
        array((2 * channels + middle, length)),
        array((6 * channels, length)),
        array(((wires // 2 - 1) * 3 * middle, length // 2)),
        array(k1.shape),
        array(k2.shape),
    ]
    if weights:
        depth, width = weights[1].shape
        outs += [array((depth // 2, 2 * width)), array((depth, 2 * width))]
    return pl.pallas_call(
        functools.partial(
            front_kernel, wires=wires, channels=channels, middle=middle, paired=len(weights) > 0
        ),
        out_shape=outs,
        in_specs=[fixed()] * (3 + len(weights)),
        out_specs=[vmem()] * len(outs),
        scratch_shapes=[
            pltpu.VMEM((wires * 3 * channels, length), BF),
            pltpu.VMEM(rows.shape, BF),
            pltpu.SemaphoreType.DMA((channels * wires // 256 + 5,)),
        ],
        compiler_params=params(12),
        name="front",
    )(*[pltpu.with_memory_space_constraint(v, pltpu.HBM) for v in (rows, k1, k2, *weights)])


def central(taps1, taps2, k1, k2, count):
    middle, outer = k1.shape[1], k2.shape[1]
    channels = k1.shape[0] // 9
    return pl.pallas_call(
        functools.partial(central_kernel, channels=channels, middle=middle),
        out_shape=(
            array((middle, taps1.shape[1]), F32),
            array((outer, taps2.shape[1]), F32),
            array((2 * outer, count)),
        ),
        in_specs=[vmem()] * 4,
        out_specs=[vmem()] * 3,
        compiler_params=params(8),
        name="central",
    )(taps1, taps2, k1, k2)


def mix(patch, embeds):
    width = embeds[0].shape[1]
    return pl.pallas_call(
        functools.partial(mix_kernel, pieces=len(embeds)),
        out_shape=(array((patch.shape[1], width), F32), array((patch.shape[0], width))),
        in_specs=[vmem()] + [fixed()] + [vmem()] * (len(embeds) - 1),
        out_specs=[vmem()] * 2,
        scratch_shapes=[
            pltpu.VMEM((patch.shape[0], width), BF),
            pltpu.VMEM(embeds[0].shape, BF),
            pltpu.SemaphoreType.DMA,
        ],
        compiler_params=params(8),
        name="mix",
    )(patch, *embeds)


def back(got, parts, k1, k2, active):
    middle = k1.shape[1]
    channels = k1.shape[0] // 9
    length = got.shape[1]
    count = active.shape[1]
    width = parts[-1].shape[1]
    return pl.pallas_call(
        functools.partial(back_kernel, channels=channels, middle=middle),
        out_shape=array((count + EXTRA, width)),
        in_specs=[vmem()] * (4 + len(parts)),
        out_specs=vmem(),
        scratch_shapes=[
            pltpu.VMEM((3 * channels, length), BF),
            pltpu.VMEM((6 * middle, length // 2), BF),
            pltpu.VMEM((2 * k2.shape[1], count), BF),
        ],
        compiler_params=params(8),
        name="back",
    )(got, *parts, k1, k2, active)


def prepare(order, weights, chunks, swap):
    shards, count = order.shape
    width = chunks[0].shape[1]
    size, near = shards * count, len(chunks) * count
    return pl.pallas_call(
        functools.partial(prepare_kernel, pieces=len(weights), chunks=len(chunks), swap=swap),
        out_shape=(array((width, 2 * width)),) + (array((near, width)),) * 3 + (array((size, size)),),
        in_specs=[vmem()] + [fixed()] + [hbm()] * (len(weights) - 1) + [vmem()] * len(chunks),
        out_specs=[vmem()] * 5,
        scratch_shapes=[pltpu.SemaphoreType.DMA((len(weights),))],
        compiler_params=params(8 + size // 128),
        name="prepare",
    )(order, *weights, *chunks)


def extend(ready, chunks, weights, early, swap):
    joined, normed, _, _, perm = ready
    width = joined.shape[0]
    size = perm.shape[0]
    count = chunks[0].shape[0] - EXTRA
    far = (len(chunks) - early) * count
    pieces = len(weights) // 2
    return pl.pallas_call(
        functools.partial(extend_kernel, pieces=pieces, chunks=len(chunks), early=early, swap=swap),
        out_shape=(
            array((width, width)),
            array((width, width)),
            array((far, width)),
            array((far, width)),
            array((count, width), F32),
            array((count, width), F32),
            array((EXTRA, size), F32),
        ),
        in_specs=[vmem()] * (3 + len(chunks)) + ([fixed()] + [hbm()] * (pieces - 1)) * 2,
        out_specs=[vmem()] * 7,
        scratch_shapes=[pltpu.VMEM((far, width), BF), pltpu.SemaphoreType.DMA((2, pieces))],
        compiler_params=params(8 + size // 128),
        name="extend",
    )(perm, joined, normed, *chunks, *weights)


def finish(ready, extra, chunks, swap):
    joined, _, keys, values, perm = ready
    query, output, keys1, values1, token, picked, on = extra
    width = joined.shape[0]
    size = perm.shape[0]
    count = token.shape[0]
    far = len(chunks) * count
    return pl.pallas_call(
        functools.partial(finish_kernel, chunks=len(chunks), swap=swap),
        out_shape=array((count, width)),
        in_specs=[vmem()] * (11 + len(chunks)),
        out_specs=vmem(),
        scratch_shapes=[
            pltpu.VMEM((far, width), BF),
            pltpu.VMEM((far, width), BF),
            pltpu.VMEM((far, width), BF),
            pltpu.VMEM((count, size), F32),
            pltpu.VMEM((count, width), BF),
        ],
        compiler_params=params(8 + size // 64),
        name="finish",
    )(perm, joined, keys, values, keys1, values1, query, output, token, picked, on, *chunks)


def exchanged(value, axis, flip):
    count = lax.axis_size(axis)
    return lax.ppermute(value, axis, [(i, i ^ flip) for i in range(count)])


def layer(
    readout, first_kernel, second_kernel, embed_weight, project_weight, output_weight, order, active
):
    shards = lax.axis_size("seq")
    paired = lax.axis_size("mp") == 2 and lax.axis_size("section") == 2 and lax.axis_size("groups") == 2
    swap = shards == 4
    channels, wires, ticks = readout.shape[1:]
    k1 = first_kernel.reshape(-1, first_kernel.shape[-1])
    k2 = second_kernel.reshape(-1, second_kernel.shape[-1])
    order = order.reshape(shards, -1)
    count = order.shape[1]
    rows = readout.reshape(channels * wires, ticks)
    weights = (project_weight, output_weight)
    if paired:
        embed_across = exchanged(embed_weight, "mp", 1)
        embed_beside = exchanged(embed_weight, "section", 1)
        embeds = [embed_weight, embed_beside, embed_across]
        embeds.append(exchanged(embed_across, "section", 1))
        front_out = front(rows, k1, k2, wires, weights)
        msg, taps1, taps2, k1, k2, near, packed = front_out
    else:
        embeds = [lax.all_gather(embed_weight, ("mp", "section"), axis=0, tiled=True)]
        msg, taps1, taps2, k1, k2 = front(rows, k1, k2, wires, ())
    got = lax.ppermute(msg, "seq", [(i, i + 1) for i in range(shards - 1)])
    first, second, patch = central(taps1, taps2, k1, k2, count)
    token, low = mix(patch, embeds)
    tokens = back(got, (first, second, token, low), k1, k2, active)
    if swap:
        chunks = [tokens] + [exchanged(tokens, "seq", flip) for flip in (1, 2)]
        chunks.append(exchanged(chunks[2], "seq", 1))
    else:
        everyone = lax.all_gather(tokens, "seq", axis=0, tiled=True)
        chunks = [everyone[i * (count + EXTRA) : (i + 1) * (count + EXTRA)] for i in range(shards)]
    if paired:
        project_beside = exchanged(project_weight, "section", 1)
        output_beside = exchanged(output_weight, "section", 1)
        near = exchanged(near, "mp", 1)
        far = exchanged(near, "groups", 1)
        packed = exchanged(packed, "mp", 1)
        kv_weights = [project_weight, project_beside, near, far]
        kv_weights.append(exchanged(near, "section", 1))
        kv_weights.append(exchanged(far, "section", 1))
        corner = exchanged(packed, "section", 1)
        last_weights = [project_weight, project_beside, packed, corner]
        last_weights += [output_weight, output_beside, packed, corner]
    else:
        kv_weights = [lax.all_gather(project_weight, ("mp", "section"), axis=0, tiled=True)]
        last_weights = kv_weights + [lax.all_gather(output_weight, ("mp", "section"), axis=0, tiled=True)]
    early, later = shards // 2, shards // 2 + shards // 4
    ready = prepare(order, kv_weights, chunks[:early], swap)
    extra = extend(ready, chunks[:later], last_weights, early, swap)
    result = finish(ready, extra, chunks[later:], swap)
    return result[None]


def solution(mesh):
    in_specs = (
        P(("groups", "mp", "section"), None, "seq", None),
        P(),
        P(),
        P(("mp", "section"), None),
        P(("mp", "section"), None),
        P(("mp", "section"), None),
        P(("groups", "mp", "section"), None),
        P(("groups", "mp", "section"), "seq"),
    )
    out_specs = P(("groups", "mp", "section"), "seq", None)
    return jax.shard_map(layer, mesh=mesh, in_specs=in_specs, out_specs=out_specs, check_vma=False)
```

```python
import functools

import jax
import jax.numpy as jnp
from jax import lax
from jax.experimental import pallas as pl
from jax.experimental.pallas import tpu as pltpu
from jax.sharding import PartitionSpec as P


HEADS = 12
masked_score = -1e30
largest = 3e38
epsilon = 1e-05
BF = jnp.bfloat16
F32 = jnp.float32
EXTRA = 8


def dot(a, b, ca=1, cb=0):
    return lax.dot_general(a, b, (((ca,), (cb,)), ((), ())), preferred_element_type=F32)


def iota(shape, axis):
    return lax.broadcasted_iota(jnp.int32, shape, axis)


def one_hot(mask):
    return jnp.where(mask, 1.0, 0.0).astype(BF)


def silu(v):
    half = 0.5 * v
    return half + half * jnp.tanh(half)


def split_matrix():
    row, col = iota((256, 256), 0), iota((256, 256), 1)
    return one_hot(row == jnp.where(col < 128, 2 * col, 2 * col - 255))


def split_time(rows, splitter):
    even, odd = [], []
    for start in range(0, rows.shape[1], 256):
        both = dot(rows[:, start : start + 256], splitter)
        even.append(both[:, :128])
        odd.append(both[:, 128:])
    if len(even) == 1:
        return even[0], odd[0]
    return jnp.concatenate(even, axis=1), jnp.concatenate(odd, axis=1)


def later(odd):
    moved = pltpu.roll(odd, 1, 1)
    return jnp.where(iota(odd.shape, 1) == 0, 0.0, moved)


def store_taps(taps, base, even, odd):
    height = even.shape[0]
    taps[base : base + height, :] = later(odd).astype(BF)
    taps[base + height : base + 2 * height, :] = even.astype(BF)
    taps[base + 2 * height : base + 3 * height, :] = odd.astype(BF)


def block_of(paired, flip=0):
    if not paired:
        return 0
    return (lax.axis_index("mp") * 2 + lax.axis_index("section")) ^ flip


def wire_rows(x_ref, block, first, wires, part):
    height = (wires - first[0]) * part if first[1] is None else (first[1] - first[0]) * part
    row, col = iota((height, 256), 0), iota((height, 256), 1)
    mixer = one_hot(col == (row % part) * wires + row // part + first[0])
    return dot(mixer, x_ref[block * 256 : (block + 1) * 256, :]).astype(BF)


def fill_taps(taps, rows, block, splitter, part, channels):
    even, odd = split_time(rows, splitter)
    lagged = later(odd)
    for wire in range(rows.shape[0] // part):
        here = slice(wire * part, (wire + 1) * part)
        base = wire * 3 * channels + block * part
        taps[base : base + part, :] = lagged[here].astype(BF)
        taps[base + channels : base + channels + part, :] = even[here].astype(BF)
        taps[base + 2 * channels : base + 2 * channels + part, :] = odd[here].astype(BF)


def front_kernel(x_hbm, k1_hbm, k2_hbm, *refs, wires, channels, middle, paired):
    if paired:
        project_hbm = refs[0]
        refs = refs[1:]
    msg_ref, x_ref, k1_ref, k2_ref = refs[:4]
    taps, sems = refs[-2:]
    part = 256 // wires
    blocks = channels // part
    loads = []
    for block in range(blocks):
        here = pl.ds(block * 256, 256)
        loads.append(pltpu.make_async_copy(x_hbm.at[here, :], x_ref.at[here, :], sems.at[block]))
    loads.append(pltpu.make_async_copy(k1_hbm, k1_ref, sems.at[blocks]))
    others = [pltpu.make_async_copy(k2_hbm, k2_ref, sems.at[blocks + 1])]
    if paired:
        near_ref, query_ref = refs[4:6]
        depth, width = query_ref.shape
        half = depth // 2
        rows = pl.ds(pl.multiple_of(lax.axis_index("groups") * half, half), half)
        others.append(
            pltpu.make_async_copy(
                project_hbm.at[rows, pl.ds(width, 2 * width)], near_ref, sems.at[blocks + 2]
            )
        )
        others.append(
            pltpu.make_async_copy(project_hbm.at[:, pl.ds(0, width)], query_ref, sems.at[blocks + 3])
        )
    for copy in loads + others:
        copy.start()
    splitter = split_matrix()
    for block in range(blocks):
        loads[block].wait()
        rows = wire_rows(x_ref, block, (wires - 3, None), wires, part)
        fill_taps(taps, rows, block, splitter, part, channels)
    msg_ref[: 2 * channels, :] = taps[7 * channels :, :]
    loads[blocks].wait()
    msg_ref[2 * channels :, :] = silu(dot(k1_ref[...], taps[...], 0, 0)).astype(BF)
    for copy in others:
        copy.wait()


def central_kernel(
    msg_ref, x_ref, k1_ref, k2_ref, first_ref, second_ref, patch, taps1, taps2, *, wires, channels, middle
):
    splitter = split_matrix()
    part = 256 // wires
    for block in range(channels // part):
        rows = wire_rows(x_ref, block, (0, wires - 2), wires, part)
        fill_taps(taps1, rows, block, splitter, part, channels)
    first_ref[...] = dot(k1_ref[3 * channels :, :], taps1[: 6 * channels, :], 0, 0)
    for level in range(1, wires // 2):
        if level == wires // 2 - 1:
            out = msg_ref[2 * channels :, :]
        else:
            start = (2 * level - 1) * 3 * channels
            out = silu(dot(k1_ref[...], taps1[start : start + 9 * channels, :], 0, 0)).astype(BF)
        even, odd = split_time(out, splitter)
        store_taps(taps2, (level - 1) * 3 * middle, even, odd)
    second_ref[...] = dot(k2_ref[6 * middle :, :], taps2[: 3 * middle, :], 0, 0)
    out = silu(dot(k2_ref[...], taps2[...], 0, 0)).astype(BF)
    store_patch(patch, out, splitter)


def mix_kernel(patch, *refs, pieces):
    embed_refs = refs[:pieces]
    token_ref, low_ref, high, own, sem = refs[pieces:]
    copy = pltpu.make_async_copy(embed_refs[0], own, sem)
    copy.start()
    row, col = iota((256, 256), 0), iota((256, 256), 1)
    mixer = one_hot(col == (row % 64) * 4 + row // 64)
    for piece in list(range(1, pieces)) + [0]:
        ref = embed_refs[piece]
        if piece == 0:
            copy.wait()
            ref = own
        parts = ref.shape[0] // 256
        for part in range(parts):
            rows = dot(mixer, ref[part * 256 : (part + 1) * 256, :]).astype(BF)
            base = pl.multiple_of((block_of(pieces > 1, piece) * parts + part) * 128, 128)
            low_ref[pl.ds(base, 128), :] = rows[:128]
            high[pl.ds(base, 128), :] = rows[128:]
    token_ref[...] = dot(patch[...], high[...], 0, 0)


def store_patch(patch, out, splitter):
    even, odd = split_time(out, splitter)
    even, odd = even.astype(BF), odd.astype(BF)
    for block in range(out.shape[0] // 64):
        here = slice(block * 64, (block + 1) * 64)
        patch[block * 128 : block * 128 + 64, :] = even[here]
        patch[block * 128 + 64 : (block + 1) * 128, :] = odd[here]


def back_kernel(
    got_ref, first_ref, second_ref, token_ref, low_ref, k1_ref, k2_ref, active_ref,
    out_ref, all1, all2, patch, *, channels, middle
):
    splitter = split_matrix()
    odd = got_ref[channels : 2 * channels, :].astype(F32)
    all1[:channels, :] = later(odd).astype(BF)
    all1[channels:, :] = got_ref[: 2 * channels, :]
    even, odd = split_time(got_ref[2 * channels :, :], splitter)
    store_taps(all2, 0, even, odd)
    first = silu(first_ref[...] + dot(k1_ref[: 3 * channels, :], all1[...], 0, 0)).astype(BF)
    even, odd = split_time(first, splitter)
    store_taps(all2, 3 * middle, even, odd)
    out = silu(second_ref[...] + dot(k2_ref[: 6 * middle, :], all2[...], 0, 0)).astype(BF)
    store_patch(patch, out, splitter)
    total = token_ref[...] + dot(patch[...], low_ref[...], 0, 0)
    count, width = total.shape
    out_ref[:count, :] = total.astype(BF)
    tail = jnp.broadcast_to(active_ref[...].astype(F32), (EXTRA, count))
    tail = jnp.concatenate([tail, jnp.zeros((EXTRA, width - count), F32)], axis=1)
    out_ref[count:, :] = tail.astype(BF)


def normal(tokens):
    value = tokens.astype(F32)
    value = value - jnp.mean(value, axis=-1, keepdims=True)
    spread = jnp.mean(value * value, axis=-1, keepdims=True)
    return (value * lax.rsqrt(spread + epsilon)).astype(BF)


def lift(joined, normed, keys, values):
    width = joined.shape[0]
    rows = normed[...]
    keys[...] = dot(rows, joined[:, :width]).astype(BF)
    values[...] = dot(rows, joined[:, width:]).astype(BF)


def collect(sources, target, sems):
    copies = []
    for index, (ref, base, column, align) in enumerate(sources):
        if not isinstance(base, int):
            base = pl.multiple_of(base, align)
        copies.append(
            pltpu.make_async_copy(
                ref.at[:, pl.ds(column, target.shape[1])],
                target.at[pl.ds(base, ref.shape[0]), :],
                sems.at[index],
            )
        )
        copies[-1].start()
    return copies


def place_of(slot, swap):
    position = lax.axis_index("seq")
    return position ^ slot if swap else slot


def prepare_kernel(order_ref, *refs, pieces, chunks, swap):
    kv_refs = refs[:pieces]
    chunk_refs = refs[pieces : pieces + chunks]
    joined, normed, keys, values, perm_ref, sems = refs[pieces + chunks :]
    width = joined.shape[0]
    if pieces > 1:
        own, beside, near, far, near_corner, far_corner = kv_refs
        depth, half = own.shape[0], near.shape[0]
        group = lax.axis_index("groups")
        sources = [
            (own, block_of(True, 0) * depth, width, depth),
            (beside, block_of(True, 1) * depth, width, depth),
        ]
        for flip, first, second in ((2, near, far), (3, near_corner, far_corner)):
            base = block_of(True, flip) * depth
            sources.append((first, base + group * half, 0, half))
            sources.append((second, base + (group ^ 1) * half, 0, half))
    else:
        sources = [(kv_refs[0], 0, width, 1)]
    copies = collect(sources, joined, sems)
    shards, count = order_ref.shape
    square = iota((count, count), 0) == iota((count, count), 1)
    lane = iota((1, count), 1)
    labels = jnp.concatenate([lane + place_of(slot, swap) * count for slot in range(shards)], axis=1)
    labels = labels.astype(F32)
    for slot in range(shards):
        row = order_ref[pl.ds(place_of(slot, swap), 1), :].astype(F32)
        across = jnp.broadcast_to(row, (count, count))
        down = jnp.sum(jnp.where(square, across, 0.0), axis=1, keepdims=True)
        perm_ref[slot * count : (slot + 1) * count, :] = one_hot(labels == down)
    for slot, ref in enumerate(chunk_refs):
        normed[slot * count : (slot + 1) * count, :] = normal(ref[:count, :])
    for copy in copies:
        copy.wait()
    lift(joined, normed, keys, values)


def extend_kernel(perm_ref, joined, normed0, *refs, pieces, chunks, early, swap):
    chunk_refs = refs[:chunks]
    weight_refs = refs[chunks : chunks + 2 * pieces]
    refs = refs[chunks + 2 * pieces :]
    query, output, keys1, values1, token_ref, picked_ref, on_ref, normed1, sems = refs
    count = token_ref.shape[0]
    copies = []
    for kind, target in enumerate((query, output)):
        sources = []
        for piece in range(pieces):
            ref = weight_refs[kind * pieces + piece]
            depth = ref.shape[0]
            sources.append((ref, block_of(pieces > 1, piece) * depth, 0, depth))
        copies += collect(sources, target, sems.at[kind])
    for slot, ref in enumerate(chunk_refs[early:]):
        normed1[slot * count : (slot + 1) * count, :] = normal(ref[:count, :])
    lift(joined, normed1, keys1, values1)
    own = own_rows(perm_ref, count, swap)
    near = early * count
    picked_ref[...] = dot(own[:, :near], normed0[...]) + dot(own[:, near : chunks * count], normed1[...])
    on, token = flags_and_tokens(perm_ref, own, chunk_refs, 0)
    on_ref[...] = on
    token_ref[...] = token
    for copy in copies:
        copy.wait()


def own_rows(perm_ref, count, swap):
    slot = 0 if swap else lax.axis_index("seq")
    return perm_ref[pl.ds(pl.multiple_of(slot * count, count), count), :]


def flags_and_tokens(perm_ref, own, chunk_refs, first):
    count = own.shape[0]
    on = token = 0.0
    for slot, ref in enumerate(chunk_refs):
        here = slice((first + slot) * count, (first + slot + 1) * count)
        on += dot(ref[count:, :count], perm_ref[here, :])
        token += dot(own[:, here], ref[:count, :])
    return on, token


def finish_kernel(
    perm_ref, joined, keys0, values0, keys1, values1, query, output, token_ref, picked_ref, on_ref, *refs,
    chunks, swap
):
    chunk_refs = refs[:chunks]
    out_ref, normed2, keys2, values2, cap, mixed = refs[chunks:]
    count, width = token_ref.shape
    first = perm_ref.shape[0] // count - chunks
    for slot, ref in enumerate(chunk_refs):
        normed2[slot * count : (slot + 1) * count, :] = normal(ref[:count, :])
    lift(joined, normed2, keys2, values2)
    own = own_rows(perm_ref, count, swap)
    picked = (picked_ref[...] + dot(own[:, first * count :], normed2[...])).astype(BF)
    head = width // HEADS
    queries = (dot(picked, query[...]) * head ** (-0.5)).astype(BF)
    on, token = flags_and_tokens(perm_ref, own, chunk_refs, first)
    on += on_ref[...]
    token += token_ref[...]
    allowed = (own.astype(F32) + jnp.broadcast_to(on[:1], own.shape)) > 0.5
    cap[...] = jnp.where(allowed, largest, masked_score)
    low = iota((count, 2 * head), 1) < head
    groups = ((keys0, values0), (keys1, values1), (keys2, values2))
    for pair in range(HEADS // 2):
        here = slice(pair * 2 * head, (pair + 1) * 2 * head)
        part_query = queries[:, here]
        zero = jnp.zeros_like(part_query)
        both = [jnp.where(low, part_query, zero), jnp.where(low, zero, part_query)]
        both = jnp.concatenate(both, axis=0)
        scores = jnp.concatenate([dot(both, keys[:, here], 1, 1) for keys, _ in groups], axis=1)
        weights, scale = [], []
        for half in range(2):
            score = jnp.minimum(scores[half * count : (half + 1) * count], cap[...])
            weight = jnp.exp(score - jnp.max(score, axis=-1, keepdims=True))
            scale.append(1.0 / jnp.sum(weight, axis=-1, keepdims=True))
            weights.append(weight.astype(BF))
        weights = jnp.concatenate(weights, axis=0)
        part, start = 0.0, 0
        for keys, values in groups:
            part += dot(weights[:, start : start + keys.shape[0]], values[:, here])
            start += keys.shape[0]
        mixed[:, here] = jnp.where(low, part[:count] * scale[0], part[count:] * scale[1]).astype(BF)
    out_ref[...] = (token + dot(mixed[...], output[...])).astype(BF)


def vmem():
    return pl.BlockSpec(memory_space=pltpu.VMEM)


def hbm():
    return pl.BlockSpec(memory_space=pl.ANY)


def fixed():
    return pl.BlockSpec(memory_space=pltpu.HBM)


def params(mib):
    return pltpu.CompilerParams(vmem_limit_bytes=mib * 1024 * 1024)


def array(shape, dtype=BF):
    return jax.ShapeDtypeStruct(shape, dtype)


def front(rows, k1, k2, wires, weights):
    channels = rows.shape[0] // wires
    middle = k1.shape[1]
    length = rows.shape[1] // 2
    outs = [array((2 * channels + middle, length)), array(rows.shape), array(k1.shape), array(k2.shape)]
    if weights:
        depth, width = weights[0].shape
        outs += [array((depth // 2, width // 3 * 2)), array((depth, width // 3))]
    operands = [pltpu.with_memory_space_constraint(v, pltpu.HBM) for v in (rows, k1, k2, *weights)]
    return pl.pallas_call(
        functools.partial(
            front_kernel, wires=wires, channels=channels, middle=middle, paired=len(weights) > 0
        ),
        out_shape=outs,
        in_specs=[fixed()] * len(operands),
        out_specs=[vmem()] * len(outs),
        scratch_shapes=[
            pltpu.VMEM((9 * channels, length), BF),
            pltpu.SemaphoreType.DMA((channels * wires // 256 + 4,)),
        ],
        compiler_params=params(8),
        name="front",
    )(*operands)


def central(msg, rows, k1, k2, wires, count):
    middle, outer = k1.shape[1], k2.shape[1]
    channels = k1.shape[0] // 9
    length = msg.shape[1]
    return pl.pallas_call(
        functools.partial(central_kernel, wires=wires, channels=channels, middle=middle),
        out_shape=(
            array((middle, length), F32),
            array((outer, length // 2), F32),
            array((2 * outer, count)),
        ),
        in_specs=[vmem()] * 4,
        out_specs=[vmem()] * 3,
        scratch_shapes=[
            pltpu.VMEM(((wires - 2) * 3 * channels, length), BF),
            pltpu.VMEM(((wires // 2 - 1) * 3 * middle, length // 2), BF),
        ],
        compiler_params=params(10),
        name="central",
    )(msg, rows, k1, k2)


def mix(patch, embeds):
    width = embeds[0].shape[1]
    return pl.pallas_call(
        functools.partial(mix_kernel, pieces=len(embeds)),
        out_shape=(array((patch.shape[1], width), F32), array((patch.shape[0], width))),
        in_specs=[vmem()] + [fixed()] + [vmem()] * (len(embeds) - 1),
        out_specs=[vmem()] * 2,
        scratch_shapes=[
            pltpu.VMEM((patch.shape[0], width), BF),
            pltpu.VMEM(embeds[0].shape, BF),
            pltpu.SemaphoreType.DMA,
        ],
        compiler_params=params(8),
        name="mix",
    )(patch, *embeds)


def back(got, parts, k1, k2, active):
    middle = k1.shape[1]
    channels = k1.shape[0] // 9
    length = got.shape[1]
    count = active.shape[1]
    width = parts[-1].shape[1]
    return pl.pallas_call(
        functools.partial(back_kernel, channels=channels, middle=middle),
        out_shape=array((count + EXTRA, width)),
        in_specs=[vmem()] * (4 + len(parts)),
        out_specs=vmem(),
        scratch_shapes=[
            pltpu.VMEM((3 * channels, length), BF),
            pltpu.VMEM((6 * middle, length // 2), BF),
            pltpu.VMEM((2 * k2.shape[1], count), BF),
        ],
        compiler_params=params(8),
        name="back",
    )(got, *parts, k1, k2, active)


def prepare(order, weights, chunks, swap):
    shards, count = order.shape
    width = chunks[0].shape[1]
    size, near = shards * count, len(chunks) * count
    return pl.pallas_call(
        functools.partial(prepare_kernel, pieces=len(weights), chunks=len(chunks), swap=swap),
        out_shape=(array((width, 2 * width)),) + (array((near, width)),) * 3 + (array((size, size)),),
        in_specs=[vmem()] + [fixed()] + [hbm()] * (len(weights) - 1) + [vmem()] * len(chunks),
        out_specs=[vmem()] * 5,
        scratch_shapes=[pltpu.SemaphoreType.DMA((len(weights),))],
        compiler_params=params(8 + size // 128),
        name="prepare",
    )(order, *weights, *chunks)


def extend(ready, chunks, weights, early, swap):
    joined, normed, _, _, perm = ready
    width = joined.shape[0]
    size = perm.shape[0]
    count = chunks[0].shape[0] - EXTRA
    far = (len(chunks) - early) * count
    pieces = len(weights) // 2
    return pl.pallas_call(
        functools.partial(extend_kernel, pieces=pieces, chunks=len(chunks), early=early, swap=swap),
        out_shape=(
            array((width, width)),
            array((width, width)),
            array((far, width)),
            array((far, width)),
            array((count, width), F32),
            array((count, width), F32),
            array((EXTRA, size), F32),
        ),
        in_specs=[vmem()] * (3 + len(chunks)) + ([fixed()] + [hbm()] * (pieces - 1)) * 2,
        out_specs=[vmem()] * 7,
        scratch_shapes=[pltpu.VMEM((far, width), BF), pltpu.SemaphoreType.DMA((2, pieces))],
        compiler_params=params(8 + size // 128),
        name="extend",
    )(perm, joined, normed, *chunks, *weights)


def finish(ready, extra, chunks, swap):
    joined, _, keys, values, perm = ready
    query, output, keys1, values1, token, picked, on = extra
    width = joined.shape[0]
    size = perm.shape[0]
    count = token.shape[0]
    far = len(chunks) * count
    return pl.pallas_call(
        functools.partial(finish_kernel, chunks=len(chunks), swap=swap),
        out_shape=array((count, width)),
        in_specs=[vmem()] * (11 + len(chunks)),
        out_specs=vmem(),
        scratch_shapes=[
            pltpu.VMEM((far, width), BF),
            pltpu.VMEM((far, width), BF),
            pltpu.VMEM((far, width), BF),
            pltpu.VMEM((count, size), F32),
            pltpu.VMEM((count, width), BF),
        ],
        compiler_params=params(8 + size // 64),
        name="finish",
    )(perm, joined, keys, values, keys1, values1, query, output, token, picked, on, *chunks)


def exchanged(value, axis, flip):
    count = lax.axis_size(axis)
    return lax.ppermute(value, axis, [(i, i ^ flip) for i in range(count)])


def layer(
    readout, first_kernel, second_kernel, embed_weight, project_weight, output_weight, order, active
):
    shards = lax.axis_size("seq")
    paired = lax.axis_size("mp") == 2 and lax.axis_size("section") == 2 and lax.axis_size("groups") == 2
    swap = shards == 4
    channels, wires, ticks = readout.shape[1:]
    k1 = first_kernel.reshape(-1, first_kernel.shape[-1])
    k2 = second_kernel.reshape(-1, second_kernel.shape[-1])
    order = order.reshape(shards, -1)
    count = order.shape[1]
    rows = readout.reshape(channels * wires, ticks)
    if paired:
        embed_across = exchanged(embed_weight, "mp", 1)
        embed_beside = exchanged(embed_weight, "section", 1)
        embeds = [embed_weight, embed_beside, embed_across]
        embeds.append(exchanged(embed_across, "section", 1))
        msg, rows, k1, k2, near, query = front(rows, k1, k2, wires, (project_weight,))
    else:
        embeds = [lax.all_gather(embed_weight, ("mp", "section"), axis=0, tiled=True)]
        msg, rows, k1, k2 = front(rows, k1, k2, wires, ())
    got = lax.ppermute(msg, "seq", [(i, i + 1) for i in range(shards - 1)])
    first, second, patch = central(msg, rows, k1, k2, wires, count)
    token, low = mix(patch, embeds)
    tokens = back(got, (first, second, token, low), k1, k2, active)
    if swap:
        chunks = [tokens] + [exchanged(tokens, "seq", flip) for flip in (1, 2)]
        chunks.append(exchanged(chunks[2], "seq", 1))
    else:
        everyone = lax.all_gather(tokens, "seq", axis=0, tiled=True)
        chunks = [everyone[i * (count + EXTRA) : (i + 1) * (count + EXTRA)] for i in range(shards)]
    if paired:
        project_beside = exchanged(project_weight, "section", 1)
        output_beside = exchanged(output_weight, "section", 1)
        near = exchanged(near, "mp", 1)
        far = exchanged(near, "groups", 1)
        query = exchanged(query, "mp", 1)
        output_across = exchanged(output_weight, "mp", 1)
        kv_weights = [project_weight, project_beside, near, far]
        kv_weights.append(exchanged(near, "section", 1))
        kv_weights.append(exchanged(far, "section", 1))
        last_weights = [project_weight, project_beside, query]
        last_weights.append(exchanged(query, "section", 1))
        last_weights += [output_weight, output_beside, output_across]
        last_weights.append(exchanged(output_across, "section", 1))
    else:
        kv_weights = [lax.all_gather(project_weight, ("mp", "section"), axis=0, tiled=True)]
        last_weights = kv_weights + [lax.all_gather(output_weight, ("mp", "section"), axis=0, tiled=True)]
    early, later = shards // 2, shards // 2 + shards // 4
    ready = prepare(order, kv_weights, chunks[:early], swap)
    extra = extend(ready, chunks[:later], last_weights, early, swap)
    result = finish(ready, extra, chunks[later:], swap)
    return result[None]


def solution(mesh):
    in_specs = (
        P(("groups", "mp", "section"), None, "seq", None),
        P(),
        P(),
        P(("mp", "section"), None),
        P(("mp", "section"), None),
        P(("mp", "section"), None),
        P(("groups", "mp", "section"), None),
        P(("groups", "mp", "section"), "seq"),
    )
    out_specs = P(("groups", "mp", "section"), "seq", None)
    return jax.shard_map(layer, mesh=mesh, in_specs=in_specs, out_specs=out_specs, check_vma=False)
```

```python
import functools

import jax
import jax.numpy as jnp
from jax import lax
from jax.experimental import pallas as pl
from jax.experimental.pallas import tpu as pltpu
from jax.sharding import PartitionSpec as P


HEADS = 12
masked_score = -1e30
largest = 3e38
epsilon = 1e-05
BF = jnp.bfloat16
F32 = jnp.float32
EXTRA = 8


def dot(a, b, ca=1, cb=0):
    return lax.dot_general(a, b, (((ca,), (cb,)), ((), ())), preferred_element_type=F32)


def iota(shape, axis):
    return lax.broadcasted_iota(jnp.int32, shape, axis)


def one_hot(mask):
    return jnp.where(mask, 1.0, 0.0).astype(BF)


def silu(v):
    half = 0.5 * v
    return half + half * jnp.tanh(half)


def split_matrix():
    row, col = iota((256, 256), 0), iota((256, 256), 1)
    return one_hot(row == jnp.where(col < 128, 2 * col, 2 * col - 255))


def split_time(rows, splitter):
    even, odd = [], []
    for start in range(0, rows.shape[1], 256):
        both = dot(rows[:, start : start + 256], splitter)
        even.append(both[:, :128])
        odd.append(both[:, 128:])
    if len(even) == 1:
        return even[0], odd[0]
    return jnp.concatenate(even, axis=1), jnp.concatenate(odd, axis=1)


def later(odd):
    moved = pltpu.roll(odd, 1, 1)
    return jnp.where(iota(odd.shape, 1) == 0, 0.0, moved)


def store_taps(taps, base, even, odd):
    height = even.shape[0]
    taps[base : base + height, :] = later(odd).astype(BF)
    taps[base + height : base + 2 * height, :] = even.astype(BF)
    taps[base + 2 * height : base + 3 * height, :] = odd.astype(BF)


def block_of(paired, flip=0):
    if not paired:
        return 0
    return (lax.axis_index("mp") * 2 + lax.axis_index("section")) ^ flip


def wire_rows(x_ref, block, first, last, wires, part):
    shape = ((last - first) * part, 256)
    row, col = iota(shape, 0), iota(shape, 1)
    mixer = one_hot(col == (row % part) * wires + row // part + first)
    return dot(mixer, x_ref[block * 256 : (block + 1) * 256, :]).astype(BF)


def fill_taps(taps, rows, block, splitter, part, channels):
    even, odd = split_time(rows, splitter)
    lagged = later(odd)
    for wire in range(rows.shape[0] // part):
        here = slice(wire * part, (wire + 1) * part)
        base = wire * 3 * channels + block * part
        taps[base : base + part, :] = lagged[here].astype(BF)
        taps[base + channels : base + channels + part, :] = even[here].astype(BF)
        taps[base + 2 * channels : base + 2 * channels + part, :] = odd[here].astype(BF)


def front_kernel(x_hbm, k1_hbm, k2_hbm, *refs, wires, channels, middle, paired):
    if paired:
        project_hbm = refs[0]
        refs = refs[1:]
    msg_ref, x_ref, k1_ref, k2_ref = refs[:4]
    taps, sems = refs[-2:]
    part = 256 // wires
    blocks = channels // part
    loads = []
    for block in range(blocks):
        here = pl.ds(block * 256, 256)
        loads.append(pltpu.make_async_copy(x_hbm.at[here, :], x_ref.at[here, :], sems.at[block]))
    loads.append(pltpu.make_async_copy(k1_hbm, k1_ref, sems.at[blocks]))
    others = [pltpu.make_async_copy(k2_hbm, k2_ref, sems.at[blocks + 1])]
    if paired:
        near_ref, query_ref = refs[4:6]
        depth, width = query_ref.shape
        half = depth // 2
        rows = pl.ds(pl.multiple_of(lax.axis_index("groups") * half, half), half)
        others.append(
            pltpu.make_async_copy(
                project_hbm.at[rows, pl.ds(width, 2 * width)], near_ref, sems.at[blocks + 2]
            )
        )
        others.append(
            pltpu.make_async_copy(project_hbm.at[:, pl.ds(0, width)], query_ref, sems.at[blocks + 3])
        )
    for copy in loads + others:
        copy.start()
    splitter = split_matrix()
    for block in range(blocks):
        loads[block].wait()
        rows = wire_rows(x_ref, block, wires - 3, wires, wires, part)
        fill_taps(taps, rows, block, splitter, part, channels)
    msg_ref[: 2 * channels, :] = taps[7 * channels :, :]
    loads[blocks].wait()
    msg_ref[2 * channels :, :] = silu(dot(k1_ref[...], taps[...], 0, 0)).astype(BF)
    for copy in others:
        copy.wait()


def central_kernel(
    msg_ref, x_ref, k1_ref, k2_ref, first_ref, second_ref, patch, taps1, taps2, *, wires, channels, middle
):
    splitter = split_matrix()
    part = 256 // wires
    for block in range(channels // part):
        rows = wire_rows(x_ref, block, 0, wires - 2, wires, part)
        fill_taps(taps1, rows, block, splitter, part, channels)
    first_ref[...] = dot(k1_ref[3 * channels :, :], taps1[: 6 * channels, :], 0, 0)
    for level in range(1, wires // 2):
        if level == wires // 2 - 1:
            out = msg_ref[2 * channels :, :]
        else:
            start = (2 * level - 1) * 3 * channels
            out = silu(dot(k1_ref[...], taps1[start : start + 9 * channels, :], 0, 0)).astype(BF)
        even, odd = split_time(out, splitter)
        store_taps(taps2, (level - 1) * 3 * middle, even, odd)
    second_ref[...] = dot(k2_ref[6 * middle :, :], taps2[: 3 * middle, :], 0, 0)
    out = silu(dot(k2_ref[...], taps2[...], 0, 0)).astype(BF)
    store_patch(patch, out, splitter)


def embed_mixer():
    row, col = iota((256, 256), 0), iota((256, 256), 1)
    return one_hot(col == (row % 64) * 4 + row // 64)


def mix_kernel(patch, *refs, pieces):
    embed_refs = refs[:pieces]
    token_ref, low_ref, high = refs[pieces:]
    mixer = embed_mixer()
    for piece in reversed(range(pieces)):
        ref = embed_refs[piece]
        parts = ref.shape[0] // 256
        for part in range(parts):
            rows = dot(mixer, ref[part * 256 : (part + 1) * 256, :]).astype(BF)
            base = pl.multiple_of((block_of(pieces > 1, piece) * parts + part) * 128, 128)
            low_ref[pl.ds(base, 128), :] = rows[:128]
            high[pl.ds(base, 128), :] = rows[128:]
    if pieces > 1:
        base = pl.multiple_of(block_of(True, pieces) * 128, 128)
        low_ref[pl.ds(base, 128), :] = jnp.zeros((128, low_ref.shape[1]), BF)
        high[pl.ds(base, 128), :] = jnp.zeros((128, high.shape[1]), BF)
    token_ref[...] = dot(patch[...], high[...], 0, 0)


def blend_kernel(patch, token_ref, embed_ref, out_ref, low_ref):
    rows = dot(embed_mixer(), embed_ref[...]).astype(BF)
    low_ref[...] = rows[:128]
    base = pl.multiple_of(block_of(True, 3) * 128, 128)
    out_ref[...] = token_ref[...] + dot(patch[pl.ds(base, 128), :], rows[128:], 0, 0)


def store_patch(patch, out, splitter):
    even, odd = split_time(out, splitter)
    even, odd = even.astype(BF), odd.astype(BF)
    for block in range(out.shape[0] // 64):
        here = slice(block * 64, (block + 1) * 64)
        patch[block * 128 : block * 128 + 64, :] = even[here]
        patch[block * 128 + 64 : (block + 1) * 128, :] = odd[here]


def back_kernel(
    got_ref, k1_ref, k2_ref, active_ref, first_ref, second_ref, token_ref, low_ref, *refs, channels, middle
):
    out_ref, upper_ref, lower_ref, all1, all2, patch = refs[-6:]
    splitter = split_matrix()
    odd = got_ref[channels : 2 * channels, :].astype(F32)
    all1[:channels, :] = later(odd).astype(BF)
    all1[channels:, :] = got_ref[: 2 * channels, :]
    even, odd = split_time(got_ref[2 * channels :, :], splitter)
    store_taps(all2, 0, even, odd)
    first = silu(first_ref[...] + dot(k1_ref[: 3 * channels, :], all1[...], 0, 0)).astype(BF)
    even, odd = split_time(first, splitter)
    store_taps(all2, 3 * middle, even, odd)
    out = silu(second_ref[...] + dot(k2_ref[: 6 * middle, :], all2[...], 0, 0)).astype(BF)
    store_patch(patch, out, splitter)
    total = token_ref[...] + dot(patch[...], low_ref[...], 0, 0)
    if len(refs) > 6:
        base = pl.multiple_of(block_of(True, 3) * 128, 128)
        total += dot(patch[pl.ds(base, 128), :], refs[0][...], 0, 0)
    count, width = total.shape
    total = total.astype(BF)
    half = count // 2
    out_ref[:count, :] = total
    upper_ref[...] = total[:half]
    lower_ref[:half, :] = total[half:]
    tail = jnp.broadcast_to(active_ref[...].astype(F32), (EXTRA, count))
    tail = jnp.concatenate([tail, jnp.zeros((EXTRA, width - count), F32)], axis=1)
    out_ref[count:, :] = tail.astype(BF)
    lower_ref[half:, :] = tail.astype(BF)


def normal(tokens):
    value = tokens.astype(F32)
    value = value - jnp.mean(value, axis=-1, keepdims=True)
    spread = jnp.mean(value * value, axis=-1, keepdims=True)
    return (value * lax.rsqrt(spread + epsilon)).astype(BF)


def unpack(refs, layout):
    chunks, start = [], 0
    for parts in layout:
        chunks.append(refs[start : start + parts])
        start += parts
    return chunks


def rows_of(chunk):
    parts = [ref[...] for ref in chunk[:-1]]
    parts.append(chunk[-1][: chunk[-1].shape[0] - EXTRA, :])
    return parts[0] if len(parts) == 1 else jnp.concatenate(parts, axis=0)


def flags_of(chunk, count):
    return chunk[-1][chunk[-1].shape[0] - EXTRA :, :count]


def lift(joined, normed, keys, values):
    width = joined.shape[0]
    rows = normed[...]
    keys[...] = dot(rows, joined[:, :width]).astype(BF)
    values[...] = dot(rows, joined[:, width:]).astype(BF)


def collect(sources, target, sems):
    copies = []
    for index, (ref, base, column, align) in enumerate(sources):
        if not isinstance(base, int):
            base = pl.multiple_of(base, align)
        copies.append(
            pltpu.make_async_copy(
                ref.at[:, pl.ds(column, target.shape[1])],
                target.at[pl.ds(base, ref.shape[0]), :],
                sems.at[index],
            )
        )
        copies[-1].start()
    return copies


def place_of(slot, swap):
    position = lax.axis_index("seq")
    return position ^ slot if swap else slot


def prepare_kernel(order_ref, *refs, pieces, chunks, swap):
    kv_refs = refs[:pieces]
    chunk_refs = refs[pieces : pieces + chunks]
    joined, normed, keys, values, perm_ref, sems = refs[pieces + chunks :]
    width = joined.shape[0]
    if pieces > 1:
        own, beside, near, far, near_corner, far_corner = kv_refs
        depth, half = own.shape[0], near.shape[0]
        group = lax.axis_index("groups")
        sources = [
            (own, block_of(True, 0) * depth, width, depth),
            (beside, block_of(True, 1) * depth, width, depth),
        ]
        for flip, first, second in ((2, near, far), (3, near_corner, far_corner)):
            base = block_of(True, flip) * depth
            sources.append((first, base + group * half, 0, half))
            sources.append((second, base + (group ^ 1) * half, 0, half))
    else:
        sources = [(kv_refs[0], 0, width, 1)]
    copies = collect(sources, joined, sems)
    shards, count = order_ref.shape
    square = iota((count, count), 0) == iota((count, count), 1)
    lane = iota((1, count), 1)
    labels = jnp.concatenate([lane + place_of(slot, swap) * count for slot in range(shards)], axis=1)
    labels = labels.astype(F32)
    for slot in range(shards):
        row = order_ref[pl.ds(place_of(slot, swap), 1), :].astype(F32)
        across = jnp.broadcast_to(row, (count, count))
        down = jnp.sum(jnp.where(square, across, 0.0), axis=1, keepdims=True)
        perm_ref[slot * count : (slot + 1) * count, :] = one_hot(labels == down)
    for slot, ref in enumerate(chunk_refs):
        normed[slot * count : (slot + 1) * count, :] = normal(rows_of([ref]))
    for copy in copies:
        copy.wait()
    lift(joined, normed, keys, values)


def extend_kernel(perm_ref, joined, normed0, *refs, pieces, layout, early, swap):
    total = sum(layout)
    chunks = unpack(refs[:total], layout)
    query_refs = refs[total : total + pieces]
    query, keys1, values1, token_ref, picked_ref, on_ref, normed1, sems = refs[total + pieces :]
    count = token_ref.shape[0]
    copies = collect(weight_rows(query_refs), query, sems)
    for slot, chunk in enumerate(chunks[early:]):
        normed1[slot * count : (slot + 1) * count, :] = normal(rows_of(chunk))
    lift(joined, normed1, keys1, values1)
    own = own_rows(perm_ref, count, swap)
    near, far = early * count, len(layout) * count
    picked_ref[...] = dot(own[:, :near], normed0[...]) + dot(own[:, near:far], normed1[...])
    on, token = flags_and_tokens(perm_ref, own, chunks, 0)
    on_ref[...] = on
    token_ref[...] = token
    for copy in copies:
        copy.wait()


def weight_rows(refs):
    sources = []
    for piece, ref in enumerate(refs):
        depth = ref.shape[0]
        sources.append((ref, block_of(len(refs) > 1, piece) * depth, 0, depth))
    return sources


def own_rows(perm_ref, count, swap):
    slot = 0 if swap else lax.axis_index("seq")
    return perm_ref[pl.ds(pl.multiple_of(slot * count, count), count), :]


def flags_and_tokens(perm_ref, own, chunks, first):
    count = own.shape[0]
    on = token = 0.0
    for slot, chunk in enumerate(chunks):
        here = slice((first + slot) * count, (first + slot + 1) * count)
        on += dot(flags_of(chunk, count), perm_ref[here, :])
        token += dot(own[:, here], rows_of(chunk))
    return on, token


def finish_kernel(
    perm_ref, joined, keys0, values0, keys1, values1, query, token_ref, picked_ref, on_ref, *refs,
    pieces, layout, swap
):
    total = sum(layout)
    chunks = unpack(refs[:total], layout)
    output_refs = refs[total : total + pieces]
    out_ref, output, normed2, keys2, values2, cap, mixed, sems = refs[total + pieces :]
    copies = collect(weight_rows(output_refs), output, sems)
    count, width = token_ref.shape
    first = perm_ref.shape[0] // count - len(layout)
    for slot, chunk in enumerate(chunks):
        normed2[slot * count : (slot + 1) * count, :] = normal(rows_of(chunk))
    lift(joined, normed2, keys2, values2)
    own = own_rows(perm_ref, count, swap)
    picked = (picked_ref[...] + dot(own[:, first * count :], normed2[...])).astype(BF)
    head = width // HEADS
    queries = (dot(picked, query[...]) * head ** (-0.5)).astype(BF)
    on, token = flags_and_tokens(perm_ref, own, chunks, first)
    on += on_ref[...]
    token += token_ref[...]
    allowed = (own.astype(F32) + jnp.broadcast_to(on[:1], own.shape)) > 0.5
    cap[...] = jnp.where(allowed, largest, masked_score)
    low = iota((count, 2 * head), 1) < head
    groups = ((keys0, values0), (keys1, values1), (keys2, values2))
    for pair in range(HEADS // 2):
        here = slice(pair * 2 * head, (pair + 1) * 2 * head)
        part_query = queries[:, here]
        zero = jnp.zeros_like(part_query)
        both = [jnp.where(low, part_query, zero), jnp.where(low, zero, part_query)]
        both = jnp.concatenate(both, axis=0)
        scores = jnp.concatenate([dot(both, keys[:, here], 1, 1) for keys, _ in groups], axis=1)
        weights, scale = [], []
        for half in range(2):
            score = jnp.minimum(scores[half * count : (half + 1) * count], cap[...])
            weight = jnp.exp(score - jnp.max(score, axis=-1, keepdims=True))
            scale.append(1.0 / jnp.sum(weight, axis=-1, keepdims=True))
            weights.append(weight.astype(BF))
        weights = jnp.concatenate(weights, axis=0)
        part, start = 0.0, 0
        for keys, values in groups:
            part += dot(weights[:, start : start + keys.shape[0]], values[:, here])
            start += keys.shape[0]
        mixed[:, here] = jnp.where(low, part[:count] * scale[0], part[count:] * scale[1]).astype(BF)
    for copy in copies:
        copy.wait()
    out_ref[...] = (token + dot(mixed[...], output[...])).astype(BF)


def vmem():
    return pl.BlockSpec(memory_space=pltpu.VMEM)


def hbm():
    return pl.BlockSpec(memory_space=pl.ANY)


def fixed():
    return pl.BlockSpec(memory_space=pltpu.HBM)


def params(mib):
    return pltpu.CompilerParams(vmem_limit_bytes=mib * 1024 * 1024)


def array(shape, dtype=BF):
    return jax.ShapeDtypeStruct(shape, dtype)


def front(rows, k1, k2, wires, weights):
    channels = rows.shape[0] // wires
    middle = k1.shape[1]
    length = rows.shape[1] // 2
    outs = [array((2 * channels + middle, length)), array(rows.shape), array(k1.shape), array(k2.shape)]
    if weights:
        depth, width = weights[0].shape
        outs += [array((depth // 2, width // 3 * 2)), array((depth, width // 3))]
    operands = [pltpu.with_memory_space_constraint(v, pltpu.HBM) for v in (rows, k1, k2, *weights)]
    return pl.pallas_call(
        functools.partial(
            front_kernel, wires=wires, channels=channels, middle=middle, paired=len(weights) > 0
        ),
        out_shape=outs,
        in_specs=[fixed()] * len(operands),
        out_specs=[vmem()] * len(outs),
        scratch_shapes=[
            pltpu.VMEM((9 * channels, length), BF),
            pltpu.SemaphoreType.DMA((channels * wires // 256 + 4,)),
        ],
        compiler_params=params(8),
        name="front",
    )(*operands)


def central(msg, rows, k1, k2, wires, count):
    middle, outer = k1.shape[1], k2.shape[1]
    channels = k1.shape[0] // 9
    length = msg.shape[1]
    return pl.pallas_call(
        functools.partial(central_kernel, wires=wires, channels=channels, middle=middle),
        out_shape=(
            array((middle, length), F32),
            array((outer, length // 2), F32),
            array((2 * outer, count)),
        ),
        in_specs=[vmem()] * 4,
        out_specs=[vmem()] * 3,
        scratch_shapes=[
            pltpu.VMEM(((wires - 2) * 3 * channels, length), BF),
            pltpu.VMEM(((wires // 2 - 1) * 3 * middle, length // 2), BF),
        ],
        compiler_params=params(10),
        name="central",
    )(msg, rows, k1, k2)


def mix(patch, embeds):
    width = embeds[0].shape[1]
    return pl.pallas_call(
        functools.partial(mix_kernel, pieces=len(embeds)),
        out_shape=(array((patch.shape[1], width), F32), array((patch.shape[0], width))),
        in_specs=[vmem()] * (1 + len(embeds)),
        out_specs=[vmem()] * 2,
        scratch_shapes=[pltpu.VMEM((patch.shape[0], width), BF)],
        compiler_params=params(8),
        name="mix",
    )(patch, *embeds)


def blend(patch, token, embed):
    return pl.pallas_call(
        blend_kernel,
        out_shape=(array(token.shape, F32), array((embed.shape[0] // 2, embed.shape[1]))),
        in_specs=[vmem()] * 3,
        out_specs=[vmem()] * 2,
        compiler_params=params(6),
        name="blend",
    )(patch, token, embed)


def back(got, k1, k2, active, *parts):
    middle = k1.shape[1]
    channels = k1.shape[0] // 9
    length = got.shape[1]
    count = active.shape[1]
    half = count // 2
    width = parts[2].shape[1]
    return pl.pallas_call(
        functools.partial(back_kernel, channels=channels, middle=middle),
        out_shape=(array((count + EXTRA, width)), array((half, width)), array((half + EXTRA, width))),
        in_specs=[vmem()] * (4 + len(parts)),
        out_specs=[vmem()] * 3,
        scratch_shapes=[
            pltpu.VMEM((3 * channels, length), BF),
            pltpu.VMEM((6 * middle, length // 2), BF),
            pltpu.VMEM((2 * k2.shape[1], count), BF),
        ],
        compiler_params=params(8),
        name="back",
    )(got, k1, k2, active, *parts)


def prepare(order, weights, chunks, swap):
    shards, count = order.shape
    width = chunks[0].shape[1]
    size, near = shards * count, len(chunks) * count
    return pl.pallas_call(
        functools.partial(prepare_kernel, pieces=len(weights), chunks=len(chunks), swap=swap),
        out_shape=(array((width, 2 * width)),) + (array((near, width)),) * 3 + (array((size, size)),),
        in_specs=[vmem()] + [fixed()] + [hbm()] * (len(weights) - 1) + [vmem()] * len(chunks),
        out_specs=[vmem()] * 5,
        scratch_shapes=[pltpu.SemaphoreType.DMA((len(weights),))],
        compiler_params=params(8 + size // 128),
        name="prepare",
    )(order, *weights, *chunks)


def extend(ready, chunks, weights, early, swap):
    joined, normed, _, _, perm = ready
    width = joined.shape[0]
    size = perm.shape[0]
    count = chunks[0][0].shape[0] - EXTRA
    far = (len(chunks) - early) * count
    pieces = len(weights)
    layout = tuple(len(chunk) for chunk in chunks)
    flat = [part for chunk in chunks for part in chunk]
    return pl.pallas_call(
        functools.partial(extend_kernel, pieces=pieces, layout=layout, early=early, swap=swap),
        out_shape=(
            array((width, width)),
            array((far, width)),
            array((far, width)),
            array((count, width), F32),
            array((count, width), F32),
            array((EXTRA, size), F32),
        ),
        in_specs=[vmem()] * (3 + len(flat)) + [fixed()] + [hbm()] * (pieces - 1),
        out_specs=[vmem()] * 6,
        scratch_shapes=[pltpu.VMEM((far, width), BF), pltpu.SemaphoreType.DMA((pieces,))],
        compiler_params=params(8 + size // 128),
        name="extend",
    )(perm, joined, normed, *flat, *weights)


def finish(ready, extra, chunks, weights, swap):
    joined, _, keys, values, perm = ready
    query, keys1, values1, token, picked, on = extra
    width = joined.shape[0]
    size = perm.shape[0]
    count = token.shape[0]
    far = len(chunks) * count
    pieces = len(weights)
    layout = tuple(len(chunk) for chunk in chunks)
    flat = [part for chunk in chunks for part in chunk]
    return pl.pallas_call(
        functools.partial(finish_kernel, pieces=pieces, layout=layout, swap=swap),
        out_shape=array((count, width)),
        in_specs=[vmem()] * (10 + len(flat)) + [fixed()] + [hbm()] * (pieces - 1),
        out_specs=vmem(),
        scratch_shapes=[
            pltpu.VMEM((width, width), BF),
            pltpu.VMEM((far, width), BF),
            pltpu.VMEM((far, width), BF),
            pltpu.VMEM((far, width), BF),
            pltpu.VMEM((count, size), F32),
            pltpu.VMEM((count, width), BF),
            pltpu.SemaphoreType.DMA((pieces,)),
        ],
        compiler_params=params(8 + size // 64),
        name="finish",
    )(perm, joined, keys, values, keys1, values1, query, token, picked, on, *flat, *weights)


def exchanged(value, axis, flip):
    count = lax.axis_size(axis)
    return lax.ppermute(value, axis, [(i, i ^ flip) for i in range(count)])


def layer(
    readout, first_kernel, second_kernel, embed_weight, project_weight, output_weight, order, active
):
    shards = lax.axis_size("seq")
    paired = lax.axis_size("mp") == 2 and lax.axis_size("section") == 2 and lax.axis_size("groups") == 2
    swap = shards == 4
    channels, wires, ticks = readout.shape[1:]
    k1 = first_kernel.reshape(-1, first_kernel.shape[-1])
    k2 = second_kernel.reshape(-1, second_kernel.shape[-1])
    order = order.reshape(shards, -1)
    count = order.shape[1]
    rows = readout.reshape(channels * wires, ticks)
    if paired:
        embed_across = exchanged(embed_weight, "mp", 1)
        embed_beside = exchanged(embed_weight, "section", 1)
        embed_corner = exchanged(embed_across, "section", 1)
        embeds = [embed_weight, embed_beside, embed_across]
        msg, rows, k1, k2, near, query = front(rows, k1, k2, wires, (project_weight,))
    else:
        embeds = [lax.all_gather(embed_weight, ("mp", "section"), axis=0, tiled=True)]
        msg, rows, k1, k2 = front(rows, k1, k2, wires, ())
    got = lax.ppermute(msg, "seq", [(i, i + 1) for i in range(shards - 1)])
    first, second, patch = central(msg, rows, k1, k2, wires, count)
    token, low = mix(patch, embeds)
    parts = [first, second, token, low]
    if paired:
        parts[2], corner_low = blend(patch, token, embed_corner)
        parts.append(corner_low)
    tokens, upper, lower = back(got, k1, k2, active, *parts)
    if swap:
        chunks = [[tokens], [exchanged(tokens, "seq", 1)]]
        chunks.append([exchanged(upper, "seq", 2), exchanged(lower, "seq", 2)])
        chunks.append([exchanged(chunks[2][0], "seq", 1), exchanged(chunks[2][1], "seq", 1)])
    else:
        everyone = lax.all_gather(tokens, "seq", axis=0, tiled=True)
        each = count + EXTRA
        chunks = [[everyone[i * each : (i + 1) * each]] for i in range(shards)]
    if paired:
        project_beside = exchanged(project_weight, "section", 1)
        output_beside = exchanged(output_weight, "section", 1)
        near = exchanged(near, "mp", 1)
        far = exchanged(near, "groups", 1)
        query = exchanged(query, "mp", 1)
        output_across = exchanged(output_weight, "mp", 1)
        kv_weights = [project_weight, project_beside, near, far]
        kv_weights.append(exchanged(near, "section", 1))
        kv_weights.append(exchanged(far, "section", 1))
        query_weights = [project_weight, project_beside, query]
        query_weights.append(exchanged(query, "section", 1))
        output_weights = [output_weight, output_beside, output_across]
        output_weights.append(exchanged(output_across, "section", 1))
    else:
        kv_weights = [lax.all_gather(project_weight, ("mp", "section"), axis=0, tiled=True)]
        query_weights = kv_weights
        output_weights = [lax.all_gather(output_weight, ("mp", "section"), axis=0, tiled=True)]
    early, later = shards // 2, shards // 2 + shards // 4
    ready = prepare(order, kv_weights, [chunk[0] for chunk in chunks[:early]], swap)
    extra = extend(ready, chunks[:later], query_weights, early, swap)
    result = finish(ready, extra, chunks[later:], output_weights, swap)
    return result[None]


def solution(mesh):
    in_specs = (
        P(("groups", "mp", "section"), None, "seq", None),
        P(),
        P(),
        P(("mp", "section"), None),
        P(("mp", "section"), None),
        P(("mp", "section"), None),
        P(("groups", "mp", "section"), None),
        P(("groups", "mp", "section"), "seq"),
    )
    out_specs = P(("groups", "mp", "section"), "seq", None)
    return jax.shard_map(layer, mesh=mesh, in_specs=in_specs, out_specs=out_specs, check_vma=False)
```

```python
import functools

import jax
import jax.numpy as jnp
from jax import lax
from jax.experimental import pallas as pl
from jax.experimental.pallas import tpu as pltpu
from jax.sharding import PartitionSpec as P


HEADS = 12
masked_score = -1e30
largest = 3e38
epsilon = 1e-05
BF = jnp.bfloat16
F32 = jnp.float32
EXTRA = 8


def dot(a, b, ca=1, cb=0):
    return lax.dot_general(a, b, (((ca,), (cb,)), ((), ())), preferred_element_type=F32)


def iota(shape, axis):
    return lax.broadcasted_iota(jnp.int32, shape, axis)


def one_hot(mask):
    return jnp.where(mask, 1.0, 0.0).astype(BF)


def silu(v):
    half = 0.5 * v
    return half + half * jnp.tanh(half)


def split_matrix():
    row, col = iota((256, 256), 0), iota((256, 256), 1)
    return one_hot(row == jnp.where(col < 128, 2 * col, 2 * col - 255))


def split_time(rows, splitter):
    even, odd = [], []
    for start in range(0, rows.shape[1], 256):
        both = dot(rows[:, start : start + 256], splitter)
        even.append(both[:, :128])
        odd.append(both[:, 128:])
    if len(even) == 1:
        return even[0], odd[0]
    return jnp.concatenate(even, axis=1), jnp.concatenate(odd, axis=1)


def later(odd):
    moved = pltpu.roll(odd, 1, 1)
    return jnp.where(iota(odd.shape, 1) == 0, 0.0, moved)


def store_taps(taps, base, even, odd):
    height = even.shape[0]
    taps[base : base + height, :] = later(odd).astype(BF)
    taps[base + height : base + 2 * height, :] = even.astype(BF)
    taps[base + 2 * height : base + 3 * height, :] = odd.astype(BF)


def block_of(paired, flip=0):
    if not paired:
        return 0
    return (lax.axis_index("mp") * 2 + lax.axis_index("section")) ^ flip


def wire_rows(x_ref, block, first, last, wires, part):
    shape = ((last - first) * part, 256)
    row, col = iota(shape, 0), iota(shape, 1)
    mixer = one_hot(col == (row % part) * wires + row // part + first)
    return dot(mixer, x_ref[block * 256 : (block + 1) * 256, :]).astype(BF)


def fill_taps(taps, rows, block, splitter, part, channels):
    even, odd = split_time(rows, splitter)
    lagged = later(odd)
    for wire in range(rows.shape[0] // part):
        here = slice(wire * part, (wire + 1) * part)
        base = wire * 3 * channels + block * part
        taps[base : base + part, :] = lagged[here].astype(BF)
        taps[base + channels : base + channels + part, :] = even[here].astype(BF)
        taps[base + 2 * channels : base + 2 * channels + part, :] = odd[here].astype(BF)


def front_kernel(x_hbm, k1_hbm, k2_hbm, *refs, wires, channels, middle, paired):
    if paired:
        project_hbm = refs[0]
        refs = refs[1:]
    msg_ref, x_ref, k1_ref, k2_ref = refs[:4]
    taps, sems = refs[-2:]
    part = 256 // wires
    blocks = channels // part
    loads = []
    for block in range(blocks):
        here = pl.ds(block * 256, 256)
        loads.append(pltpu.make_async_copy(x_hbm.at[here, :], x_ref.at[here, :], sems.at[block]))
    loads.append(pltpu.make_async_copy(k1_hbm, k1_ref, sems.at[blocks]))
    others = [pltpu.make_async_copy(k2_hbm, k2_ref, sems.at[blocks + 1])]
    if paired:
        near_ref, query_ref = refs[4:6]
        depth, width = query_ref.shape
        half = depth // 2
        rows = pl.ds(pl.multiple_of(lax.axis_index("groups") * half, half), half)
        others.append(
            pltpu.make_async_copy(
                project_hbm.at[rows, pl.ds(width, 2 * width)], near_ref, sems.at[blocks + 2]
            )
        )
        others.append(
            pltpu.make_async_copy(project_hbm.at[:, pl.ds(0, width)], query_ref, sems.at[blocks + 3])
        )
    for copy in loads + others:
        copy.start()
    splitter = split_matrix()
    for block in range(blocks):
        loads[block].wait()
        rows = wire_rows(x_ref, block, wires - 3, wires, wires, part)
        fill_taps(taps, rows, block, splitter, part, channels)
    msg_ref[: 2 * channels, :] = taps[7 * channels :, :]
    loads[blocks].wait()
    msg_ref[2 * channels :, :] = silu(dot(k1_ref[...], taps[...], 0, 0)).astype(BF)
    for copy in others:
        copy.wait()


def central_kernel(
    msg_ref, x_ref, k1_ref, k2_ref, first_ref, second_ref, patch, taps1, taps2, *, wires, channels, middle
):
    splitter = split_matrix()
    part = 256 // wires
    for block in range(channels // part):
        rows = wire_rows(x_ref, block, 0, wires - 2, wires, part)
        fill_taps(taps1, rows, block, splitter, part, channels)
    first_ref[...] = dot(k1_ref[3 * channels :, :], taps1[: 6 * channels, :], 0, 0)
    for level in range(1, wires // 2):
        if level == wires // 2 - 1:
            out = msg_ref[2 * channels :, :]
        else:
            start = (2 * level - 1) * 3 * channels
            out = silu(dot(k1_ref[...], taps1[start : start + 9 * channels, :], 0, 0)).astype(BF)
        even, odd = split_time(out, splitter)
        store_taps(taps2, (level - 1) * 3 * middle, even, odd)
    second_ref[...] = dot(k2_ref[6 * middle :, :], taps2[: 3 * middle, :], 0, 0)
    out = silu(dot(k2_ref[...], taps2[...], 0, 0)).astype(BF)
    store_patch(patch, out, splitter)


def embed_mixer():
    row, col = iota((256, 256), 0), iota((256, 256), 1)
    return one_hot(col == (row % 64) * 4 + row // 64)


def mix_kernel(patch, *refs, pieces):
    embed_refs = refs[:pieces]
    token_ref, low_ref, high = refs[pieces:]
    mixer = embed_mixer()
    for piece in reversed(range(pieces)):
        ref = embed_refs[piece]
        parts = ref.shape[0] // 256
        for part in range(parts):
            rows = dot(mixer, ref[part * 256 : (part + 1) * 256, :]).astype(BF)
            base = pl.multiple_of((block_of(pieces > 1, piece) * parts + part) * 128, 128)
            low_ref[pl.ds(base, 128), :] = rows[:128]
            high[pl.ds(base, 128), :] = rows[128:]
    if pieces > 1:
        base = pl.multiple_of(block_of(True, pieces) * 128, 128)
        low_ref[pl.ds(base, 128), :] = jnp.zeros((128, low_ref.shape[1]), BF)
        high[pl.ds(base, 128), :] = jnp.zeros((128, high.shape[1]), BF)
    token_ref[...] = dot(patch[...], high[...], 0, 0)


def blend_kernel(patch, token_ref, embed_ref, out_ref, low_ref):
    rows = dot(embed_mixer(), embed_ref[...]).astype(BF)
    low_ref[...] = rows[:128]
    base = pl.multiple_of(block_of(True, 3) * 128, 128)
    out_ref[...] = token_ref[...] + dot(patch[pl.ds(base, 128), :], rows[128:], 0, 0)


def store_patch(patch, out, splitter):
    even, odd = split_time(out, splitter)
    even, odd = even.astype(BF), odd.astype(BF)
    for block in range(out.shape[0] // 64):
        here = slice(block * 64, (block + 1) * 64)
        patch[block * 128 : block * 128 + 64, :] = even[here]
        patch[block * 128 + 64 : (block + 1) * 128, :] = odd[here]


def back_kernel(
    got_ref, k1_ref, k2_ref, active_ref, first_ref, second_ref, token_ref, low_ref, *refs, channels, middle
):
    out_ref, all1, all2, patch = refs[-4:]
    splitter = split_matrix()
    odd = got_ref[channels : 2 * channels, :].astype(F32)
    all1[:channels, :] = later(odd).astype(BF)
    all1[channels:, :] = got_ref[: 2 * channels, :]
    even, odd = split_time(got_ref[2 * channels :, :], splitter)
    store_taps(all2, 0, even, odd)
    first = silu(first_ref[...] + dot(k1_ref[: 3 * channels, :], all1[...], 0, 0)).astype(BF)
    even, odd = split_time(first, splitter)
    store_taps(all2, 3 * middle, even, odd)
    out = silu(second_ref[...] + dot(k2_ref[: 6 * middle, :], all2[...], 0, 0)).astype(BF)
    store_patch(patch, out, splitter)
    total = token_ref[...] + dot(patch[...], low_ref[...], 0, 0)
    if len(refs) > 4:
        base = pl.multiple_of(block_of(True, 3) * 128, 128)
        total += dot(patch[pl.ds(base, 128), :], refs[0][...], 0, 0)
    count, width = total.shape
    out_ref[:count, :] = total.astype(BF)
    tail = jnp.broadcast_to(active_ref[...].astype(F32), (EXTRA, count))
    tail = jnp.concatenate([tail, jnp.zeros((EXTRA, width - count), F32)], axis=1)
    out_ref[count:, :] = tail.astype(BF)


def normal(tokens):
    value = tokens.astype(F32)
    value = value - jnp.mean(value, axis=-1, keepdims=True)
    spread = jnp.mean(value * value, axis=-1, keepdims=True)
    return (value * lax.rsqrt(spread + epsilon)).astype(BF)


def lift(joined, normed, keys, values):
    width = joined.shape[0]
    rows = normed[...]
    keys[...] = dot(rows, joined[:, :width]).astype(BF)
    values[...] = dot(rows, joined[:, width:]).astype(BF)


def collect(sources, target, sems):
    copies = []
    for index, (ref, base, column, align) in enumerate(sources):
        if not isinstance(base, int):
            base = pl.multiple_of(base, align)
        copies.append(
            pltpu.make_async_copy(
                ref.at[:, pl.ds(column, target.shape[1])],
                target.at[pl.ds(base, ref.shape[0]), :],
                sems.at[index],
            )
        )
        copies[-1].start()
    return copies


def place_of(slot, swap):
    position = lax.axis_index("seq")
    return position ^ slot if swap else slot


def prepare_kernel(order_ref, *refs, pieces, chunks, swap):
    kv_refs = refs[:pieces]
    chunk_refs = refs[pieces : pieces + chunks]
    joined, normed, keys, values, perm_ref, sems = refs[pieces + chunks :]
    width = joined.shape[0]
    if pieces > 1:
        own, beside, near, far, near_corner, far_corner = kv_refs
        depth, half = own.shape[0], near.shape[0]
        group = lax.axis_index("groups")
        sources = [
            (own, block_of(True, 0) * depth, width, depth),
            (beside, block_of(True, 1) * depth, width, depth),
        ]
        for flip, first, second in ((2, near, far), (3, near_corner, far_corner)):
            base = block_of(True, flip) * depth
            sources.append((first, base + group * half, 0, half))
            sources.append((second, base + (group ^ 1) * half, 0, half))
    else:
        sources = [(kv_refs[0], 0, width, 1)]
    copies = collect(sources, joined, sems)
    shards, count = order_ref.shape
    square = iota((count, count), 0) == iota((count, count), 1)
    lane = iota((1, count), 1)
    labels = jnp.concatenate([lane + place_of(slot, swap) * count for slot in range(shards)], axis=1)
    labels = labels.astype(F32)
    for slot in range(shards):
        row = order_ref[pl.ds(place_of(slot, swap), 1), :].astype(F32)
        across = jnp.broadcast_to(row, (count, count))
        down = jnp.sum(jnp.where(square, across, 0.0), axis=1, keepdims=True)
        perm_ref[slot * count : (slot + 1) * count, :] = one_hot(labels == down)
    for slot, ref in enumerate(chunk_refs):
        normed[slot * count : (slot + 1) * count, :] = normal(ref[:count, :])
    for copy in copies:
        copy.wait()
    lift(joined, normed, keys, values)


def extend_kernel(perm_ref, joined, normed0, *refs, pieces, chunks, early, swap):
    chunk_refs = refs[:chunks]
    query_refs = refs[chunks : chunks + pieces]
    query, keys1, values1, token_ref, picked_ref, on_ref, normed1, sems = refs[chunks + pieces :]
    count = token_ref.shape[0]
    copies = collect(weight_rows(query_refs), query, sems)
    for slot, ref in enumerate(chunk_refs[early:]):
        normed1[slot * count : (slot + 1) * count, :] = normal(ref[:count, :])
    lift(joined, normed1, keys1, values1)
    own = own_rows(perm_ref, count, swap)
    near, far = early * count, chunks * count
    picked_ref[...] = dot(own[:, :near], normed0[...]) + dot(own[:, near:far], normed1[...])
    on, token = flags_and_tokens(perm_ref, own, chunk_refs, 0)
    on_ref[...] = on
    token_ref[...] = token
    for copy in copies:
        copy.wait()


def weight_rows(refs):
    sources = []
    for piece, ref in enumerate(refs):
        depth = ref.shape[0]
        sources.append((ref, block_of(len(refs) > 1, piece) * depth, 0, depth))
    return sources


def own_rows(perm_ref, count, swap):
    slot = 0 if swap else lax.axis_index("seq")
    return perm_ref[pl.ds(pl.multiple_of(slot * count, count), count), :]


def flags_and_tokens(perm_ref, own, chunk_refs, first):
    count = own.shape[0]
    on = token = 0.0
    for slot, ref in enumerate(chunk_refs):
        here = slice((first + slot) * count, (first + slot + 1) * count)
        on += dot(ref[count:, :count], perm_ref[here, :])
        token += dot(own[:, here], ref[:count, :])
    return on, token


def finish_kernel(
    perm_ref, joined, keys0, values0, keys1, values1, query, token_ref, picked_ref, on_ref, *refs,
    pieces, chunks, swap
):
    chunk_refs = refs[:chunks]
    output_refs = refs[chunks : chunks + pieces]
    out_ref, output, normed2, keys2, values2, cap, mixed, sems = refs[chunks + pieces :]
    copies = collect(weight_rows(output_refs), output, sems)
    count, width = token_ref.shape
    first = perm_ref.shape[0] // count - chunks
    for slot, ref in enumerate(chunk_refs):
        normed2[slot * count : (slot + 1) * count, :] = normal(ref[:count, :])
    lift(joined, normed2, keys2, values2)
    own = own_rows(perm_ref, count, swap)
    picked = (picked_ref[...] + dot(own[:, first * count :], normed2[...])).astype(BF)
    head = width // HEADS
    queries = (dot(picked, query[...]) * head ** (-0.5)).astype(BF)
    on, token = flags_and_tokens(perm_ref, own, chunk_refs, first)
    on += on_ref[...]
    token += token_ref[...]
    allowed = (own.astype(F32) + jnp.broadcast_to(on[:1], own.shape)) > 0.5
    cap[...] = jnp.where(allowed, largest, masked_score)
    low = iota((count, 2 * head), 1) < head
    groups = ((keys0, values0), (keys1, values1), (keys2, values2))
    for pair in range(HEADS // 2):
        here = slice(pair * 2 * head, (pair + 1) * 2 * head)
        part_query = queries[:, here]
        zero = jnp.zeros_like(part_query)
        both = [jnp.where(low, part_query, zero), jnp.where(low, zero, part_query)]
        both = jnp.concatenate(both, axis=0)
        scores = jnp.concatenate([dot(both, keys[:, here], 1, 1) for keys, _ in groups], axis=1)
        weights, scale = [], []
        for half in range(2):
            score = jnp.minimum(scores[half * count : (half + 1) * count], cap[...])
            weight = jnp.exp(score - jnp.max(score, axis=-1, keepdims=True))
            scale.append(1.0 / jnp.sum(weight, axis=-1, keepdims=True))
            weights.append(weight.astype(BF))
        weights = jnp.concatenate(weights, axis=0)
        part, start = 0.0, 0
        for keys, values in groups:
            part += dot(weights[:, start : start + keys.shape[0]], values[:, here])
            start += keys.shape[0]
        mixed[:, here] = jnp.where(low, part[:count] * scale[0], part[count:] * scale[1]).astype(BF)
    for copy in copies:
        copy.wait()
    out_ref[...] = (token + dot(mixed[...], output[...])).astype(BF)


def vmem():
    return pl.BlockSpec(memory_space=pltpu.VMEM)


def hbm():
    return pl.BlockSpec(memory_space=pl.ANY)


def fixed():
    return pl.BlockSpec(memory_space=pltpu.HBM)


def params(mib):
    return pltpu.CompilerParams(vmem_limit_bytes=mib * 1024 * 1024)


def array(shape, dtype=BF):
    return jax.ShapeDtypeStruct(shape, dtype)


def front(rows, k1, k2, wires, weights):
    channels = rows.shape[0] // wires
    middle = k1.shape[1]
    length = rows.shape[1] // 2
    outs = [array((2 * channels + middle, length)), array(rows.shape), array(k1.shape), array(k2.shape)]
    if weights:
        depth, width = weights[0].shape
        outs += [array((depth // 2, width // 3 * 2)), array((depth, width // 3))]
    operands = [pltpu.with_memory_space_constraint(v, pltpu.HBM) for v in (rows, k1, k2, *weights)]
    return pl.pallas_call(
        functools.partial(
            front_kernel, wires=wires, channels=channels, middle=middle, paired=len(weights) > 0
        ),
        out_shape=outs,
        in_specs=[fixed()] * len(operands),
        out_specs=[vmem()] * len(outs),
        scratch_shapes=[
            pltpu.VMEM((9 * channels, length), BF),
            pltpu.SemaphoreType.DMA((channels * wires // 256 + 4,)),
        ],
        compiler_params=params(8),
        name="front",
    )(*operands)


def central(msg, rows, k1, k2, wires, count):
    middle, outer = k1.shape[1], k2.shape[1]
    channels = k1.shape[0] // 9
    length = msg.shape[1]
    return pl.pallas_call(
        functools.partial(central_kernel, wires=wires, channels=channels, middle=middle),
        out_shape=(
            array((middle, length), F32),
            array((outer, length // 2), F32),
            array((2 * outer, count)),
        ),
        in_specs=[vmem()] * 4,
        out_specs=[vmem()] * 3,
        scratch_shapes=[
            pltpu.VMEM(((wires - 2) * 3 * channels, length), BF),
            pltpu.VMEM(((wires // 2 - 1) * 3 * middle, length // 2), BF),
        ],
        compiler_params=params(10),
        name="central",
    )(msg, rows, k1, k2)


def mix(patch, embeds):
    width = embeds[0].shape[1]
    return pl.pallas_call(
        functools.partial(mix_kernel, pieces=len(embeds)),
        out_shape=(array((patch.shape[1], width), F32), array((patch.shape[0], width))),
        in_specs=[vmem()] * (1 + len(embeds)),
        out_specs=[vmem()] * 2,
        scratch_shapes=[pltpu.VMEM((patch.shape[0], width), BF)],
        compiler_params=params(8),
        name="mix",
    )(patch, *embeds)


def blend(patch, token, embed):
    return pl.pallas_call(
        blend_kernel,
        out_shape=(array(token.shape, F32), array((embed.shape[0] // 2, embed.shape[1]))),
        in_specs=[vmem()] * 3,
        out_specs=[vmem()] * 2,
        compiler_params=params(6),
        name="blend",
    )(patch, token, embed)


def back(got, k1, k2, active, *parts):
    middle = k1.shape[1]
    channels = k1.shape[0] // 9
    length = got.shape[1]
    count = active.shape[1]
    width = parts[2].shape[1]
    return pl.pallas_call(
        functools.partial(back_kernel, channels=channels, middle=middle),
        out_shape=array((count + EXTRA, width)),
        in_specs=[vmem()] * (4 + len(parts)),
        out_specs=vmem(),
        scratch_shapes=[
            pltpu.VMEM((3 * channels, length), BF),
            pltpu.VMEM((6 * middle, length // 2), BF),
            pltpu.VMEM((2 * k2.shape[1], count), BF),
        ],
        compiler_params=params(8),
        name="back",
    )(got, k1, k2, active, *parts)


def prepare(order, weights, chunks, swap):
    shards, count = order.shape
    width = chunks[0].shape[1]
    size, near = shards * count, len(chunks) * count
    return pl.pallas_call(
        functools.partial(prepare_kernel, pieces=len(weights), chunks=len(chunks), swap=swap),
        out_shape=(array((width, 2 * width)),) + (array((near, width)),) * 3 + (array((size, size)),),
        in_specs=[vmem()] + [fixed()] + [hbm()] * (len(weights) - 1) + [vmem()] * len(chunks),
        out_specs=[vmem()] * 5,
        scratch_shapes=[pltpu.SemaphoreType.DMA((len(weights),))],
        compiler_params=params(8 + size // 128),
        name="prepare",
    )(order, *weights, *chunks)


def extend(ready, chunks, weights, early, swap):
    joined, normed, _, _, perm = ready
    width = joined.shape[0]
    size = perm.shape[0]
    count = chunks[0].shape[0] - EXTRA
    far = (len(chunks) - early) * count
    pieces = len(weights)
    return pl.pallas_call(
        functools.partial(extend_kernel, pieces=pieces, chunks=len(chunks), early=early, swap=swap),
        out_shape=(
            array((width, width)),
            array((far, width)),
            array((far, width)),
            array((count, width), F32),
            array((count, width), F32),
            array((EXTRA, size), F32),
        ),
        in_specs=[vmem()] * (3 + len(chunks)) + [fixed()] + [hbm()] * (pieces - 1),
        out_specs=[vmem()] * 6,
        scratch_shapes=[pltpu.VMEM((far, width), BF), pltpu.SemaphoreType.DMA((pieces,))],
        compiler_params=params(8 + size // 128),
        name="extend",
    )(perm, joined, normed, *chunks, *weights)


def finish(ready, extra, chunks, weights, swap):
    joined, _, keys, values, perm = ready
    query, keys1, values1, token, picked, on = extra
    width = joined.shape[0]
    size = perm.shape[0]
    count = token.shape[0]
    far = len(chunks) * count
    pieces = len(weights)
    return pl.pallas_call(
        functools.partial(finish_kernel, pieces=pieces, chunks=len(chunks), swap=swap),
        out_shape=array((count, width)),
        in_specs=[vmem()] * (10 + len(chunks)) + [fixed()] + [hbm()] * (pieces - 1),
        out_specs=vmem(),
        scratch_shapes=[
            pltpu.VMEM((width, width), BF),
            pltpu.VMEM((far, width), BF),
            pltpu.VMEM((far, width), BF),
            pltpu.VMEM((far, width), BF),
            pltpu.VMEM((count, size), F32),
            pltpu.VMEM((count, width), BF),
            pltpu.SemaphoreType.DMA((pieces,)),
        ],
        compiler_params=params(8 + size // 64),
        name="finish",
    )(perm, joined, keys, values, keys1, values1, query, token, picked, on, *chunks, *weights)


def exchanged(value, axis, flip):
    count = lax.axis_size(axis)
    return lax.ppermute(value, axis, [(i, i ^ flip) for i in range(count)])


def layer(
    readout, first_kernel, second_kernel, embed_weight, project_weight, output_weight, order, active
):
    shards = lax.axis_size("seq")
    paired = lax.axis_size("mp") == 2 and lax.axis_size("section") == 2 and lax.axis_size("groups") == 2
    swap = shards == 4
    channels, wires, ticks = readout.shape[1:]
    k1 = first_kernel.reshape(-1, first_kernel.shape[-1])
    k2 = second_kernel.reshape(-1, second_kernel.shape[-1])
    order = order.reshape(shards, -1)
    count = order.shape[1]
    rows = readout.reshape(channels * wires, ticks)
    if paired:
        embed_across = exchanged(embed_weight, "mp", 1)
        embed_beside = exchanged(embed_weight, "section", 1)
        embed_corner = exchanged(embed_across, "section", 1)
        embeds = [embed_weight, embed_beside, embed_across]
        msg, rows, k1, k2, near, query = front(rows, k1, k2, wires, (project_weight,))
    else:
        embeds = [lax.all_gather(embed_weight, ("mp", "section"), axis=0, tiled=True)]
        msg, rows, k1, k2 = front(rows, k1, k2, wires, ())
    got = lax.ppermute(msg, "seq", [(i, i + 1) for i in range(shards - 1)])
    first, second, patch = central(msg, rows, k1, k2, wires, count)
    token, low = mix(patch, embeds)
    parts = [first, second, token, low]
    if paired:
        parts[2], corner_low = blend(patch, token, embed_corner)
        parts.append(corner_low)
    tokens = back(got, k1, k2, active, *parts)
    if swap:
        chunks = [tokens] + [exchanged(tokens, "seq", flip) for flip in (1, 2)]
        chunks.append(exchanged(chunks[2], "seq", 1))
    else:
        everyone = lax.all_gather(tokens, "seq", axis=0, tiled=True)
        each = count + EXTRA
        chunks = [everyone[i * each : (i + 1) * each] for i in range(shards)]
    if paired:
        project_beside = exchanged(project_weight, "section", 1)
        output_beside = exchanged(output_weight, "section", 1)
        near = exchanged(near, "mp", 1)
        far = exchanged(near, "groups", 1)
        query = exchanged(query, "mp", 1)
        output_across = exchanged(output_weight, "mp", 1)
        kv_weights = [project_weight, project_beside, near, far]
        kv_weights.append(exchanged(near, "section", 1))
        kv_weights.append(exchanged(far, "section", 1))
        query_weights = [project_weight, project_beside, query]
        query_weights.append(exchanged(query, "section", 1))
        output_weights = [output_weight, output_beside, output_across]
        output_weights.append(exchanged(output_across, "section", 1))
    else:
        kv_weights = [lax.all_gather(project_weight, ("mp", "section"), axis=0, tiled=True)]
        query_weights = kv_weights
        output_weights = [lax.all_gather(output_weight, ("mp", "section"), axis=0, tiled=True)]
    early, later = shards // 2, shards // 2 + shards // 4
    ready = prepare(order, kv_weights, chunks[:early], swap)
    extra = extend(ready, chunks[:later], query_weights, early, swap)
    result = finish(ready, extra, chunks[later:], output_weights, swap)
    return result[None]


def solution(mesh):
    in_specs = (
        P(("groups", "mp", "section"), None, "seq", None),
        P(),
        P(),
        P(("mp", "section"), None),
        P(("mp", "section"), None),
        P(("mp", "section"), None),
        P(("groups", "mp", "section"), None),
        P(("groups", "mp", "section"), "seq"),
    )
    out_specs = P(("groups", "mp", "section"), "seq", None)
    return jax.shard_map(layer, mesh=mesh, in_specs=in_specs, out_specs=out_specs, check_vma=False)
```

```python
import functools

import jax
import jax.numpy as jnp
from jax import lax
from jax.experimental import pallas as pl
from jax.experimental.pallas import tpu as pltpu
from jax.sharding import PartitionSpec as P


HEADS = 12
masked_score = -1e30
largest = 3e38
epsilon = 1e-05
BF = jnp.bfloat16
F32 = jnp.float32
EXTRA = 8


def dot(a, b, ca=1, cb=0):
    return lax.dot_general(a, b, (((ca,), (cb,)), ((), ())), preferred_element_type=F32)


def iota(shape, axis):
    return lax.broadcasted_iota(jnp.int32, shape, axis)


def one_hot(mask):
    return jnp.where(mask, 1.0, 0.0).astype(BF)


def silu(v):
    half = 0.5 * v
    return half + half * jnp.tanh(half)


def split_matrix():
    row, col = iota((256, 256), 0), iota((256, 256), 1)
    return one_hot(row == jnp.where(col < 128, 2 * col, 2 * col - 255))


def split_time(rows, splitter):
    even, odd = [], []
    for start in range(0, rows.shape[1], 256):
        both = dot(rows[:, start : start + 256], splitter)
        even.append(both[:, :128])
        odd.append(both[:, 128:])
    if len(even) == 1:
        return even[0], odd[0]
    return jnp.concatenate(even, axis=1), jnp.concatenate(odd, axis=1)


def later(odd):
    moved = pltpu.roll(odd, 1, 1)
    return jnp.where(iota(odd.shape, 1) == 0, 0.0, moved)


def store_taps(taps, base, even, odd):
    height = even.shape[0]
    taps[base : base + height, :] = later(odd).astype(BF)
    taps[base + height : base + 2 * height, :] = even.astype(BF)
    taps[base + 2 * height : base + 3 * height, :] = odd.astype(BF)


def block_of(paired, flip=0):
    if not paired:
        return 0
    return (lax.axis_index("mp") * 2 + lax.axis_index("section")) ^ flip


def wire_rows(x_ref, block, first, last, wires, part):
    shape = ((last - first) * part, 256)
    row, col = iota(shape, 0), iota(shape, 1)
    mixer = one_hot(col == (row % part) * wires + row // part + first)
    return dot(mixer, x_ref[block * 256 : (block + 1) * 256, :]).astype(BF)


def fill_taps(taps, rows, block, splitter, part, channels):
    even, odd = split_time(rows, splitter)
    lagged = later(odd)
    for wire in range(rows.shape[0] // part):
        here = slice(wire * part, (wire + 1) * part)
        base = wire * 3 * channels + block * part
        taps[base : base + part, :] = lagged[here].astype(BF)
        taps[base + channels : base + channels + part, :] = even[here].astype(BF)
        taps[base + 2 * channels : base + 2 * channels + part, :] = odd[here].astype(BF)


def front_kernel(x_hbm, k1_hbm, k2_hbm, *refs, wires, channels, middle, paired):
    if paired:
        project_hbm = refs[0]
        refs = refs[1:]
    msg_ref, x_ref, k1_ref, k2_ref = refs[:4]
    taps, sems = refs[-2:]
    part = 256 // wires
    blocks = channels // part
    loads = []
    for block in range(blocks):
        here = pl.ds(block * 256, 256)
        loads.append(pltpu.make_async_copy(x_hbm.at[here, :], x_ref.at[here, :], sems.at[block]))
    loads.append(pltpu.make_async_copy(k1_hbm, k1_ref, sems.at[blocks]))
    others = [pltpu.make_async_copy(k2_hbm, k2_ref, sems.at[blocks + 1])]
    if paired:
        near_ref, query_ref = refs[4:6]
        depth, width = query_ref.shape
        half = depth // 2
        rows = pl.ds(pl.multiple_of(lax.axis_index("groups") * half, half), half)
        others.append(
            pltpu.make_async_copy(
                project_hbm.at[rows, pl.ds(width, 2 * width)], near_ref, sems.at[blocks + 2]
            )
        )
        others.append(
            pltpu.make_async_copy(project_hbm.at[:, pl.ds(0, width)], query_ref, sems.at[blocks + 3])
        )
    for copy in loads + others:
        copy.start()
    splitter = split_matrix()
    for block in range(blocks):
        loads[block].wait()
        rows = wire_rows(x_ref, block, wires - 3, wires, wires, part)
        fill_taps(taps, rows, block, splitter, part, channels)
    msg_ref[: 2 * channels, :] = taps[7 * channels :, :]
    loads[blocks].wait()
    msg_ref[2 * channels :, :] = silu(dot(k1_ref[...], taps[...], 0, 0)).astype(BF)
    for copy in others:
        copy.wait()


def central_kernel(
    msg_ref, x_ref, k1_ref, k2_ref, first_ref, second_ref, patch, taps1, taps2, *, wires, channels, middle
):
    splitter = split_matrix()
    part = 256 // wires
    for block in range(channels // part):
        rows = wire_rows(x_ref, block, 0, wires - 2, wires, part)
        fill_taps(taps1, rows, block, splitter, part, channels)
    first_ref[...] = dot(k1_ref[3 * channels :, :], taps1[: 6 * channels, :], 0, 0)
    for level in range(1, wires // 2):
        if level == wires // 2 - 1:
            out = msg_ref[2 * channels :, :]
        else:
            start = (2 * level - 1) * 3 * channels
            out = silu(dot(k1_ref[...], taps1[start : start + 9 * channels, :], 0, 0)).astype(BF)
        even, odd = split_time(out, splitter)
        store_taps(taps2, (level - 1) * 3 * middle, even, odd)
    second_ref[...] = dot(k2_ref[6 * middle :, :], taps2[: 3 * middle, :], 0, 0)
    out = silu(dot(k2_ref[...], taps2[...], 0, 0)).astype(BF)
    store_patch(patch, out, splitter)


def embed_mixer():
    row, col = iota((256, 256), 0), iota((256, 256), 1)
    return one_hot(col == (row % 64) * 4 + row // 64)


def mix_kernel(patch, *refs, pieces):
    embed_refs = refs[:pieces]
    token_ref, low_ref, high = refs[pieces:]
    mixer = embed_mixer()
    for piece in reversed(range(pieces)):
        ref = embed_refs[piece]
        parts = ref.shape[0] // 256
        for part in range(parts):
            rows = dot(mixer, ref[part * 256 : (part + 1) * 256, :]).astype(BF)
            base = pl.multiple_of((block_of(pieces > 1, piece) * parts + part) * 128, 128)
            low_ref[pl.ds(base, 128), :] = rows[:128]
            high[pl.ds(base, 128), :] = rows[128:]
    if pieces > 1:
        base = pl.multiple_of(block_of(True, pieces) * 128, 128)
        low_ref[pl.ds(base, 128), :] = jnp.zeros((128, low_ref.shape[1]), BF)
        high[pl.ds(base, 128), :] = jnp.zeros((128, high.shape[1]), BF)
    token_ref[...] = dot(patch[...], high[...], 0, 0)


def blend_kernel(patch, token_ref, embed_ref, out_ref, low_ref):
    rows = dot(embed_mixer(), embed_ref[...]).astype(BF)
    low_ref[...] = rows[:128]
    base = pl.multiple_of(block_of(True, 3) * 128, 128)
    out_ref[...] = token_ref[...] + dot(patch[pl.ds(base, 128), :], rows[128:], 0, 0)


def store_patch(patch, out, splitter):
    even, odd = split_time(out, splitter)
    even, odd = even.astype(BF), odd.astype(BF)
    for block in range(out.shape[0] // 64):
        here = slice(block * 64, (block + 1) * 64)
        patch[block * 128 : block * 128 + 64, :] = even[here]
        patch[block * 128 + 64 : (block + 1) * 128, :] = odd[here]


def back_kernel(
    got_ref, k1_ref, k2_ref, active_ref, first_ref, second_ref, token_ref, low_ref, *refs, channels, middle
):
    out_ref, all1, all2, patch = refs[-4:]
    splitter = split_matrix()
    odd = got_ref[channels : 2 * channels, :].astype(F32)
    all1[:channels, :] = later(odd).astype(BF)
    all1[channels:, :] = got_ref[: 2 * channels, :]
    even, odd = split_time(got_ref[2 * channels :, :], splitter)
    store_taps(all2, 0, even, odd)
    first = silu(first_ref[...] + dot(k1_ref[: 3 * channels, :], all1[...], 0, 0)).astype(BF)
    even, odd = split_time(first, splitter)
    store_taps(all2, 3 * middle, even, odd)
    out = silu(second_ref[...] + dot(k2_ref[: 6 * middle, :], all2[...], 0, 0)).astype(BF)
    store_patch(patch, out, splitter)
    total = token_ref[...] + dot(patch[...], low_ref[...], 0, 0)
    if len(refs) > 4:
        base = pl.multiple_of(block_of(True, 3) * 128, 128)
        total += dot(patch[pl.ds(base, 128), :], refs[0][...], 0, 0)
    count, width = total.shape
    total = total.astype(BF)
    for start in range(0, width, count):
        out_ref[start : start + count, :] = total[:, start : start + count]
    out_ref[width:, :] = jnp.broadcast_to(active_ref[...].astype(F32), (EXTRA, count)).astype(BF)


def tokens_of(ref):
    count = ref.shape[1]
    return jnp.concatenate(
        [ref[start : start + count, :] for start in range(0, ref.shape[0] - EXTRA, count)], axis=1
    )


def flags_of(ref):
    return ref[ref.shape[0] - EXTRA :, :]


def normal(tokens):
    value = tokens.astype(F32)
    value = value - jnp.mean(value, axis=-1, keepdims=True)
    spread = jnp.mean(value * value, axis=-1, keepdims=True)
    return (value * lax.rsqrt(spread + epsilon)).astype(BF)


def lift(joined, normed, keys, values):
    width = joined.shape[0]
    rows = normed[...]
    keys[...] = dot(rows, joined[:, :width]).astype(BF)
    values[...] = dot(rows, joined[:, width:]).astype(BF)


def collect(sources, target, sems):
    copies = []
    for index, (ref, base, column, align) in enumerate(sources):
        if not isinstance(base, int):
            base = pl.multiple_of(base, align)
        copies.append(
            pltpu.make_async_copy(
                ref.at[:, pl.ds(column, target.shape[1])],
                target.at[pl.ds(base, ref.shape[0]), :],
                sems.at[index],
            )
        )
        copies[-1].start()
    return copies


def place_of(slot, swap):
    position = lax.axis_index("seq")
    return position ^ slot if swap else slot


def prepare_kernel(order_ref, *refs, pieces, chunks, swap):
    kv_refs = refs[:pieces]
    chunk_refs = refs[pieces : pieces + chunks]
    joined, normed, keys, values, perm_ref, sems = refs[pieces + chunks :]
    width = joined.shape[0]
    if pieces > 1:
        own, beside, near, far, near_corner, far_corner = kv_refs
        depth, half = own.shape[0], near.shape[0]
        group = lax.axis_index("groups")
        sources = [
            (own, block_of(True, 0) * depth, width, depth),
            (beside, block_of(True, 1) * depth, width, depth),
        ]
        for flip, first, second in ((2, near, far), (3, near_corner, far_corner)):
            base = block_of(True, flip) * depth
            sources.append((first, base + group * half, 0, half))
            sources.append((second, base + (group ^ 1) * half, 0, half))
    else:
        sources = [(kv_refs[0], 0, width, 1)]
    copies = collect(sources, joined, sems)
    shards, count = order_ref.shape
    square = iota((count, count), 0) == iota((count, count), 1)
    lane = iota((1, count), 1)
    labels = jnp.concatenate([lane + place_of(slot, swap) * count for slot in range(shards)], axis=1)
    labels = labels.astype(F32)
    for slot in range(shards):
        row = order_ref[pl.ds(place_of(slot, swap), 1), :].astype(F32)
        across = jnp.broadcast_to(row, (count, count))
        down = jnp.sum(jnp.where(square, across, 0.0), axis=1, keepdims=True)
        perm_ref[slot * count : (slot + 1) * count, :] = one_hot(labels == down)
    for slot, ref in enumerate(chunk_refs):
        normed[slot * count : (slot + 1) * count, :] = normal(tokens_of(ref))
    for copy in copies:
        copy.wait()
    lift(joined, normed, keys, values)


def extend_kernel(perm_ref, joined, normed0, *refs, pieces, chunks, early, swap):
    chunk_refs = refs[:chunks]
    query_refs = refs[chunks : chunks + pieces]
    query, keys1, values1, token_ref, picked_ref, on_ref, normed1, sems = refs[chunks + pieces :]
    count = token_ref.shape[0]
    copies = collect(weight_rows(query_refs), query, sems)
    for slot, ref in enumerate(chunk_refs[early:]):
        normed1[slot * count : (slot + 1) * count, :] = normal(tokens_of(ref))
    lift(joined, normed1, keys1, values1)
    own = own_rows(perm_ref, count, swap)
    near, far = early * count, chunks * count
    picked_ref[...] = dot(own[:, :near], normed0[...]) + dot(own[:, near:far], normed1[...])
    on, token = flags_and_tokens(perm_ref, own, chunk_refs, 0)
    on_ref[...] = on
    token_ref[...] = token
    for copy in copies:
        copy.wait()


def weight_rows(refs):
    sources = []
    for piece, ref in enumerate(refs):
        depth = ref.shape[0]
        sources.append((ref, block_of(len(refs) > 1, piece) * depth, 0, depth))
    return sources


def own_rows(perm_ref, count, swap):
    slot = 0 if swap else lax.axis_index("seq")
    return perm_ref[pl.ds(pl.multiple_of(slot * count, count), count), :]


def flags_and_tokens(perm_ref, own, chunk_refs, first):
    count = own.shape[0]
    on = token = 0.0
    for slot, ref in enumerate(chunk_refs):
        here = slice((first + slot) * count, (first + slot + 1) * count)
        on += dot(flags_of(ref), perm_ref[here, :])
        token += dot(own[:, here], tokens_of(ref))
    return on, token


def finish_kernel(
    perm_ref, joined, keys0, values0, keys1, values1, query, token_ref, picked_ref, on_ref, *refs,
    pieces, chunks, swap
):
    chunk_refs = refs[:chunks]
    output_refs = refs[chunks : chunks + pieces]
    out_ref, output, normed2, keys2, values2, cap, mixed, sems = refs[chunks + pieces :]
    copies = collect(weight_rows(output_refs), output, sems)
    count, width = token_ref.shape
    first = perm_ref.shape[0] // count - chunks
    for slot, ref in enumerate(chunk_refs):
        normed2[slot * count : (slot + 1) * count, :] = normal(tokens_of(ref))
    lift(joined, normed2, keys2, values2)
    own = own_rows(perm_ref, count, swap)
    picked = (picked_ref[...] + dot(own[:, first * count :], normed2[...])).astype(BF)
    head = width // HEADS
    queries = (dot(picked, query[...]) * head ** (-0.5)).astype(BF)
    on, token = flags_and_tokens(perm_ref, own, chunk_refs, first)
    on += on_ref[...]
    token += token_ref[...]
    allowed = (own.astype(F32) + jnp.broadcast_to(on[:1], own.shape)) > 0.5
    cap[...] = jnp.where(allowed, largest, masked_score)
    low = iota((count, 2 * head), 1) < head
    groups = ((keys0, values0), (keys1, values1), (keys2, values2))
    for pair in range(HEADS // 2):
        here = slice(pair * 2 * head, (pair + 1) * 2 * head)
        part_query = queries[:, here]
        zero = jnp.zeros_like(part_query)
        both = [jnp.where(low, part_query, zero), jnp.where(low, zero, part_query)]
        both = jnp.concatenate(both, axis=0)
        scores = jnp.concatenate([dot(both, keys[:, here], 1, 1) for keys, _ in groups], axis=1)
        weights, scale = [], []
        for half in range(2):
            score = jnp.minimum(scores[half * count : (half + 1) * count], cap[...])
            weight = jnp.exp(score - jnp.max(score, axis=-1, keepdims=True))
            scale.append(1.0 / jnp.sum(weight, axis=-1, keepdims=True))
            weights.append(weight.astype(BF))
        weights = jnp.concatenate(weights, axis=0)
        part, start = 0.0, 0
        for keys, values in groups:
            part += dot(weights[:, start : start + keys.shape[0]], values[:, here])
            start += keys.shape[0]
        mixed[:, here] = jnp.where(low, part[:count] * scale[0], part[count:] * scale[1]).astype(BF)
    for copy in copies:
        copy.wait()
    out_ref[...] = (token + dot(mixed[...], output[...])).astype(BF)


def vmem():
    return pl.BlockSpec(memory_space=pltpu.VMEM)


def hbm():
    return pl.BlockSpec(memory_space=pl.ANY)


def fixed():
    return pl.BlockSpec(memory_space=pltpu.HBM)


def params(mib):
    return pltpu.CompilerParams(vmem_limit_bytes=mib * 1024 * 1024)


def array(shape, dtype=BF):
    return jax.ShapeDtypeStruct(shape, dtype)


def front(rows, k1, k2, wires, weights):
    channels = rows.shape[0] // wires
    middle = k1.shape[1]
    length = rows.shape[1] // 2
    outs = [array((2 * channels + middle, length)), array(rows.shape), array(k1.shape), array(k2.shape)]
    if weights:
        depth, width = weights[0].shape
        outs += [array((depth // 2, width // 3 * 2)), array((depth, width // 3))]
    operands = [pltpu.with_memory_space_constraint(v, pltpu.HBM) for v in (rows, k1, k2, *weights)]
    return pl.pallas_call(
        functools.partial(
            front_kernel, wires=wires, channels=channels, middle=middle, paired=len(weights) > 0
        ),
        out_shape=outs,
        in_specs=[fixed()] * len(operands),
        out_specs=[vmem()] * len(outs),
        scratch_shapes=[
            pltpu.VMEM((9 * channels, length), BF),
            pltpu.SemaphoreType.DMA((channels * wires // 256 + 4,)),
        ],
        compiler_params=params(8),
        name="front",
    )(*operands)


def central(msg, rows, k1, k2, wires, count):
    middle, outer = k1.shape[1], k2.shape[1]
    channels = k1.shape[0] // 9
    length = msg.shape[1]
    return pl.pallas_call(
        functools.partial(central_kernel, wires=wires, channels=channels, middle=middle),
        out_shape=(
            array((middle, length), F32),
            array((outer, length // 2), F32),
            array((2 * outer, count)),
        ),
        in_specs=[vmem()] * 4,
        out_specs=[vmem()] * 3,
        scratch_shapes=[
            pltpu.VMEM(((wires - 2) * 3 * channels, length), BF),
            pltpu.VMEM(((wires // 2 - 1) * 3 * middle, length // 2), BF),
        ],
        compiler_params=params(10),
        name="central",
    )(msg, rows, k1, k2)


def mix(patch, embeds):
    width = embeds[0].shape[1]
    return pl.pallas_call(
        functools.partial(mix_kernel, pieces=len(embeds)),
        out_shape=(array((patch.shape[1], width), F32), array((patch.shape[0], width))),
        in_specs=[vmem()] * (1 + len(embeds)),
        out_specs=[vmem()] * 2,
        scratch_shapes=[pltpu.VMEM((patch.shape[0], width), BF)],
        compiler_params=params(8),
        name="mix",
    )(patch, *embeds)


def blend(patch, token, embed):
    return pl.pallas_call(
        blend_kernel,
        out_shape=(array(token.shape, F32), array((embed.shape[0] // 2, embed.shape[1]))),
        in_specs=[vmem()] * 3,
        out_specs=[vmem()] * 2,
        compiler_params=params(6),
        name="blend",
    )(patch, token, embed)


def back(got, k1, k2, active, *parts):
    middle = k1.shape[1]
    channels = k1.shape[0] // 9
    length = got.shape[1]
    count = active.shape[1]
    width = parts[2].shape[1]
    return pl.pallas_call(
        functools.partial(back_kernel, channels=channels, middle=middle),
        out_shape=array((width + EXTRA, count)),
        in_specs=[vmem()] * (4 + len(parts)),
        out_specs=vmem(),
        scratch_shapes=[
            pltpu.VMEM((3 * channels, length), BF),
            pltpu.VMEM((6 * middle, length // 2), BF),
            pltpu.VMEM((2 * k2.shape[1], count), BF),
        ],
        compiler_params=params(8),
        name="back",
    )(got, k1, k2, active, *parts)


def prepare(order, weights, chunks, swap):
    shards, count = order.shape
    width = chunks[0].shape[0] - EXTRA
    size, near = shards * count, len(chunks) * count
    return pl.pallas_call(
        functools.partial(prepare_kernel, pieces=len(weights), chunks=len(chunks), swap=swap),
        out_shape=(array((width, 2 * width)),) + (array((near, width)),) * 3 + (array((size, size)),),
        in_specs=[vmem()] + [fixed()] + [hbm()] * (len(weights) - 1) + [vmem()] * len(chunks),
        out_specs=[vmem()] * 5,
        scratch_shapes=[pltpu.SemaphoreType.DMA((len(weights),))],
        compiler_params=params(8 + size // 128),
        name="prepare",
    )(order, *weights, *chunks)


def extend(ready, chunks, weights, early, swap):
    joined, normed, _, _, perm = ready
    width = joined.shape[0]
    size = perm.shape[0]
    count = chunks[0].shape[1]
    far = (len(chunks) - early) * count
    pieces = len(weights)
    return pl.pallas_call(
        functools.partial(extend_kernel, pieces=pieces, chunks=len(chunks), early=early, swap=swap),
        out_shape=(
            array((width, width)),
            array((far, width)),
            array((far, width)),
            array((count, width), F32),
            array((count, width), F32),
            array((EXTRA, size), F32),
        ),
        in_specs=[vmem()] * (3 + len(chunks)) + [fixed()] + [hbm()] * (pieces - 1),
        out_specs=[vmem()] * 6,
        scratch_shapes=[pltpu.VMEM((far, width), BF), pltpu.SemaphoreType.DMA((pieces,))],
        compiler_params=params(8 + size // 128),
        name="extend",
    )(perm, joined, normed, *chunks, *weights)


def finish(ready, extra, chunks, weights, swap):
    joined, _, keys, values, perm = ready
    query, keys1, values1, token, picked, on = extra
    width = joined.shape[0]
    size = perm.shape[0]
    count = token.shape[0]
    far = len(chunks) * count
    pieces = len(weights)
    return pl.pallas_call(
        functools.partial(finish_kernel, pieces=pieces, chunks=len(chunks), swap=swap),
        out_shape=array((count, width)),
        in_specs=[vmem()] * (10 + len(chunks)) + [fixed()] + [hbm()] * (pieces - 1),
        out_specs=vmem(),
        scratch_shapes=[
            pltpu.VMEM((width, width), BF),
            pltpu.VMEM((far, width), BF),
            pltpu.VMEM((far, width), BF),
            pltpu.VMEM((far, width), BF),
            pltpu.VMEM((count, size), F32),
            pltpu.VMEM((count, width), BF),
            pltpu.SemaphoreType.DMA((pieces,)),
        ],
        compiler_params=params(8 + size // 64),
        name="finish",
    )(perm, joined, keys, values, keys1, values1, query, token, picked, on, *chunks, *weights)


def exchanged(value, axis, flip):
    count = lax.axis_size(axis)
    return lax.ppermute(value, axis, [(i, i ^ flip) for i in range(count)])


def layer(
    readout, first_kernel, second_kernel, embed_weight, project_weight, output_weight, order, active
):
    shards = lax.axis_size("seq")
    paired = lax.axis_size("mp") == 2 and lax.axis_size("section") == 2 and lax.axis_size("groups") == 2
    swap = shards == 4
    channels, wires, ticks = readout.shape[1:]
    k1 = first_kernel.reshape(-1, first_kernel.shape[-1])
    k2 = second_kernel.reshape(-1, second_kernel.shape[-1])
    order = order.reshape(shards, -1)
    count = order.shape[1]
    rows = readout.reshape(channels * wires, ticks)
    if paired:
        embed_across = exchanged(embed_weight, "mp", 1)
        embed_beside = exchanged(embed_weight, "section", 1)
        embed_corner = exchanged(embed_across, "section", 1)
        embeds = [embed_weight, embed_beside, embed_across]
        msg, rows, k1, k2, near, query = front(rows, k1, k2, wires, (project_weight,))
    else:
        embeds = [lax.all_gather(embed_weight, ("mp", "section"), axis=0, tiled=True)]
        msg, rows, k1, k2 = front(rows, k1, k2, wires, ())
    got = lax.ppermute(msg, "seq", [(i, i + 1) for i in range(shards - 1)])
    first, second, patch = central(msg, rows, k1, k2, wires, count)
    token, low = mix(patch, embeds)
    parts = [first, second, token, low]
    if paired:
        parts[2], corner_low = blend(patch, token, embed_corner)
        parts.append(corner_low)
    tokens = back(got, k1, k2, active, *parts)
    if swap:
        chunks = [tokens] + [exchanged(tokens, "seq", flip) for flip in (1, 2)]
        chunks.append(exchanged(chunks[2], "seq", 1))
    else:
        everyone = lax.all_gather(tokens, "seq", axis=0, tiled=True)
        each = everyone.shape[0] // shards
        chunks = [everyone[i * each : (i + 1) * each] for i in range(shards)]
    if paired:
        project_beside = exchanged(project_weight, "section", 1)
        output_beside = exchanged(output_weight, "section", 1)
        near = exchanged(near, "mp", 1)
        far = exchanged(near, "groups", 1)
        query = exchanged(query, "mp", 1)
        output_across = exchanged(output_weight, "mp", 1)
        kv_weights = [project_weight, project_beside, near, far]
        kv_weights.append(exchanged(near, "section", 1))
        kv_weights.append(exchanged(far, "section", 1))
        query_weights = [project_weight, project_beside, query]
        query_weights.append(exchanged(query, "section", 1))
        output_weights = [output_weight, output_beside, output_across]
        output_weights.append(exchanged(output_across, "section", 1))
    else:
        kv_weights = [lax.all_gather(project_weight, ("mp", "section"), axis=0, tiled=True)]
        query_weights = kv_weights
        output_weights = [lax.all_gather(output_weight, ("mp", "section"), axis=0, tiled=True)]
    early, later = shards // 2, shards // 2 + shards // 4
    ready = prepare(order, kv_weights, chunks[:early], swap)
    extra = extend(ready, chunks[:later], query_weights, early, swap)
    result = finish(ready, extra, chunks[later:], output_weights, swap)
    return result[None]


def solution(mesh):
    in_specs = (
        P(("groups", "mp", "section"), None, "seq", None),
        P(),
        P(),
        P(("mp", "section"), None),
        P(("mp", "section"), None),
        P(("mp", "section"), None),
        P(("groups", "mp", "section"), None),
        P(("groups", "mp", "section"), "seq"),
    )
    out_specs = P(("groups", "mp", "section"), "seq", None)
    return jax.shard_map(layer, mesh=mesh, in_specs=in_specs, out_specs=out_specs, check_vma=False)
```

```python
import functools

import jax
import jax.numpy as jnp
from jax import lax
from jax.experimental import pallas as pl
from jax.experimental.pallas import tpu as pltpu
from jax.sharding import PartitionSpec as P


HEADS = 12
masked_score = -1e30
largest = 3e38
epsilon = 1e-05
BF = jnp.bfloat16
F32 = jnp.float32
EXTRA = 8


def dot(a, b, ca=1, cb=0):
    return lax.dot_general(a, b, (((ca,), (cb,)), ((), ())), preferred_element_type=F32)


def iota(shape, axis):
    return lax.broadcasted_iota(jnp.int32, shape, axis)


def one_hot(mask):
    return jnp.where(mask, 1.0, 0.0).astype(BF)


def silu(v):
    half = 0.5 * v
    return half + half * jnp.tanh(half)


def split_matrix():
    row, col = iota((256, 256), 0), iota((256, 256), 1)
    return one_hot(row == jnp.where(col < 128, 2 * col, 2 * col - 255))


def split_time(rows, splitter):
    even, odd = [], []
    for start in range(0, rows.shape[1], 256):
        both = dot(rows[:, start : start + 256], splitter)
        even.append(both[:, :128])
        odd.append(both[:, 128:])
    if len(even) == 1:
        return even[0], odd[0]
    return jnp.concatenate(even, axis=1), jnp.concatenate(odd, axis=1)


def later(odd):
    moved = pltpu.roll(odd, 1, 1)
    return jnp.where(iota(odd.shape, 1) == 0, 0.0, moved)


def store_taps(taps, base, even, odd):
    height = even.shape[0]
    taps[base : base + height, :] = later(odd).astype(BF)
    taps[base + height : base + 2 * height, :] = even.astype(BF)
    taps[base + 2 * height : base + 3 * height, :] = odd.astype(BF)


def block_of(paired, flip=0):
    if not paired:
        return 0
    return (lax.axis_index("mp") * 2 + lax.axis_index("section")) ^ flip


def wire_rows(x_ref, block, first, last, wires, part):
    shape = ((last - first) * part, 256)
    row, col = iota(shape, 0), iota(shape, 1)
    mixer = one_hot(col == (row % part) * wires + row // part + first)
    return dot(mixer, x_ref[block * 256 : (block + 1) * 256, :]).astype(BF)


def fill_taps(taps, rows, block, splitter, part, channels):
    even, odd = split_time(rows, splitter)
    lagged = later(odd)
    for wire in range(rows.shape[0] // part):
        here = slice(wire * part, (wire + 1) * part)
        base = wire * 3 * channels + block * part
        taps[base : base + part, :] = lagged[here].astype(BF)
        taps[base + channels : base + channels + part, :] = even[here].astype(BF)
        taps[base + 2 * channels : base + 2 * channels + part, :] = odd[here].astype(BF)


def front_kernel(x_hbm, k1_hbm, k2_hbm, *refs, wires, channels, middle, paired):
    if paired:
        project_hbm = refs[0]
        refs = refs[1:]
    msg_ref, x_ref, k1_ref, k2_ref = refs[:4]
    taps, sems = refs[-2:]
    part = 256 // wires
    blocks = channels // part
    loads = []
    for block in range(blocks):
        here = pl.ds(block * 256, 256)
        loads.append(pltpu.make_async_copy(x_hbm.at[here, :], x_ref.at[here, :], sems.at[block]))
    loads.append(pltpu.make_async_copy(k1_hbm, k1_ref, sems.at[blocks]))
    others = [pltpu.make_async_copy(k2_hbm, k2_ref, sems.at[blocks + 1])]
    if paired:
        near_ref, query_ref = refs[4:6]
        depth, width = query_ref.shape
        half = depth // 2
        rows = pl.ds(pl.multiple_of(lax.axis_index("groups") * half, half), half)
        others.append(
            pltpu.make_async_copy(
                project_hbm.at[rows, pl.ds(width, 2 * width)], near_ref, sems.at[blocks + 2]
            )
        )
        others.append(
            pltpu.make_async_copy(project_hbm.at[:, pl.ds(0, width)], query_ref, sems.at[blocks + 3])
        )
    for copy in loads + others:
        copy.start()
    splitter = split_matrix()
    for block in range(blocks):
        loads[block].wait()
        rows = wire_rows(x_ref, block, wires - 3, wires, wires, part)
        fill_taps(taps, rows, block, splitter, part, channels)
    msg_ref[: 2 * channels, :] = taps[7 * channels :, :]
    loads[blocks].wait()
    msg_ref[2 * channels :, :] = silu(dot(k1_ref[...], taps[...], 0, 0)).astype(BF)
    for copy in others:
        copy.wait()


def central_kernel(
    msg_ref, x_ref, k1_ref, k2_ref, first_ref, second_ref, patch, taps1, taps2, *, wires, channels, middle
):
    splitter = split_matrix()
    part = 256 // wires
    for block in range(channels // part):
        rows = wire_rows(x_ref, block, 0, wires - 2, wires, part)
        fill_taps(taps1, rows, block, splitter, part, channels)
    first_ref[...] = dot(k1_ref[3 * channels :, :], taps1[: 6 * channels, :], 0, 0)
    for level in range(1, wires // 2):
        if level == wires // 2 - 1:
            out = msg_ref[2 * channels :, :]
        else:
            start = (2 * level - 1) * 3 * channels
            out = silu(dot(k1_ref[...], taps1[start : start + 9 * channels, :], 0, 0)).astype(BF)
        even, odd = split_time(out, splitter)
        store_taps(taps2, (level - 1) * 3 * middle, even, odd)
    second_ref[...] = dot(k2_ref[6 * middle :, :], taps2[: 3 * middle, :], 0, 0)
    out = silu(dot(k2_ref[...], taps2[...], 0, 0)).astype(BF)
    store_patch(patch, out, splitter)


def embed_mixer():
    row, col = iota((256, 256), 0), iota((256, 256), 1)
    return one_hot(col == (row % 64) * 4 + row // 64)


def mix_kernel(patch, *refs, pieces):
    embed_refs = refs[:pieces]
    token_ref, low_ref, high = refs[pieces:]
    mixer = embed_mixer()
    for piece in reversed(range(pieces)):
        ref = embed_refs[piece]
        parts = ref.shape[0] // 256
        for part in range(parts):
            rows = dot(mixer, ref[part * 256 : (part + 1) * 256, :]).astype(BF)
            base = pl.multiple_of((block_of(pieces > 1, piece) * parts + part) * 128, 128)
            low_ref[pl.ds(base, 128), :] = rows[:128]
            high[pl.ds(base, 128), :] = rows[128:]
    if pieces > 1:
        base = pl.multiple_of(block_of(True, pieces) * 128, 128)
        low_ref[pl.ds(base, 128), :] = jnp.zeros((128, low_ref.shape[1]), BF)
        high[pl.ds(base, 128), :] = jnp.zeros((128, high.shape[1]), BF)
    token_ref[...] = dot(patch[...], high[...], 0, 0)


def blend_kernel(patch, token_ref, embed_ref, out_ref, low_ref):
    rows = dot(embed_mixer(), embed_ref[...]).astype(BF)
    low_ref[...] = rows[:128]
    base = pl.multiple_of(block_of(True, 3) * 128, 128)
    out_ref[...] = token_ref[...] + dot(patch[pl.ds(base, 128), :], rows[128:], 0, 0)


def store_patch(patch, out, splitter):
    even, odd = split_time(out, splitter)
    even, odd = even.astype(BF), odd.astype(BF)
    for block in range(out.shape[0] // 64):
        here = slice(block * 64, (block + 1) * 64)
        patch[block * 128 : block * 128 + 64, :] = even[here]
        patch[block * 128 + 64 : (block + 1) * 128, :] = odd[here]


def back_kernel(
    got_ref, k1_ref, k2_ref, active_ref, first_ref, second_ref, token_ref, low_ref, *refs, channels, middle
):
    out_ref, all1, all2, patch = refs[-4:]
    splitter = split_matrix()
    odd = got_ref[channels : 2 * channels, :].astype(F32)
    all1[:channels, :] = later(odd).astype(BF)
    all1[channels:, :] = got_ref[: 2 * channels, :]
    even, odd = split_time(got_ref[2 * channels :, :], splitter)
    store_taps(all2, 0, even, odd)
    first = silu(first_ref[...] + dot(k1_ref[: 3 * channels, :], all1[...], 0, 0)).astype(BF)
    even, odd = split_time(first, splitter)
    store_taps(all2, 3 * middle, even, odd)
    out = silu(second_ref[...] + dot(k2_ref[: 6 * middle, :], all2[...], 0, 0)).astype(BF)
    store_patch(patch, out, splitter)
    total = token_ref[...] + dot(patch[...], low_ref[...], 0, 0)
    if len(refs) > 4:
        base = pl.multiple_of(block_of(True, 3) * 128, 128)
        total += dot(patch[pl.ds(base, 128), :], refs[0][...], 0, 0)
    count, width = total.shape
    total = total.astype(BF)
    for start in range(0, width, count):
        out_ref[start : start + count, :] = total[:, start : start + count]
    out_ref[width:, :] = jnp.broadcast_to(active_ref[...].astype(F32), (EXTRA, count)).astype(BF)


def tokens_of(ref):
    count = ref.shape[1]
    return jnp.concatenate(
        [ref[start : start + count, :] for start in range(0, ref.shape[0] - EXTRA, count)], axis=1
    )


def flags_of(ref):
    return ref[ref.shape[0] - EXTRA :, :]


def normal(tokens):
    value = tokens.astype(F32)
    value = value - jnp.mean(value, axis=-1, keepdims=True)
    spread = jnp.mean(value * value, axis=-1, keepdims=True)
    return (value * lax.rsqrt(spread + epsilon)).astype(BF)


def lift(joined, normed, keys, values):
    width = joined.shape[0]
    rows = normed[...]
    keys[...] = dot(rows, joined[:, :width]).astype(BF)
    lifted = dot(rows, joined[:, width:]).astype(BF)
    for start in range(0, width, 128):
        values[:, 2 * start : 2 * start + 128] = lifted[:, start : start + 128]
        values[:, 2 * start + 128 : 2 * start + 256] = jnp.ones((rows.shape[0], 128), BF)


def collect(sources, target, sems):
    copies = []
    for index, (ref, base, column, align) in enumerate(sources):
        if not isinstance(base, int):
            base = pl.multiple_of(base, align)
        copies.append(
            pltpu.make_async_copy(
                ref.at[:, pl.ds(column, target.shape[1])],
                target.at[pl.ds(base, ref.shape[0]), :],
                sems.at[index],
            )
        )
        copies[-1].start()
    return copies


def place_of(slot, swap):
    position = lax.axis_index("seq")
    return position ^ slot if swap else slot


def prepare_kernel(order_ref, *refs, pieces, chunks, swap):
    kv_refs = refs[:pieces]
    chunk_refs = refs[pieces : pieces + chunks]
    joined, normed, keys, values, perm_ref, sems = refs[pieces + chunks :]
    width = joined.shape[0]
    if pieces > 1:
        own, beside, near, far, near_corner, far_corner = kv_refs
        depth, half = own.shape[0], near.shape[0]
        group = lax.axis_index("groups")
        sources = [
            (own, block_of(True, 0) * depth, width, depth),
            (beside, block_of(True, 1) * depth, width, depth),
        ]
        for flip, first, second in ((2, near, far), (3, near_corner, far_corner)):
            base = block_of(True, flip) * depth
            sources.append((first, base + group * half, 0, half))
            sources.append((second, base + (group ^ 1) * half, 0, half))
    else:
        sources = [(kv_refs[0], 0, width, 1)]
    copies = collect(sources, joined, sems)
    shards, count = order_ref.shape
    square = iota((count, count), 0) == iota((count, count), 1)
    lane = iota((1, count), 1)
    labels = jnp.concatenate([lane + place_of(slot, swap) * count for slot in range(shards)], axis=1)
    labels = labels.astype(F32)
    for slot in range(shards):
        row = order_ref[pl.ds(place_of(slot, swap), 1), :].astype(F32)
        across = jnp.broadcast_to(row, (count, count))
        down = jnp.sum(jnp.where(square, across, 0.0), axis=1, keepdims=True)
        perm_ref[slot * count : (slot + 1) * count, :] = one_hot(labels == down)
    for slot, ref in enumerate(chunk_refs):
        normed[slot * count : (slot + 1) * count, :] = normal(tokens_of(ref))
    for copy in copies:
        copy.wait()
    lift(joined, normed, keys, values)


def extend_kernel(perm_ref, joined, normed0, *refs, pieces, chunks, early, swap):
    chunk_refs = refs[:chunks]
    query_refs = refs[chunks : chunks + pieces]
    query, keys1, values1, token_ref, picked_ref, on_ref, normed1, sems = refs[chunks + pieces :]
    count = token_ref.shape[0]
    copies = collect(weight_rows(query_refs), query, sems)
    for slot, ref in enumerate(chunk_refs[early:]):
        normed1[slot * count : (slot + 1) * count, :] = normal(tokens_of(ref))
    lift(joined, normed1, keys1, values1)
    own = own_rows(perm_ref, count, swap)
    near, far = early * count, chunks * count
    picked_ref[...] = dot(own[:, :near], normed0[...]) + dot(own[:, near:far], normed1[...])
    on, token = flags_and_tokens(perm_ref, own, chunk_refs, 0)
    on_ref[...] = on
    token_ref[...] = token
    for copy in copies:
        copy.wait()


def gather_kernel(*refs):
    output, sems = refs[-2:]
    for copy in collect(weight_rows(refs[:-2]), output, sems):
        copy.wait()


def weight_rows(refs):
    sources = []
    for piece, ref in enumerate(refs):
        depth = ref.shape[0]
        sources.append((ref, block_of(len(refs) > 1, piece) * depth, 0, depth))
    return sources


def own_rows(perm_ref, count, swap):
    slot = 0 if swap else lax.axis_index("seq")
    return perm_ref[pl.ds(pl.multiple_of(slot * count, count), count), :]


def flags_and_tokens(perm_ref, own, chunk_refs, first):
    count = own.shape[0]
    on = token = 0.0
    for slot, ref in enumerate(chunk_refs):
        here = slice((first + slot) * count, (first + slot + 1) * count)
        on += dot(flags_of(ref), perm_ref[here, :])
        token += dot(own[:, here], tokens_of(ref))
    return on, token


def finish_kernel(
    perm_ref, joined, keys0, values0, keys1, values1, query, output, token_ref, picked_ref, on_ref,
    *refs, chunks, swap
):
    chunk_refs = refs[:chunks]
    out_ref, normed2, keys2, values2, cap, mixed = refs[chunks:]
    count, width = token_ref.shape
    first = perm_ref.shape[0] // count - chunks
    for slot, ref in enumerate(chunk_refs):
        normed2[slot * count : (slot + 1) * count, :] = normal(tokens_of(ref))
    lift(joined, normed2, keys2, values2)
    own = own_rows(perm_ref, count, swap)
    picked = (picked_ref[...] + dot(own[:, first * count :], normed2[...])).astype(BF)
    head = width // HEADS
    queries = (dot(picked, query[...]) * head ** (-0.5)).astype(BF)
    on, token = flags_and_tokens(perm_ref, own, chunk_refs, first)
    on += on_ref[...]
    token += token_ref[...]
    allowed = (own.astype(F32) + jnp.broadcast_to(on[:1], own.shape)) > 0.5
    cap[...] = jnp.where(allowed, largest, masked_score)
    low = iota((count, 2 * head), 1) < head
    groups = ((keys0, values0), (keys1, values1), (keys2, values2))
    for pair in range(HEADS // 2):
        here = slice(pair * 2 * head, (pair + 1) * 2 * head)
        part_query = queries[:, here]
        zero = jnp.zeros_like(part_query)
        both = [jnp.where(low, part_query, zero), jnp.where(low, zero, part_query)]
        both = jnp.concatenate(both, axis=0)
        scores = jnp.concatenate([dot(both, keys[:, here], 1, 1) for keys, _ in groups], axis=1)
        weights = []
        for half in range(2):
            score = jnp.minimum(scores[half * count : (half + 1) * count], cap[...])
            weights.append(jnp.exp(score - jnp.max(score, axis=-1, keepdims=True)).astype(BF))
        weights = jnp.concatenate(weights, axis=0)
        part, start = 0.0, 0
        there = slice(2 * pair * 2 * head, 2 * (pair + 1) * 2 * head)
        for keys, values in groups:
            part += dot(weights[:, start : start + keys.shape[0]], values[:, there])
            start += keys.shape[0]
        part = part[:, : 2 * head] / part[:, 2 * head :]
        mixed[:, here] = jnp.where(low, part[:count], part[count:]).astype(BF)
    out_ref[...] = (token + dot(mixed[...], output[...])).astype(BF)


def vmem():
    return pl.BlockSpec(memory_space=pltpu.VMEM)


def hbm():
    return pl.BlockSpec(memory_space=pl.ANY)


def fixed():
    return pl.BlockSpec(memory_space=pltpu.HBM)


def params(mib):
    return pltpu.CompilerParams(vmem_limit_bytes=mib * 1024 * 1024)


def array(shape, dtype=BF):
    return jax.ShapeDtypeStruct(shape, dtype)


def front(rows, k1, k2, wires, weights):
    channels = rows.shape[0] // wires
    middle = k1.shape[1]
    length = rows.shape[1] // 2
    outs = [array((2 * channels + middle, length)), array(rows.shape), array(k1.shape), array(k2.shape)]
    if weights:
        depth, width = weights[0].shape
        outs += [array((depth // 2, width // 3 * 2)), array((depth, width // 3))]
    operands = [pltpu.with_memory_space_constraint(v, pltpu.HBM) for v in (rows, k1, k2, *weights)]
    return pl.pallas_call(
        functools.partial(
            front_kernel, wires=wires, channels=channels, middle=middle, paired=len(weights) > 0
        ),
        out_shape=outs,
        in_specs=[fixed()] * len(operands),
        out_specs=[vmem()] * len(outs),
        scratch_shapes=[
            pltpu.VMEM((9 * channels, length), BF),
            pltpu.SemaphoreType.DMA((channels * wires // 256 + 4,)),
        ],
        compiler_params=params(8),
        name="front",
    )(*operands)


def central(msg, rows, k1, k2, wires, count):
    middle, outer = k1.shape[1], k2.shape[1]
    channels = k1.shape[0] // 9
    length = msg.shape[1]
    return pl.pallas_call(
        functools.partial(central_kernel, wires=wires, channels=channels, middle=middle),
        out_shape=(
            array((middle, length), F32),
            array((outer, length // 2), F32),
            array((2 * outer, count)),
        ),
        in_specs=[vmem()] * 4,
        out_specs=[vmem()] * 3,
        scratch_shapes=[
            pltpu.VMEM(((wires - 2) * 3 * channels, length), BF),
            pltpu.VMEM(((wires // 2 - 1) * 3 * middle, length // 2), BF),
        ],
        compiler_params=params(10),
        name="central",
    )(msg, rows, k1, k2)


def mix(patch, embeds):
    width = embeds[0].shape[1]
    return pl.pallas_call(
        functools.partial(mix_kernel, pieces=len(embeds)),
        out_shape=(array((patch.shape[1], width), F32), array((patch.shape[0], width))),
        in_specs=[vmem()] * (1 + len(embeds)),
        out_specs=[vmem()] * 2,
        scratch_shapes=[pltpu.VMEM((patch.shape[0], width), BF)],
        compiler_params=params(8),
        name="mix",
    )(patch, *embeds)


def blend(patch, token, embed):
    return pl.pallas_call(
        blend_kernel,
        out_shape=(array(token.shape, F32), array((embed.shape[0] // 2, embed.shape[1]))),
        in_specs=[vmem()] * 3,
        out_specs=[vmem()] * 2,
        compiler_params=params(6),
        name="blend",
    )(patch, token, embed)


def back(got, k1, k2, active, *parts):
    middle = k1.shape[1]
    channels = k1.shape[0] // 9
    length = got.shape[1]
    count = active.shape[1]
    width = parts[2].shape[1]
    return pl.pallas_call(
        functools.partial(back_kernel, channels=channels, middle=middle),
        out_shape=array((width + EXTRA, count)),
        in_specs=[vmem()] * (4 + len(parts)),
        out_specs=vmem(),
        scratch_shapes=[
            pltpu.VMEM((3 * channels, length), BF),
            pltpu.VMEM((6 * middle, length // 2), BF),
            pltpu.VMEM((2 * k2.shape[1], count), BF),
        ],
        compiler_params=params(8),
        name="back",
    )(got, k1, k2, active, *parts)


def prepare(order, weights, chunks, swap):
    shards, count = order.shape
    width = chunks[0].shape[0] - EXTRA
    size, near = shards * count, len(chunks) * count
    return pl.pallas_call(
        functools.partial(prepare_kernel, pieces=len(weights), chunks=len(chunks), swap=swap),
        out_shape=(array((width, 2 * width)),) + (array((near, width)),) * 2 + (array((near, 2 * width)), array((size, size))),
        in_specs=[vmem()] + [fixed()] + [hbm()] * (len(weights) - 1) + [vmem()] * len(chunks),
        out_specs=[vmem()] * 5,
        scratch_shapes=[pltpu.SemaphoreType.DMA((len(weights),))],
        compiler_params=params(8 + size // 128),
        name="prepare",
    )(order, *weights, *chunks)


def extend(ready, chunks, weights, early, swap):
    joined, normed, _, _, perm = ready
    width = joined.shape[0]
    size = perm.shape[0]
    count = chunks[0].shape[1]
    far = (len(chunks) - early) * count
    pieces = len(weights)
    return pl.pallas_call(
        functools.partial(extend_kernel, pieces=pieces, chunks=len(chunks), early=early, swap=swap),
        out_shape=(
            array((width, width)),
            array((far, width)),
            array((far, 2 * width)),
            array((count, width), F32),
            array((count, width), F32),
            array((EXTRA, size), F32),
        ),
        in_specs=[vmem()] * (3 + len(chunks)) + [fixed()] + [hbm()] * (pieces - 1),
        out_specs=[vmem()] * 6,
        scratch_shapes=[pltpu.VMEM((far, width), BF), pltpu.SemaphoreType.DMA((pieces,))],
        compiler_params=params(8 + size // 128),
        name="extend",
    )(perm, joined, normed, *chunks, *weights)


def gather(weights):
    width = weights[0].shape[1]
    return pl.pallas_call(
        gather_kernel,
        out_shape=array((width, width)),
        in_specs=[fixed()] + [hbm()] * (len(weights) - 1),
        out_specs=vmem(),
        scratch_shapes=[pltpu.SemaphoreType.DMA((len(weights),))],
        compiler_params=params(4),
        name="gather",
    )(*weights)


def finish(ready, extra, output, chunks, swap):
    joined, _, keys, values, perm = ready
    query, keys1, values1, token, picked, on = extra
    width = joined.shape[0]
    size = perm.shape[0]
    count = token.shape[0]
    far = len(chunks) * count
    return pl.pallas_call(
        functools.partial(finish_kernel, chunks=len(chunks), swap=swap),
        out_shape=array((count, width)),
        in_specs=[vmem()] * (11 + len(chunks)),
        out_specs=vmem(),
        scratch_shapes=[
            pltpu.VMEM((far, width), BF),
            pltpu.VMEM((far, width), BF),
            pltpu.VMEM((far, 2 * width), BF),
            pltpu.VMEM((count, size), F32),
            pltpu.VMEM((count, width), BF),
        ],
        compiler_params=params(8 + size // 64),
        name="finish",
    )(perm, joined, keys, values, keys1, values1, query, output, token, picked, on, *chunks)


def exchanged(value, axis, flip):
    count = lax.axis_size(axis)
    return lax.ppermute(value, axis, [(i, i ^ flip) for i in range(count)])


def layer(
    readout, first_kernel, second_kernel, embed_weight, project_weight, output_weight, order, active
):
    shards = lax.axis_size("seq")
    paired = lax.axis_size("mp") == 2 and lax.axis_size("section") == 2 and lax.axis_size("groups") == 2
    swap = shards == 4
    channels, wires, ticks = readout.shape[1:]
    k1 = first_kernel.reshape(-1, first_kernel.shape[-1])
    k2 = second_kernel.reshape(-1, second_kernel.shape[-1])
    order = order.reshape(shards, -1)
    count = order.shape[1]
    rows = readout.reshape(channels * wires, ticks)
    if paired:
        embed_across = exchanged(embed_weight, "mp", 1)
        embed_beside = exchanged(embed_weight, "section", 1)
        embed_corner = exchanged(embed_across, "section", 1)
        embeds = [embed_weight, embed_beside, embed_across]
        msg, rows, k1, k2, near, query = front(rows, k1, k2, wires, (project_weight,))
    else:
        embeds = [lax.all_gather(embed_weight, ("mp", "section"), axis=0, tiled=True)]
        msg, rows, k1, k2 = front(rows, k1, k2, wires, ())
    got = lax.ppermute(msg, "seq", [(i, i + 1) for i in range(shards - 1)])
    first, second, patch = central(msg, rows, k1, k2, wires, count)
    token, low = mix(patch, embeds)
    parts = [first, second, token, low]
    if paired:
        parts[2], corner_low = blend(patch, token, embed_corner)
        parts.append(corner_low)
    tokens = back(got, k1, k2, active, *parts)
    if swap:
        chunks = [tokens] + [exchanged(tokens, "seq", flip) for flip in (1, 2)]
        chunks.append(exchanged(chunks[2], "seq", 1))
    else:
        everyone = lax.all_gather(tokens, "seq", axis=0, tiled=True)
        each = everyone.shape[0] // shards
        chunks = [everyone[i * each : (i + 1) * each] for i in range(shards)]
    if paired:
        project_beside = exchanged(project_weight, "section", 1)
        output_beside = exchanged(output_weight, "section", 1)
        near = exchanged(near, "mp", 1)
        far = exchanged(near, "groups", 1)
        query = exchanged(query, "mp", 1)
        output_across = exchanged(output_weight, "mp", 1)
        kv_weights = [project_weight, project_beside, near, far]
        kv_weights.append(exchanged(near, "section", 1))
        kv_weights.append(exchanged(far, "section", 1))
        query_weights = [project_weight, project_beside, query]
        query_weights.append(exchanged(query, "section", 1))
        output_weights = [output_weight, output_beside, output_across]
        output_weights.append(exchanged(output_across, "section", 1))
    else:
        kv_weights = [lax.all_gather(project_weight, ("mp", "section"), axis=0, tiled=True)]
        query_weights = kv_weights
        output_weights = [lax.all_gather(output_weight, ("mp", "section"), axis=0, tiled=True)]
    early, later = shards // 2, shards // 2 + shards // 4
    ready = prepare(order, kv_weights, chunks[:early], swap)
    extra = extend(ready, chunks[:later], query_weights, early, swap)
    output = gather(output_weights)
    result = finish(ready, extra, output, chunks[later:], swap)
    return result[None]


def solution(mesh):
    in_specs = (
        P(("groups", "mp", "section"), None, "seq", None),
        P(),
        P(),
        P(("mp", "section"), None),
        P(("mp", "section"), None),
        P(("mp", "section"), None),
        P(("groups", "mp", "section"), None),
        P(("groups", "mp", "section"), "seq"),
    )
    out_specs = P(("groups", "mp", "section"), "seq", None)
    return jax.shard_map(layer, mesh=mesh, in_specs=in_specs, out_specs=out_specs, check_vma=False)
```

```python
import functools

import jax
import jax.numpy as jnp
from jax import lax
from jax.experimental import pallas as pl
from jax.experimental.pallas import tpu as pltpu
from jax.sharding import PartitionSpec as P


HEADS = 12
masked_score = -1e30
largest = 3e38
epsilon = 1e-05
BF = jnp.bfloat16
F32 = jnp.float32
EXTRA = 8


def dot(a, b, ca=1, cb=0):
    return lax.dot_general(a, b, (((ca,), (cb,)), ((), ())), preferred_element_type=F32)


def iota(shape, axis):
    return lax.broadcasted_iota(jnp.int32, shape, axis)


def one_hot(mask):
    return jnp.where(mask, 1.0, 0.0).astype(BF)


def silu(v):
    half = 0.5 * v
    return half + half * jnp.tanh(half)


def split_matrix():
    row, col = iota((256, 256), 0), iota((256, 256), 1)
    return one_hot(row == jnp.where(col < 128, 2 * col, 2 * col - 255))


def split_time(rows, splitter):
    even, odd = [], []
    for start in range(0, rows.shape[1], 256):
        both = dot(rows[:, start : start + 256], splitter)
        even.append(both[:, :128])
        odd.append(both[:, 128:])
    if len(even) == 1:
        return even[0], odd[0]
    return jnp.concatenate(even, axis=1), jnp.concatenate(odd, axis=1)


def later(odd):
    moved = pltpu.roll(odd, 1, 1)
    return jnp.where(iota(odd.shape, 1) == 0, 0.0, moved)


def store_taps(taps, base, even, odd):
    height = even.shape[0]
    taps[base : base + height, :] = later(odd).astype(BF)
    taps[base + height : base + 2 * height, :] = even.astype(BF)
    taps[base + 2 * height : base + 3 * height, :] = odd.astype(BF)


def block_of(paired, flip=0):
    if not paired:
        return 0
    return (lax.axis_index("mp") * 2 + lax.axis_index("section")) ^ flip


def wire_rows(x_ref, block, first, last, wires, part):
    shape = ((last - first) * part, 256)
    row, col = iota(shape, 0), iota(shape, 1)
    mixer = one_hot(col == (row % part) * wires + row // part + first)
    return dot(mixer, x_ref[block * 256 : (block + 1) * 256, :]).astype(BF)


def fill_taps(taps, rows, block, splitter, part, channels):
    even, odd = split_time(rows, splitter)
    lagged = later(odd)
    for wire in range(rows.shape[0] // part):
        here = slice(wire * part, (wire + 1) * part)
        base = wire * 3 * channels + block * part
        taps[base : base + part, :] = lagged[here].astype(BF)
        taps[base + channels : base + channels + part, :] = even[here].astype(BF)
        taps[base + 2 * channels : base + 2 * channels + part, :] = odd[here].astype(BF)


def front_kernel(x_hbm, k1_hbm, k2_hbm, *refs, wires, channels, middle, paired):
    if paired:
        project_hbm = refs[0]
        refs = refs[1:]
    msg_ref, x_ref, k1_ref, k2_ref = refs[:4]
    taps, sems = refs[-2:]
    part = 256 // wires
    blocks = channels // part
    loads = []
    for block in range(blocks):
        here = pl.ds(block * 256, 256)
        loads.append(pltpu.make_async_copy(x_hbm.at[here, :], x_ref.at[here, :], sems.at[block]))
    loads.append(pltpu.make_async_copy(k1_hbm, k1_ref, sems.at[blocks]))
    others = [pltpu.make_async_copy(k2_hbm, k2_ref, sems.at[blocks + 1])]
    if paired:
        near_ref, query_ref = refs[4:6]
        depth, width = query_ref.shape
        half = depth // 2
        rows = pl.ds(pl.multiple_of(lax.axis_index("groups") * half, half), half)
        others.append(
            pltpu.make_async_copy(
                project_hbm.at[rows, pl.ds(width, 2 * width)], near_ref, sems.at[blocks + 2]
            )
        )
        others.append(
            pltpu.make_async_copy(project_hbm.at[:, pl.ds(0, width)], query_ref, sems.at[blocks + 3])
        )
    for copy in loads + others:
        copy.start()
    splitter = split_matrix()
    for block in range(blocks):
        loads[block].wait()
        rows = wire_rows(x_ref, block, wires - 3, wires, wires, part)
        fill_taps(taps, rows, block, splitter, part, channels)
    msg_ref[: 2 * channels, :] = taps[7 * channels :, :]
    loads[blocks].wait()
    msg_ref[2 * channels :, :] = silu(dot(k1_ref[...], taps[...], 0, 0)).astype(BF)
    for copy in others:
        copy.wait()


def central_kernel(
    msg_ref, x_ref, k1_ref, k2_ref, first_ref, second_ref, patch, taps1, taps2, *, wires, channels, middle
):
    splitter = split_matrix()
    part = 256 // wires
    for block in range(channels // part):
        rows = wire_rows(x_ref, block, 0, wires - 2, wires, part)
        fill_taps(taps1, rows, block, splitter, part, channels)
    first_ref[...] = dot(k1_ref[3 * channels :, :], taps1[: 6 * channels, :], 0, 0)
    for level in range(1, wires // 2):
        if level == wires // 2 - 1:
            out = msg_ref[2 * channels :, :]
        else:
            start = (2 * level - 1) * 3 * channels
            out = silu(dot(k1_ref[...], taps1[start : start + 9 * channels, :], 0, 0)).astype(BF)
        even, odd = split_time(out, splitter)
        store_taps(taps2, (level - 1) * 3 * middle, even, odd)
    second_ref[...] = dot(k2_ref[6 * middle :, :], taps2[: 3 * middle, :], 0, 0)
    out = silu(dot(k2_ref[...], taps2[...], 0, 0)).astype(BF)
    store_patch(patch, out, splitter)


def embed_mixer():
    row, col = iota((256, 256), 0), iota((256, 256), 1)
    return one_hot(col == (row % 64) * 4 + row // 64)


def mix_kernel(patch, *refs, pieces):
    embed_refs = refs[:pieces]
    token_ref, low_ref, high = refs[pieces:]
    mixer = embed_mixer()
    for piece in reversed(range(pieces)):
        ref = embed_refs[piece]
        parts = ref.shape[0] // 256
        for part in range(parts):
            rows = dot(mixer, ref[part * 256 : (part + 1) * 256, :]).astype(BF)
            base = pl.multiple_of((block_of(pieces > 1, piece) * parts + part) * 128, 128)
            low_ref[pl.ds(base, 128), :] = rows[:128]
            high[pl.ds(base, 128), :] = rows[128:]
    if pieces > 1:
        base = pl.multiple_of(block_of(True, pieces) * 128, 128)
        low_ref[pl.ds(base, 128), :] = jnp.zeros((128, low_ref.shape[1]), BF)
        high[pl.ds(base, 128), :] = jnp.zeros((128, high.shape[1]), BF)
    token_ref[...] = dot(patch[...], high[...], 0, 0)


def blend_kernel(patch, token_ref, embed_ref, out_ref, low_ref):
    rows = dot(embed_mixer(), embed_ref[...]).astype(BF)
    low_ref[...] = rows[:128]
    base = pl.multiple_of(block_of(True, 3) * 128, 128)
    out_ref[...] = token_ref[...] + dot(patch[pl.ds(base, 128), :], rows[128:], 0, 0)


def store_patch(patch, out, splitter):
    even, odd = split_time(out, splitter)
    even, odd = even.astype(BF), odd.astype(BF)
    for block in range(out.shape[0] // 64):
        here = slice(block * 64, (block + 1) * 64)
        patch[block * 128 : block * 128 + 64, :] = even[here]
        patch[block * 128 + 64 : (block + 1) * 128, :] = odd[here]


def back_kernel(
    got_ref, k1_ref, k2_ref, active_ref, first_ref, second_ref, token_ref, low_ref, *refs, channels, middle
):
    out_ref, all1, all2, patch = refs[-4:]
    splitter = split_matrix()
    got = got_ref[...]
    got = jnp.where(lax.axis_index("seq") > 0, got, jnp.zeros_like(got))
    all1[:channels, :] = later(got[channels : 2 * channels].astype(F32)).astype(BF)
    all1[channels:, :] = got[: 2 * channels]
    even, odd = split_time(got[2 * channels :], splitter)
    store_taps(all2, 0, even, odd)
    first = silu(first_ref[...] + dot(k1_ref[: 3 * channels, :], all1[...], 0, 0)).astype(BF)
    even, odd = split_time(first, splitter)
    store_taps(all2, 3 * middle, even, odd)
    out = silu(second_ref[...] + dot(k2_ref[: 6 * middle, :], all2[...], 0, 0)).astype(BF)
    store_patch(patch, out, splitter)
    total = token_ref[...] + dot(patch[...], low_ref[...], 0, 0)
    if len(refs) > 4:
        base = pl.multiple_of(block_of(True, 3) * 128, 128)
        total += dot(patch[pl.ds(base, 128), :], refs[0][...], 0, 0)
    count, width = total.shape
    total = total.astype(BF)
    for start in range(0, width, count):
        out_ref[start : start + count, :] = total[:, start : start + count]
    out_ref[width:, :] = jnp.broadcast_to(active_ref[...].astype(F32), (EXTRA, count)).astype(BF)


def tokens_of(ref):
    count = ref.shape[1]
    return jnp.concatenate(
        [ref[start : start + count, :] for start in range(0, ref.shape[0] - EXTRA, count)], axis=1
    )


def flags_of(ref):
    return ref[ref.shape[0] - EXTRA :, :]


def normal(tokens):
    value = tokens.astype(F32)
    value = value - jnp.mean(value, axis=-1, keepdims=True)
    spread = jnp.mean(value * value, axis=-1, keepdims=True)
    return (value * lax.rsqrt(spread + epsilon)).astype(BF)


def lift(joined, normed, keys, values):
    width = joined.shape[0]
    rows = normed[...]
    keys[...] = dot(rows, joined[:, :width]).astype(BF)
    lifted = dot(rows, joined[:, width:]).astype(BF)
    for start in range(0, width, 128):
        values[:, 2 * start : 2 * start + 128] = lifted[:, start : start + 128]
        values[:, 2 * start + 128 : 2 * start + 256] = jnp.ones((rows.shape[0], 128), BF)


def collect(sources, target, sems):
    copies = []
    for index, (ref, base, column, align) in enumerate(sources):
        if not isinstance(base, int):
            base = pl.multiple_of(base, align)
        copies.append(
            pltpu.make_async_copy(
                ref.at[:, pl.ds(column, target.shape[1])],
                target.at[pl.ds(base, ref.shape[0]), :],
                sems.at[index],
            )
        )
        copies[-1].start()
    return copies


def place_of(slot, swap):
    position = lax.axis_index("seq")
    return position ^ slot if swap else slot


def prepare_kernel(order_ref, *refs, pieces, chunks, swap):
    kv_refs = refs[:pieces]
    chunk_refs = refs[pieces : pieces + chunks]
    joined, normed, keys, values, perm_ref, sems = refs[pieces + chunks :]
    width = joined.shape[0]
    if pieces > 1:
        own, beside, near, far, near_corner, far_corner = kv_refs
        depth, half = own.shape[0], near.shape[0]
        group = lax.axis_index("groups")
        sources = [
            (own, block_of(True, 0) * depth, width, depth),
            (beside, block_of(True, 1) * depth, width, depth),
        ]
        for flip, first, second in ((2, near, far), (3, near_corner, far_corner)):
            base = block_of(True, flip) * depth
            sources.append((first, base + group * half, 0, half))
            sources.append((second, base + (group ^ 1) * half, 0, half))
    else:
        sources = [(kv_refs[0], 0, width, 1)]
    copies = collect(sources, joined, sems)
    shards, count = order_ref.shape
    square = iota((count, count), 0) == iota((count, count), 1)
    lane = iota((1, count), 1)
    labels = jnp.concatenate([lane + place_of(slot, swap) * count for slot in range(shards)], axis=1)
    labels = labels.astype(F32)
    for slot in range(shards):
        row = order_ref[pl.ds(place_of(slot, swap), 1), :].astype(F32)
        across = jnp.broadcast_to(row, (count, count))
        down = jnp.sum(jnp.where(square, across, 0.0), axis=1, keepdims=True)
        perm_ref[slot * count : (slot + 1) * count, :] = one_hot(labels == down)
    for slot, ref in enumerate(chunk_refs):
        normed[slot * count : (slot + 1) * count, :] = normal(tokens_of(ref))
    for copy in copies:
        copy.wait()
    lift(joined, normed, keys, values)


def extend_kernel(perm_ref, joined, normed0, *refs, chunks, early, swap):
    chunk_refs = refs[:chunks]
    keys1, values1, token_ref, picked_ref, on_ref, normed1 = refs[chunks:]
    count = token_ref.shape[0]
    for slot, ref in enumerate(chunk_refs[early:]):
        normed1[slot * count : (slot + 1) * count, :] = normal(tokens_of(ref))
    lift(joined, normed1, keys1, values1)
    own = own_rows(perm_ref, count, swap)
    near, far = early * count, chunks * count
    picked_ref[...] = dot(own[:, :near], normed0[...]) + dot(own[:, near:far], normed1[...])
    on, token = flags_and_tokens(perm_ref, own, chunk_refs, 0)
    on_ref[...] = on
    token_ref[...] = token


def gather_kernel(*refs):
    query, output, sems = refs[-3:]
    pieces = len(refs) // 2 - 1
    copies = collect(weight_rows(refs[:pieces]), query, sems.at[0])
    copies += collect(weight_rows(refs[pieces : 2 * pieces]), output, sems.at[1])
    for copy in copies:
        copy.wait()


def weight_rows(refs):
    sources = []
    for piece, ref in enumerate(refs):
        depth = ref.shape[0]
        sources.append((ref, block_of(len(refs) > 1, piece) * depth, 0, depth))
    return sources


def own_rows(perm_ref, count, swap):
    slot = 0 if swap else lax.axis_index("seq")
    return perm_ref[pl.ds(pl.multiple_of(slot * count, count), count), :]


def flags_and_tokens(perm_ref, own, chunk_refs, first):
    count = own.shape[0]
    on = token = 0.0
    for slot, ref in enumerate(chunk_refs):
        here = slice((first + slot) * count, (first + slot + 1) * count)
        on += dot(flags_of(ref), perm_ref[here, :])
        token += dot(own[:, here], tokens_of(ref))
    return on, token


def finish_kernel(
    perm_ref, joined, keys0, values0, keys1, values1, query, output, token_ref, picked_ref, on_ref,
    *refs, chunks, swap
):
    chunk_refs = refs[:chunks]
    out_ref, normed2, keys2, values2, cap, mixed = refs[chunks:]
    count, width = token_ref.shape
    first = perm_ref.shape[0] // count - chunks
    for slot, ref in enumerate(chunk_refs):
        normed2[slot * count : (slot + 1) * count, :] = normal(tokens_of(ref))
    lift(joined, normed2, keys2, values2)
    own = own_rows(perm_ref, count, swap)
    picked = (picked_ref[...] + dot(own[:, first * count :], normed2[...])).astype(BF)
    head = width // HEADS
    queries = (dot(picked, query[...]) * head ** (-0.5)).astype(BF)
    on, token = flags_and_tokens(perm_ref, own, chunk_refs, first)
    on += on_ref[...]
    token += token_ref[...]
    allowed = (own.astype(F32) + jnp.broadcast_to(on[:1], own.shape)) > 0.5
    cap[...] = jnp.where(allowed, largest, masked_score)
    low = iota((count, 2 * head), 1) < head
    groups = ((keys0, values0), (keys1, values1), (keys2, values2))
    for pair in range(HEADS // 2):
        here = slice(pair * 2 * head, (pair + 1) * 2 * head)
        part_query = queries[:, here]
        zero = jnp.zeros_like(part_query)
        both = [jnp.where(low, part_query, zero), jnp.where(low, zero, part_query)]
        both = jnp.concatenate(both, axis=0)
        scores = jnp.concatenate([dot(both, keys[:, here], 1, 1) for keys, _ in groups], axis=1)
        weights = []
        for half in range(2):
            score = jnp.minimum(scores[half * count : (half + 1) * count], cap[...])
            weights.append(jnp.exp(score - jnp.max(score, axis=-1, keepdims=True)).astype(BF))
        weights = jnp.concatenate(weights, axis=0)
        part, start = 0.0, 0
        there = slice(2 * pair * 2 * head, 2 * (pair + 1) * 2 * head)
        for keys, values in groups:
            part += dot(weights[:, start : start + keys.shape[0]], values[:, there])
            start += keys.shape[0]
        part = part[:, : 2 * head] / part[:, 2 * head :]
        mixed[:, here] = jnp.where(low, part[:count], part[count:]).astype(BF)
    out_ref[...] = (token + dot(mixed[...], output[...])).astype(BF)


def vmem():
    return pl.BlockSpec(memory_space=pltpu.VMEM)


def hbm():
    return pl.BlockSpec(memory_space=pl.ANY)


def fixed():
    return pl.BlockSpec(memory_space=pltpu.HBM)


def params(mib):
    return pltpu.CompilerParams(vmem_limit_bytes=mib * 1024 * 1024)


def array(shape, dtype=BF):
    return jax.ShapeDtypeStruct(shape, dtype)


def front(rows, k1, k2, wires, weights):
    channels = rows.shape[0] // wires
    middle = k1.shape[1]
    length = rows.shape[1] // 2
    outs = [array((2 * channels + middle, length)), array(rows.shape), array(k1.shape), array(k2.shape)]
    if weights:
        depth, width = weights[0].shape
        outs += [array((depth // 2, width // 3 * 2)), array((depth, width // 3))]
    operands = [pltpu.with_memory_space_constraint(v, pltpu.HBM) for v in (rows, k1, k2, *weights)]
    return pl.pallas_call(
        functools.partial(
            front_kernel, wires=wires, channels=channels, middle=middle, paired=len(weights) > 0
        ),
        out_shape=outs,
        in_specs=[fixed()] * len(operands),
        out_specs=[vmem()] * len(outs),
        scratch_shapes=[
            pltpu.VMEM((9 * channels, length), BF),
            pltpu.SemaphoreType.DMA((channels * wires // 256 + 4,)),
        ],
        compiler_params=params(8),
        name="front",
    )(*operands)


def central(msg, rows, k1, k2, wires, count):
    middle, outer = k1.shape[1], k2.shape[1]
    channels = k1.shape[0] // 9
    length = msg.shape[1]
    return pl.pallas_call(
        functools.partial(central_kernel, wires=wires, channels=channels, middle=middle),
        out_shape=(
            array((middle, length), F32),
            array((outer, length // 2), F32),
            array((2 * outer, count)),
        ),
        in_specs=[vmem()] * 4,
        out_specs=[vmem()] * 3,
        scratch_shapes=[
            pltpu.VMEM(((wires - 2) * 3 * channels, length), BF),
            pltpu.VMEM(((wires // 2 - 1) * 3 * middle, length // 2), BF),
        ],
        compiler_params=params(10),
        name="central",
    )(msg, rows, k1, k2)


def mix(patch, embeds):
    width = embeds[0].shape[1]
    return pl.pallas_call(
        functools.partial(mix_kernel, pieces=len(embeds)),
        out_shape=(array((patch.shape[1], width), F32), array((patch.shape[0], width))),
        in_specs=[vmem()] * (1 + len(embeds)),
        out_specs=[vmem()] * 2,
        scratch_shapes=[pltpu.VMEM((patch.shape[0], width), BF)],
        compiler_params=params(8),
        name="mix",
    )(patch, *embeds)


def blend(patch, token, embed):
    return pl.pallas_call(
        blend_kernel,
        out_shape=(array(token.shape, F32), array((embed.shape[0] // 2, embed.shape[1]))),
        in_specs=[vmem()] * 3,
        out_specs=[vmem()] * 2,
        compiler_params=params(6),
        name="blend",
    )(patch, token, embed)


def back(got, k1, k2, active, *parts):
    middle = k1.shape[1]
    channels = k1.shape[0] // 9
    length = got.shape[1]
    count = active.shape[1]
    width = parts[2].shape[1]
    return pl.pallas_call(
        functools.partial(back_kernel, channels=channels, middle=middle),
        out_shape=array((width + EXTRA, count)),
        in_specs=[vmem()] * (4 + len(parts)),
        out_specs=vmem(),
        scratch_shapes=[
            pltpu.VMEM((3 * channels, length), BF),
            pltpu.VMEM((6 * middle, length // 2), BF),
            pltpu.VMEM((2 * k2.shape[1], count), BF),
        ],
        compiler_params=params(8),
        name="back",
    )(got, k1, k2, active, *parts)


def prepare(order, weights, chunks, swap):
    shards, count = order.shape
    width = chunks[0].shape[0] - EXTRA
    size, near = shards * count, len(chunks) * count
    return pl.pallas_call(
        functools.partial(prepare_kernel, pieces=len(weights), chunks=len(chunks), swap=swap),
        out_shape=(array((width, 2 * width)),) + (array((near, width)),) * 2 + (array((near, 2 * width)), array((size, size))),
        in_specs=[vmem()] + [fixed()] + [hbm()] * (len(weights) - 1) + [vmem()] * len(chunks),
        out_specs=[vmem()] * 5,
        scratch_shapes=[pltpu.SemaphoreType.DMA((len(weights),))],
        compiler_params=params(8 + size // 128),
        name="prepare",
    )(order, *weights, *chunks)


def extend(ready, chunks, early, swap):
    joined, normed, _, _, perm = ready
    width = joined.shape[0]
    size = perm.shape[0]
    count = chunks[0].shape[1]
    far = (len(chunks) - early) * count
    return pl.pallas_call(
        functools.partial(extend_kernel, chunks=len(chunks), early=early, swap=swap),
        out_shape=(
            array((far, width)),
            array((far, 2 * width)),
            array((count, width), F32),
            array((count, width), F32),
            array((EXTRA, size), F32),
        ),
        in_specs=[vmem()] * (3 + len(chunks)),
        out_specs=[vmem()] * 5,
        scratch_shapes=[pltpu.VMEM((far, width), BF)],
        compiler_params=params(8 + size // 128),
        name="extend",
    )(perm, joined, normed, *chunks)


def gather(query_weights, output_weights):
    width = output_weights[0].shape[1]
    pieces = len(output_weights)
    return pl.pallas_call(
        gather_kernel,
        out_shape=(array((width, width)), array((width, width))),
        in_specs=([fixed()] + [hbm()] * (pieces - 1)) * 2,
        out_specs=[vmem()] * 2,
        scratch_shapes=[pltpu.SemaphoreType.DMA((2, pieces))],
        compiler_params=params(4),
        name="gather",
    )(*query_weights, *output_weights)


def finish(ready, extra, weights, chunks, swap):
    joined, _, keys, values, perm = ready
    keys1, values1, token, picked, on = extra
    width = joined.shape[0]
    size = perm.shape[0]
    count = token.shape[0]
    far = len(chunks) * count
    return pl.pallas_call(
        functools.partial(finish_kernel, chunks=len(chunks), swap=swap),
        out_shape=array((count, width)),
        in_specs=[vmem()] * (11 + len(chunks)),
        out_specs=vmem(),
        scratch_shapes=[
            pltpu.VMEM((far, width), BF),
            pltpu.VMEM((far, width), BF),
            pltpu.VMEM((far, 2 * width), BF),
            pltpu.VMEM((count, size), F32),
            pltpu.VMEM((count, width), BF),
        ],
        compiler_params=params(8 + size // 64),
        name="finish",
    )(perm, joined, keys, values, keys1, values1, *weights, token, picked, on, *chunks)


def exchanged(value, axis, flip):
    count = lax.axis_size(axis)
    return lax.ppermute(value, axis, [(i, i ^ flip) for i in range(count)])


def layer(
    readout, first_kernel, second_kernel, embed_weight, project_weight, output_weight, order, active
):
    shards = lax.axis_size("seq")
    paired = lax.axis_size("mp") == 2 and lax.axis_size("section") == 2 and lax.axis_size("groups") == 2
    swap = shards == 4
    channels, wires, ticks = readout.shape[1:]
    k1 = first_kernel.reshape(-1, first_kernel.shape[-1])
    k2 = second_kernel.reshape(-1, second_kernel.shape[-1])
    order = order.reshape(shards, -1)
    count = order.shape[1]
    rows = readout.reshape(channels * wires, ticks)
    if paired:
        embed_across = exchanged(embed_weight, "mp", 1)
        embed_beside = exchanged(embed_weight, "section", 1)
        embed_corner = exchanged(embed_across, "section", 1)
        embeds = [embed_weight, embed_beside, embed_across]
        msg, rows, k1, k2, near, query = front(rows, k1, k2, wires, (project_weight,))
    else:
        embeds = [lax.all_gather(embed_weight, ("mp", "section"), axis=0, tiled=True)]
        msg, rows, k1, k2 = front(rows, k1, k2, wires, ())
    got = lax.ppermute(msg, "seq", [(i, (i + 1) % shards) for i in range(shards)])
    first, second, patch = central(msg, rows, k1, k2, wires, count)
    token, low = mix(patch, embeds)
    parts = [first, second, token, low]
    if paired:
        parts[2], corner_low = blend(patch, token, embed_corner)
        parts.append(corner_low)
    tokens = back(got, k1, k2, active, *parts)
    if swap:
        chunks = [tokens] + [exchanged(tokens, "seq", flip) for flip in (1, 2)]
        chunks.append(exchanged(chunks[2], "seq", 1))
    else:
        everyone = lax.all_gather(tokens, "seq", axis=0, tiled=True)
        each = everyone.shape[0] // shards
        chunks = [everyone[i * each : (i + 1) * each] for i in range(shards)]
    if paired:
        project_beside = exchanged(project_weight, "section", 1)
        output_beside = exchanged(output_weight, "section", 1)
        near = exchanged(near, "mp", 1)
        far = exchanged(near, "groups", 1)
        query = exchanged(query, "mp", 1)
        output_across = exchanged(output_weight, "mp", 1)
        kv_weights = [project_weight, project_beside, near, far]
        kv_weights.append(exchanged(near, "section", 1))
        kv_weights.append(exchanged(far, "section", 1))
        query_weights = [project_weight, project_beside, query]
        query_weights.append(exchanged(query, "section", 1))
        output_weights = [output_weight, output_beside, output_across]
        output_weights.append(exchanged(output_across, "section", 1))
    else:
        kv_weights = [lax.all_gather(project_weight, ("mp", "section"), axis=0, tiled=True)]
        query_weights = kv_weights
        output_weights = [lax.all_gather(output_weight, ("mp", "section"), axis=0, tiled=True)]
    early, later = shards // 2, shards // 2 + shards // 4
    ready = prepare(order, kv_weights, chunks[:early], swap)
    extra = extend(ready, chunks[:later], early, swap)
    weights = gather(query_weights, output_weights)
    result = finish(ready, extra, weights, chunks[later:], swap)
    return result[None]


def solution(mesh):
    in_specs = (
        P(("groups", "mp", "section"), None, "seq", None),
        P(),
        P(),
        P(("mp", "section"), None),
        P(("mp", "section"), None),
        P(("mp", "section"), None),
        P(("groups", "mp", "section"), None),
        P(("groups", "mp", "section"), "seq"),
    )
    out_specs = P(("groups", "mp", "section"), "seq", None)
    return jax.shard_map(layer, mesh=mesh, in_specs=in_specs, out_specs=out_specs, check_vma=False)
```

```python
import functools

import jax
import jax.numpy as jnp
from jax import lax
from jax.experimental import pallas as pl
from jax.experimental.pallas import tpu as pltpu
from jax.sharding import PartitionSpec as P


HEADS = 12
masked_score = -1e30
largest = 3e38
epsilon = 1e-05
BF = jnp.bfloat16
F32 = jnp.float32
EXTRA = 8


def dot(a, b, ca=1, cb=0):
    return lax.dot_general(a, b, (((ca,), (cb,)), ((), ())), preferred_element_type=F32)


def iota(shape, axis):
    return lax.broadcasted_iota(jnp.int32, shape, axis)


def one_hot(mask):
    return jnp.where(mask, 1.0, 0.0).astype(BF)


def silu(v):
    half = 0.5 * v
    return half + half * jnp.tanh(half)


def split_matrix():
    row, col = iota((256, 256), 0), iota((256, 256), 1)
    return one_hot(row == jnp.where(col < 128, 2 * col, 2 * col - 255))


def split_time(rows, splitter):
    even, odd = [], []
    for start in range(0, rows.shape[1], 256):
        both = dot(rows[:, start : start + 256], splitter)
        even.append(both[:, :128])
        odd.append(both[:, 128:])
    if len(even) == 1:
        return even[0], odd[0]
    return jnp.concatenate(even, axis=1), jnp.concatenate(odd, axis=1)


def later(odd):
    moved = pltpu.roll(odd, 1, 1)
    return jnp.where(iota(odd.shape, 1) == 0, 0.0, moved)


def store_taps(taps, base, even, odd):
    height = even.shape[0]
    taps[base : base + height, :] = later(odd).astype(BF)
    taps[base + height : base + 2 * height, :] = even.astype(BF)
    taps[base + 2 * height : base + 3 * height, :] = odd.astype(BF)


def block_of(paired, flip=0):
    if not paired:
        return 0
    return (lax.axis_index("mp") * 2 + lax.axis_index("section")) ^ flip


def wire_rows(x_ref, block, first, last, wires, part):
    shape = ((last - first) * part, 256)
    row, col = iota(shape, 0), iota(shape, 1)
    mixer = one_hot(col == (row % part) * wires + row // part + first)
    return dot(mixer, x_ref[block * 256 : (block + 1) * 256, :]).astype(BF)


def fill_taps(taps, rows, block, splitter, part, channels):
    even, odd = split_time(rows, splitter)
    lagged = later(odd)
    for wire in range(rows.shape[0] // part):
        here = slice(wire * part, (wire + 1) * part)
        base = wire * 3 * channels + block * part
        taps[base : base + part, :] = lagged[here].astype(BF)
        taps[base + channels : base + channels + part, :] = even[here].astype(BF)
        taps[base + 2 * channels : base + 2 * channels + part, :] = odd[here].astype(BF)


def front_kernel(x_hbm, k1_hbm, k2_hbm, *refs, wires, channels, middle, paired):
    if paired:
        project_hbm = refs[0]
        refs = refs[1:]
    msg_ref, x_ref, k1_ref, k2_ref = refs[:4]
    taps, sems = refs[-2:]
    part = 256 // wires
    blocks = channels // part
    loads = []
    for block in range(blocks):
        here = pl.ds(block * 256, 256)
        loads.append(pltpu.make_async_copy(x_hbm.at[here, :], x_ref.at[here, :], sems.at[block]))
    loads.append(pltpu.make_async_copy(k1_hbm, k1_ref, sems.at[blocks]))
    others = [pltpu.make_async_copy(k2_hbm, k2_ref, sems.at[blocks + 1])]
    if paired:
        near_ref, query_ref = refs[4:6]
        depth, width = query_ref.shape
        half = depth // 2
        rows = pl.ds(pl.multiple_of(lax.axis_index("groups") * half, half), half)
        others.append(
            pltpu.make_async_copy(
                project_hbm.at[rows, pl.ds(width, 2 * width)], near_ref, sems.at[blocks + 2]
            )
        )
        others.append(
            pltpu.make_async_copy(project_hbm.at[:, pl.ds(0, width)], query_ref, sems.at[blocks + 3])
        )
    for copy in loads + others:
        copy.start()
    splitter = split_matrix()
    for block in range(blocks):
        loads[block].wait()
        rows = wire_rows(x_ref, block, wires - 3, wires, wires, part)
        fill_taps(taps, rows, block, splitter, part, channels)
    msg_ref[: 2 * channels, :] = taps[7 * channels :, :]
    loads[blocks].wait()
    msg_ref[2 * channels :, :] = silu(dot(k1_ref[...], taps[...], 0, 0)).astype(BF)
    for copy in others:
        copy.wait()


def central_kernel(
    msg_ref, x_ref, k1_ref, k2_ref, first_ref, second_ref, patch, taps1, taps2, *, wires, channels, middle
):
    splitter = split_matrix()
    part = 256 // wires
    for block in range(channels // part):
        rows = wire_rows(x_ref, block, 0, wires - 2, wires, part)
        fill_taps(taps1, rows, block, splitter, part, channels)
    first_ref[...] = dot(k1_ref[3 * channels :, :], taps1[: 6 * channels, :], 0, 0)
    for level in range(1, wires // 2):
        if level == wires // 2 - 1:
            out = msg_ref[2 * channels :, :]
        else:
            start = (2 * level - 1) * 3 * channels
            out = silu(dot(k1_ref[...], taps1[start : start + 9 * channels, :], 0, 0)).astype(BF)
        even, odd = split_time(out, splitter)
        store_taps(taps2, (level - 1) * 3 * middle, even, odd)
    second_ref[...] = dot(k2_ref[6 * middle :, :], taps2[: 3 * middle, :], 0, 0)
    out = silu(dot(k2_ref[...], taps2[...], 0, 0)).astype(BF)
    store_patch(patch, out, splitter)


def embed_mixer():
    row, col = iota((256, 256), 0), iota((256, 256), 1)
    return one_hot(col == (row % 64) * 4 + row // 64)


def mix_kernel(patch, *refs, pieces):
    embed_refs = refs[:pieces]
    token_ref, low_ref, high = refs[pieces:]
    mixer = embed_mixer()
    for piece in reversed(range(pieces)):
        ref = embed_refs[piece]
        parts = ref.shape[0] // 256
        for part in range(parts):
            rows = dot(mixer, ref[part * 256 : (part + 1) * 256, :]).astype(BF)
            base = pl.multiple_of((block_of(pieces > 1, piece) * parts + part) * 128, 128)
            low_ref[pl.ds(base, 128), :] = rows[:128]
            high[pl.ds(base, 128), :] = rows[128:]
    if pieces > 1:
        base = pl.multiple_of(block_of(True, pieces) * 128, 128)
        low_ref[pl.ds(base, 128), :] = jnp.zeros((128, low_ref.shape[1]), BF)
        high[pl.ds(base, 128), :] = jnp.zeros((128, high.shape[1]), BF)
    token_ref[...] = dot(patch[...], high[...], 0, 0)


def blend_kernel(patch, token_ref, embed_ref, out_ref, low_ref):
    rows = dot(embed_mixer(), embed_ref[...]).astype(BF)
    low_ref[...] = rows[:128]
    base = pl.multiple_of(block_of(True, 3) * 128, 128)
    out_ref[...] = token_ref[...] + dot(patch[pl.ds(base, 128), :], rows[128:], 0, 0)


def store_patch(patch, out, splitter):
    even, odd = split_time(out, splitter)
    even, odd = even.astype(BF), odd.astype(BF)
    for block in range(out.shape[0] // 64):
        here = slice(block * 64, (block + 1) * 64)
        patch[block * 128 : block * 128 + 64, :] = even[here]
        patch[block * 128 + 64 : (block + 1) * 128, :] = odd[here]


def back_kernel(
    got_ref, k1_ref, k2_ref, active_ref, first_ref, second_ref, token_ref, low_ref, *refs, channels, middle
):
    out_ref, all1, all2, patch = refs[-4:]
    splitter = split_matrix()
    got = got_ref[...]
    got = jnp.where(lax.axis_index("seq") > 0, got, jnp.zeros_like(got))
    all1[:channels, :] = later(got[channels : 2 * channels].astype(F32)).astype(BF)
    all1[channels:, :] = got[: 2 * channels]
    even, odd = split_time(got[2 * channels :], splitter)
    store_taps(all2, 0, even, odd)
    first = silu(first_ref[...] + dot(k1_ref[: 3 * channels, :], all1[...], 0, 0)).astype(BF)
    even, odd = split_time(first, splitter)
    store_taps(all2, 3 * middle, even, odd)
    out = silu(second_ref[...] + dot(k2_ref[: 6 * middle, :], all2[...], 0, 0)).astype(BF)
    store_patch(patch, out, splitter)
    total = token_ref[...] + dot(patch[...], low_ref[...], 0, 0)
    if len(refs) > 4:
        base = pl.multiple_of(block_of(True, 3) * 128, 128)
        total += dot(patch[pl.ds(base, 128), :], refs[0][...], 0, 0)
    count, width = total.shape
    total = total.astype(BF)
    for start in range(0, width, count):
        out_ref[start : start + count, :] = total[:, start : start + count]
    out_ref[width:, :] = jnp.broadcast_to(active_ref[...].astype(F32), (EXTRA, count)).astype(BF)


def tokens_of(ref):
    count = ref.shape[1]
    return jnp.concatenate(
        [ref[start : start + count, :] for start in range(0, ref.shape[0] - EXTRA, count)], axis=1
    )


def flags_of(ref):
    return ref[ref.shape[0] - EXTRA :, :]


def normal(tokens):
    value = tokens.astype(F32)
    value = value - jnp.mean(value, axis=-1, keepdims=True)
    spread = jnp.mean(value * value, axis=-1, keepdims=True)
    return (value * lax.rsqrt(spread + epsilon)).astype(BF)


def lift(joined, normed, keys, values):
    width = joined.shape[0]
    rows = normed[...]
    keys[...] = dot(rows, joined[:, :width]).astype(BF)
    lifted = dot(rows, joined[:, width:]).astype(BF)
    for start in range(0, width, 128):
        values[:, 2 * start : 2 * start + 128] = lifted[:, start : start + 128]
        values[:, 2 * start + 128 : 2 * start + 256] = jnp.ones((rows.shape[0], 128), BF)


def collect(sources, target, sems):
    copies = []
    for index, (ref, base, column, align) in enumerate(sources):
        if not isinstance(base, int):
            base = pl.multiple_of(base, align)
        copies.append(
            pltpu.make_async_copy(
                ref.at[:, pl.ds(column, target.shape[1])],
                target.at[pl.ds(base, ref.shape[0]), :],
                sems.at[index],
            )
        )
        copies[-1].start()
    return copies


def place_of(slot, swap):
    position = lax.axis_index("seq")
    return position ^ slot if swap else slot


def place_kernel(order_ref, perm_ref, *, swap):
    shards, count = order_ref.shape
    square = iota((count, count), 0) == iota((count, count), 1)
    lane = iota((1, count), 1)
    labels = jnp.concatenate([lane + place_of(slot, swap) * count for slot in range(shards)], axis=1)
    labels = labels.astype(F32)
    for slot in range(shards):
        row = order_ref[pl.ds(place_of(slot, swap), 1), :].astype(F32)
        across = jnp.broadcast_to(row, (count, count))
        down = jnp.sum(jnp.where(square, across, 0.0), axis=1, keepdims=True)
        perm_ref[slot * count : (slot + 1) * count, :] = one_hot(labels == down)


def prepare_kernel(*refs, pieces, chunks):
    kv_refs = refs[:pieces]
    chunk_refs = refs[pieces : pieces + chunks]
    joined, normed, keys, values, sems = refs[pieces + chunks :]
    width = joined.shape[0]
    if pieces > 1:
        own, beside, near, far, near_corner, far_corner = kv_refs
        depth, half = own.shape[0], near.shape[0]
        group = lax.axis_index("groups")
        sources = [
            (own, block_of(True, 0) * depth, width, depth),
            (beside, block_of(True, 1) * depth, width, depth),
        ]
        for flip, first, second in ((2, near, far), (3, near_corner, far_corner)):
            base = block_of(True, flip) * depth
            sources.append((first, base + group * half, 0, half))
            sources.append((second, base + (group ^ 1) * half, 0, half))
    else:
        sources = [(kv_refs[0], 0, width, 1)]
    copies = collect(sources, joined, sems)
    for slot, ref in enumerate(chunk_refs):
        count = ref.shape[1]
        normed[slot * count : (slot + 1) * count, :] = normal(tokens_of(ref))
    for copy in copies:
        copy.wait()
    lift(joined, normed, keys, values)


def extend_kernel(perm_ref, joined, normed0, *refs, pieces, chunks, early, swap):
    chunk_refs = refs[:chunks]
    query_refs = refs[chunks : chunks + pieces]
    query, keys1, values1, token_ref, picked_ref, on_ref, normed1, sems = refs[chunks + pieces :]
    count = token_ref.shape[0]
    copies = collect(weight_rows(query_refs), query, sems)
    for slot, ref in enumerate(chunk_refs[early:]):
        normed1[slot * count : (slot + 1) * count, :] = normal(tokens_of(ref))
    lift(joined, normed1, keys1, values1)
    own = own_rows(perm_ref, count, swap)
    near, far = early * count, chunks * count
    picked_ref[...] = dot(own[:, :near], normed0[...]) + dot(own[:, near:far], normed1[...])
    on, token = flags_and_tokens(perm_ref, own, chunk_refs, 0)
    on_ref[...] = on
    token_ref[...] = token
    for copy in copies:
        copy.wait()


def gather_kernel(*refs):
    output, sems = refs[-2:]
    for copy in collect(weight_rows(refs[:-2]), output, sems):
        copy.wait()


def weight_rows(refs):
    sources = []
    for piece, ref in enumerate(refs):
        depth = ref.shape[0]
        sources.append((ref, block_of(len(refs) > 1, piece) * depth, 0, depth))
    return sources


def own_rows(perm_ref, count, swap):
    slot = 0 if swap else lax.axis_index("seq")
    return perm_ref[pl.ds(pl.multiple_of(slot * count, count), count), :]


def flags_and_tokens(perm_ref, own, chunk_refs, first):
    count = own.shape[0]
    on = token = 0.0
    for slot, ref in enumerate(chunk_refs):
        here = slice((first + slot) * count, (first + slot + 1) * count)
        on += dot(flags_of(ref), perm_ref[here, :])
        token += dot(own[:, here], tokens_of(ref))
    return on, token


def finish_kernel(
    perm_ref, joined, keys0, values0, keys1, values1, query, output, token_ref, picked_ref, on_ref,
    *refs, chunks, swap
):
    chunk_refs = refs[:chunks]
    out_ref, normed2, keys2, values2, cap, mixed = refs[chunks:]
    count, width = token_ref.shape
    first = perm_ref.shape[0] // count - chunks
    for slot, ref in enumerate(chunk_refs):
        normed2[slot * count : (slot + 1) * count, :] = normal(tokens_of(ref))
    lift(joined, normed2, keys2, values2)
    own = own_rows(perm_ref, count, swap)
    picked = (picked_ref[...] + dot(own[:, first * count :], normed2[...])).astype(BF)
    head = width // HEADS
    queries = (dot(picked, query[...]) * head ** (-0.5)).astype(BF)
    on, token = flags_and_tokens(perm_ref, own, chunk_refs, first)
    on += on_ref[...]
    token += token_ref[...]
    allowed = (own.astype(F32) + jnp.broadcast_to(on[:1], own.shape)) > 0.5
    cap[...] = jnp.where(allowed, largest, masked_score)
    low = iota((count, 2 * head), 1) < head
    groups = ((keys0, values0), (keys1, values1), (keys2, values2))
    for pair in range(HEADS // 2):
        here = slice(pair * 2 * head, (pair + 1) * 2 * head)
        part_query = queries[:, here]
        zero = jnp.zeros_like(part_query)
        both = [jnp.where(low, part_query, zero), jnp.where(low, zero, part_query)]
        both = jnp.concatenate(both, axis=0)
        scores = jnp.concatenate([dot(both, keys[:, here], 1, 1) for keys, _ in groups], axis=1)
        weights = []
        for half in range(2):
            score = jnp.minimum(scores[half * count : (half + 1) * count], cap[...])
            weights.append(jnp.exp(score - jnp.max(score, axis=-1, keepdims=True)).astype(BF))
        weights = jnp.concatenate(weights, axis=0)
        part, start = 0.0, 0
        there = slice(2 * pair * 2 * head, 2 * (pair + 1) * 2 * head)
        for keys, values in groups:
            part += dot(weights[:, start : start + keys.shape[0]], values[:, there])
            start += keys.shape[0]
        part = part[:, : 2 * head] / part[:, 2 * head :]
        mixed[:, here] = jnp.where(low, part[:count], part[count:]).astype(BF)
    out_ref[...] = (token + dot(mixed[...], output[...])).astype(BF)


def vmem():
    return pl.BlockSpec(memory_space=pltpu.VMEM)


def hbm():
    return pl.BlockSpec(memory_space=pl.ANY)


def fixed():
    return pl.BlockSpec(memory_space=pltpu.HBM)


def params(mib):
    return pltpu.CompilerParams(vmem_limit_bytes=mib * 1024 * 1024)


def array(shape, dtype=BF):
    return jax.ShapeDtypeStruct(shape, dtype)


def front(rows, k1, k2, wires, weights):
    channels = rows.shape[0] // wires
    middle = k1.shape[1]
    length = rows.shape[1] // 2
    outs = [array((2 * channels + middle, length)), array(rows.shape), array(k1.shape), array(k2.shape)]
    if weights:
        depth, width = weights[0].shape
        outs += [array((depth // 2, width // 3 * 2)), array((depth, width // 3))]
    operands = [pltpu.with_memory_space_constraint(v, pltpu.HBM) for v in (rows, k1, k2, *weights)]
    return pl.pallas_call(
        functools.partial(
            front_kernel, wires=wires, channels=channels, middle=middle, paired=len(weights) > 0
        ),
        out_shape=outs,
        in_specs=[fixed()] * len(operands),
        out_specs=[vmem()] * len(outs),
        scratch_shapes=[
            pltpu.VMEM((9 * channels, length), BF),
            pltpu.SemaphoreType.DMA((channels * wires // 256 + 4,)),
        ],
        compiler_params=params(8),
        name="front",
    )(*operands)


def central(msg, rows, k1, k2, wires, count):
    middle, outer = k1.shape[1], k2.shape[1]
    channels = k1.shape[0] // 9
    length = msg.shape[1]
    return pl.pallas_call(
        functools.partial(central_kernel, wires=wires, channels=channels, middle=middle),
        out_shape=(
            array((middle, length), F32),
            array((outer, length // 2), F32),
            array((2 * outer, count)),
        ),
        in_specs=[vmem()] * 4,
        out_specs=[vmem()] * 3,
        scratch_shapes=[
            pltpu.VMEM(((wires - 2) * 3 * channels, length), BF),
            pltpu.VMEM(((wires // 2 - 1) * 3 * middle, length // 2), BF),
        ],
        compiler_params=params(10),
        name="central",
    )(msg, rows, k1, k2)


def mix(patch, embeds):
    width = embeds[0].shape[1]
    return pl.pallas_call(
        functools.partial(mix_kernel, pieces=len(embeds)),
        out_shape=(array((patch.shape[1], width), F32), array((patch.shape[0], width))),
        in_specs=[vmem()] * (1 + len(embeds)),
        out_specs=[vmem()] * 2,
        scratch_shapes=[pltpu.VMEM((patch.shape[0], width), BF)],
        compiler_params=params(8),
        name="mix",
    )(patch, *embeds)


def blend(patch, token, embed):
    return pl.pallas_call(
        blend_kernel,
        out_shape=(array(token.shape, F32), array((embed.shape[0] // 2, embed.shape[1]))),
        in_specs=[vmem()] * 3,
        out_specs=[vmem()] * 2,
        compiler_params=params(6),
        name="blend",
    )(patch, token, embed)


def back(got, k1, k2, active, *parts):
    middle = k1.shape[1]
    channels = k1.shape[0] // 9
    length = got.shape[1]
    count = active.shape[1]
    width = parts[2].shape[1]
    return pl.pallas_call(
        functools.partial(back_kernel, channels=channels, middle=middle),
        out_shape=array((width + EXTRA, count)),
        in_specs=[vmem()] * (4 + len(parts)),
        out_specs=vmem(),
        scratch_shapes=[
            pltpu.VMEM((3 * channels, length), BF),
            pltpu.VMEM((6 * middle, length // 2), BF),
            pltpu.VMEM((2 * k2.shape[1], count), BF),
        ],
        compiler_params=params(8),
        name="back",
    )(got, k1, k2, active, *parts)


def place(order, swap):
    size = order.shape[0] * order.shape[1]
    return pl.pallas_call(
        functools.partial(place_kernel, swap=swap),
        out_shape=array((size, size)),
        in_specs=[vmem()],
        out_specs=vmem(),
        compiler_params=params(4 + size // 256),
        name="place",
    )(order)


def prepare(weights, chunks):
    width = chunks[0].shape[0] - EXTRA
    near = len(chunks) * chunks[0].shape[1]
    return pl.pallas_call(
        functools.partial(prepare_kernel, pieces=len(weights), chunks=len(chunks)),
        out_shape=(array((width, 2 * width)),) + (array((near, width)),) * 2 + (array((near, 2 * width)),),
        in_specs=[fixed()] + [hbm()] * (len(weights) - 1) + [vmem()] * len(chunks),
        out_specs=[vmem()] * 4,
        scratch_shapes=[pltpu.SemaphoreType.DMA((len(weights),))],
        compiler_params=params(8 + near // 64),
        name="prepare",
    )(*weights, *chunks)


def extend(ready, chunks, weights, early, swap):
    joined, normed, _, _, perm = ready
    width = joined.shape[0]
    size = perm.shape[0]
    count = chunks[0].shape[1]
    far = (len(chunks) - early) * count
    pieces = len(weights)
    return pl.pallas_call(
        functools.partial(extend_kernel, pieces=pieces, chunks=len(chunks), early=early, swap=swap),
        out_shape=(
            array((width, width)),
            array((far, width)),
            array((far, 2 * width)),
            array((count, width), F32),
            array((count, width), F32),
            array((EXTRA, size), F32),
        ),
        in_specs=[vmem()] * (3 + len(chunks)) + [fixed()] + [hbm()] * (pieces - 1),
        out_specs=[vmem()] * 6,
        scratch_shapes=[pltpu.VMEM((far, width), BF), pltpu.SemaphoreType.DMA((pieces,))],
        compiler_params=params(8 + size // 128),
        name="extend",
    )(perm, joined, normed, *chunks, *weights)


def gather(weights):
    width = weights[0].shape[1]
    return pl.pallas_call(
        gather_kernel,
        out_shape=array((width, width)),
        in_specs=[fixed()] + [hbm()] * (len(weights) - 1),
        out_specs=vmem(),
        scratch_shapes=[pltpu.SemaphoreType.DMA((len(weights),))],
        compiler_params=params(4),
        name="gather",
    )(*weights)


def finish(ready, extra, output, chunks, swap):
    joined, _, keys, values, perm = ready
    query, keys1, values1, token, picked, on = extra
    width = joined.shape[0]
    size = perm.shape[0]
    count = token.shape[0]
    far = len(chunks) * count
    return pl.pallas_call(
        functools.partial(finish_kernel, chunks=len(chunks), swap=swap),
        out_shape=array((count, width)),
        in_specs=[vmem()] * (11 + len(chunks)),
        out_specs=vmem(),
        scratch_shapes=[
            pltpu.VMEM((far, width), BF),
            pltpu.VMEM((far, width), BF),
            pltpu.VMEM((far, 2 * width), BF),
            pltpu.VMEM((count, size), F32),
            pltpu.VMEM((count, width), BF),
        ],
        compiler_params=params(8 + size // 64),
        name="finish",
    )(perm, joined, keys, values, keys1, values1, query, output, token, picked, on, *chunks)


def exchanged(value, axis, flip):
    count = lax.axis_size(axis)
    return lax.ppermute(value, axis, [(i, i ^ flip) for i in range(count)])


def layer(
    readout, first_kernel, second_kernel, embed_weight, project_weight, output_weight, order, active
):
    shards = lax.axis_size("seq")
    paired = lax.axis_size("mp") == 2 and lax.axis_size("section") == 2 and lax.axis_size("groups") == 2
    swap = shards == 4
    channels, wires, ticks = readout.shape[1:]
    k1 = first_kernel.reshape(-1, first_kernel.shape[-1])
    k2 = second_kernel.reshape(-1, second_kernel.shape[-1])
    order = order.reshape(shards, -1)
    count = order.shape[1]
    rows = readout.reshape(channels * wires, ticks)
    if paired:
        embed_across = exchanged(embed_weight, "mp", 1)
        embed_beside = exchanged(embed_weight, "section", 1)
        embed_corner = exchanged(embed_across, "section", 1)
        embeds = [embed_weight, embed_beside, embed_across]
        msg, rows, k1, k2, near, query = front(rows, k1, k2, wires, (project_weight,))
    else:
        embeds = [lax.all_gather(embed_weight, ("mp", "section"), axis=0, tiled=True)]
        msg, rows, k1, k2 = front(rows, k1, k2, wires, ())
    got = lax.ppermute(msg, "seq", [(i, (i + 1) % shards) for i in range(shards)])
    first, second, patch = central(msg, rows, k1, k2, wires, count)
    token, low = mix(patch, embeds)
    parts = [first, second, token, low]
    if paired:
        parts[2], corner_low = blend(patch, token, embed_corner)
        parts.append(corner_low)
    tokens = back(got, k1, k2, active, *parts)
    if swap:
        chunks = [tokens] + [exchanged(tokens, "seq", flip) for flip in (1, 2)]
        chunks.append(exchanged(chunks[2], "seq", 1))
    else:
        everyone = lax.all_gather(tokens, "seq", axis=0, tiled=True)
        each = everyone.shape[0] // shards
        chunks = [everyone[i * each : (i + 1) * each] for i in range(shards)]
    if paired:
        project_beside = exchanged(project_weight, "section", 1)
        output_beside = exchanged(output_weight, "section", 1)
        near = exchanged(near, "mp", 1)
        far = exchanged(near, "groups", 1)
        query = exchanged(query, "mp", 1)
        output_across = exchanged(output_weight, "mp", 1)
        kv_weights = [project_weight, project_beside, near, far]
        kv_weights.append(exchanged(near, "section", 1))
        kv_weights.append(exchanged(far, "section", 1))
        query_weights = [project_weight, project_beside, query]
        query_weights.append(exchanged(query, "section", 1))
        output_weights = [output_weight, output_beside, output_across]
        output_weights.append(exchanged(output_across, "section", 1))
    else:
        kv_weights = [lax.all_gather(project_weight, ("mp", "section"), axis=0, tiled=True)]
        query_weights = kv_weights
        output_weights = [lax.all_gather(output_weight, ("mp", "section"), axis=0, tiled=True)]
    early, later = shards // 2, shards // 2 + shards // 4
    perm = place(order, swap)
    ready = (*prepare(kv_weights, chunks[:early]), perm)
    extra = extend(ready, chunks[:later], query_weights, early, swap)
    output = gather(output_weights)
    result = finish(ready, extra, output, chunks[later:], swap)
    return result[None]


def solution(mesh):
    in_specs = (
        P(("groups", "mp", "section"), None, "seq", None),
        P(),
        P(),
        P(("mp", "section"), None),
        P(("mp", "section"), None),
        P(("mp", "section"), None),
        P(("groups", "mp", "section"), None),
        P(("groups", "mp", "section"), "seq"),
    )
    out_specs = P(("groups", "mp", "section"), "seq", None)
    return jax.shard_map(layer, mesh=mesh, in_specs=in_specs, out_specs=out_specs, check_vma=False)
```

```python
import functools

import jax
import jax.numpy as jnp
from jax import lax
from jax.experimental import pallas as pl
from jax.experimental.pallas import tpu as pltpu
from jax.sharding import PartitionSpec as P


HEADS = 12
masked_score = -1e30
largest = 3e38
epsilon = 1e-05
BF = jnp.bfloat16
F32 = jnp.float32
EXTRA = 8


def dot(a, b, ca=1, cb=0):
    return lax.dot_general(a, b, (((ca,), (cb,)), ((), ())), preferred_element_type=F32)


def iota(shape, axis):
    return lax.broadcasted_iota(jnp.int32, shape, axis)


def one_hot(mask):
    return jnp.where(mask, 1.0, 0.0).astype(BF)


def silu(v):
    half = 0.5 * v
    return half + half * jnp.tanh(half)


def split_matrix():
    row, col = iota((256, 256), 0), iota((256, 256), 1)
    return one_hot(row == jnp.where(col < 128, 2 * col, 2 * col - 255))


def split_time(rows, splitter):
    even, odd = [], []
    for start in range(0, rows.shape[1], 256):
        both = dot(rows[:, start : start + 256], splitter)
        even.append(both[:, :128])
        odd.append(both[:, 128:])
    if len(even) == 1:
        return even[0], odd[0]
    return jnp.concatenate(even, axis=1), jnp.concatenate(odd, axis=1)


def later(odd):
    moved = pltpu.roll(odd, 1, 1)
    return jnp.where(iota(odd.shape, 1) == 0, 0.0, moved)


def store_taps(taps, base, even, odd):
    height = even.shape[0]
    taps[base : base + height, :] = later(odd).astype(BF)
    taps[base + height : base + 2 * height, :] = even.astype(BF)
    taps[base + 2 * height : base + 3 * height, :] = odd.astype(BF)


def block_of(paired, flip=0):
    if not paired:
        return 0
    return (lax.axis_index("mp") * 2 + lax.axis_index("section")) ^ flip


def wire_rows(x_ref, block, first, last, wires, part):
    shape = ((last - first) * part, 256)
    row, col = iota(shape, 0), iota(shape, 1)
    mixer = one_hot(col == (row % part) * wires + row // part + first)
    return dot(mixer, x_ref[block * 256 : (block + 1) * 256, :]).astype(BF)


def fill_taps(taps, rows, block, splitter, part, channels):
    even, odd = split_time(rows, splitter)
    lagged = later(odd)
    for wire in range(rows.shape[0] // part):
        here = slice(wire * part, (wire + 1) * part)
        base = wire * 3 * channels + block * part
        taps[base : base + part, :] = lagged[here].astype(BF)
        taps[base + channels : base + channels + part, :] = even[here].astype(BF)
        taps[base + 2 * channels : base + 2 * channels + part, :] = odd[here].astype(BF)


def front_kernel(x_hbm, k1_hbm, k2_hbm, *refs, wires, channels, middle, paired):
    if paired:
        project_hbm = refs[0]
        refs = refs[1:]
    msg_ref, x_ref, k1_ref, k2_ref = refs[:4]
    taps, sems = refs[-2:]
    part = 256 // wires
    blocks = channels // part
    loads = []
    for block in range(blocks):
        here = pl.ds(block * 256, 256)
        loads.append(pltpu.make_async_copy(x_hbm.at[here, :], x_ref.at[here, :], sems.at[block]))
    loads.append(pltpu.make_async_copy(k1_hbm, k1_ref, sems.at[blocks]))
    others = [pltpu.make_async_copy(k2_hbm, k2_ref, sems.at[blocks + 1])]
    if paired:
        near_ref, query_ref = refs[4:6]
        depth, width = query_ref.shape
        half = depth // 2
        rows = pl.ds(pl.multiple_of(lax.axis_index("groups") * half, half), half)
        others.append(
            pltpu.make_async_copy(
                project_hbm.at[rows, pl.ds(width, 2 * width)], near_ref, sems.at[blocks + 2]
            )
        )
        others.append(
            pltpu.make_async_copy(project_hbm.at[:, pl.ds(0, width)], query_ref, sems.at[blocks + 3])
        )
    for copy in loads + others:
        copy.start()
    splitter = split_matrix()
    for block in range(blocks):
        loads[block].wait()
        rows = wire_rows(x_ref, block, wires - 3, wires, wires, part)
        fill_taps(taps, rows, block, splitter, part, channels)
    msg_ref[: 2 * channels, :] = taps[7 * channels :, :]
    loads[blocks].wait()
    msg_ref[2 * channels :, :] = silu(dot(k1_ref[...], taps[...], 0, 0)).astype(BF)
    for copy in others:
        copy.wait()


def central_kernel(
    msg_ref, x_ref, k1_ref, k2_ref, first_ref, second_ref, patch, taps1, taps2, *, wires, channels, middle
):
    splitter = split_matrix()
    part = 256 // wires
    for block in range(channels // part):
        rows = wire_rows(x_ref, block, 0, wires - 2, wires, part)
        fill_taps(taps1, rows, block, splitter, part, channels)
    first_ref[...] = dot(k1_ref[3 * channels :, :], taps1[: 6 * channels, :], 0, 0)
    for level in range(1, wires // 2):
        if level == wires // 2 - 1:
            out = msg_ref[2 * channels :, :]
        else:
            start = (2 * level - 1) * 3 * channels
            out = silu(dot(k1_ref[...], taps1[start : start + 9 * channels, :], 0, 0)).astype(BF)
        even, odd = split_time(out, splitter)
        store_taps(taps2, (level - 1) * 3 * middle, even, odd)
    second_ref[...] = dot(k2_ref[6 * middle :, :], taps2[: 3 * middle, :], 0, 0)
    out = silu(dot(k2_ref[...], taps2[...], 0, 0)).astype(BF)
    store_patch(patch, out, splitter)


def embed_mixer():
    row, col = iota((256, 256), 0), iota((256, 256), 1)
    return one_hot(col == (row % 64) * 4 + row // 64)


def mix_kernel(patch, *refs, pieces):
    embed_refs = refs[:pieces]
    token_ref, low_ref, high = refs[pieces:]
    mixer = embed_mixer()
    for piece in reversed(range(pieces)):
        ref = embed_refs[piece]
        parts = ref.shape[0] // 256
        for part in range(parts):
            rows = dot(mixer, ref[part * 256 : (part + 1) * 256, :]).astype(BF)
            base = pl.multiple_of((block_of(pieces > 1, piece) * parts + part) * 128, 128)
            low_ref[pl.ds(base, 128), :] = rows[:128]
            high[pl.ds(base, 128), :] = rows[128:]
    if pieces > 1:
        base = pl.multiple_of(block_of(True, pieces) * 128, 128)
        low_ref[pl.ds(base, 128), :] = jnp.zeros((128, low_ref.shape[1]), BF)
        high[pl.ds(base, 128), :] = jnp.zeros((128, high.shape[1]), BF)
    token_ref[...] = dot(patch[...], high[...], 0, 0)


def blend_kernel(patch, token_ref, embed_ref, out_ref, low_ref):
    rows = dot(embed_mixer(), embed_ref[...]).astype(BF)
    low_ref[...] = rows[:128]
    base = pl.multiple_of(block_of(True, 3) * 128, 128)
    out_ref[...] = token_ref[...] + dot(patch[pl.ds(base, 128), :], rows[128:], 0, 0)


def store_patch(patch, out, splitter):
    even, odd = split_time(out, splitter)
    even, odd = even.astype(BF), odd.astype(BF)
    for block in range(out.shape[0] // 64):
        here = slice(block * 64, (block + 1) * 64)
        patch[block * 128 : block * 128 + 64, :] = even[here]
        patch[block * 128 + 64 : (block + 1) * 128, :] = odd[here]


def back_kernel(
    got_ref, k1_ref, k2_ref, active_ref, first_ref, second_ref, token_ref, low_ref, *refs, channels, middle
):
    out_ref, all1, all2, patch = refs[-4:]
    splitter = split_matrix()
    got = got_ref[...]
    got = jnp.where(lax.axis_index("seq") > 0, got, jnp.zeros_like(got))
    all1[:channels, :] = later(got[channels : 2 * channels].astype(F32)).astype(BF)
    all1[channels:, :] = got[: 2 * channels]
    even, odd = split_time(got[2 * channels :], splitter)
    store_taps(all2, 0, even, odd)
    first = silu(first_ref[...] + dot(k1_ref[: 3 * channels, :], all1[...], 0, 0)).astype(BF)
    even, odd = split_time(first, splitter)
    store_taps(all2, 3 * middle, even, odd)
    out = silu(second_ref[...] + dot(k2_ref[: 6 * middle, :], all2[...], 0, 0)).astype(BF)
    store_patch(patch, out, splitter)
    total = token_ref[...] + dot(patch[...], low_ref[...], 0, 0)
    if len(refs) > 4:
        base = pl.multiple_of(block_of(True, 3) * 128, 128)
        total += dot(patch[pl.ds(base, 128), :], refs[0][...], 0, 0)
    count, width = total.shape
    total = total.astype(BF)
    for start in range(0, width, count):
        out_ref[start : start + count, :] = total[:, start : start + count]
    out_ref[width:, :] = jnp.broadcast_to(active_ref[...].astype(F32), (EXTRA, count)).astype(BF)


def tokens_of(ref):
    count = ref.shape[1]
    return jnp.concatenate(
        [ref[start : start + count, :] for start in range(0, ref.shape[0] - EXTRA, count)], axis=1
    )


def flags_of(ref):
    return ref[ref.shape[0] - EXTRA :, :]


def normal(tokens):
    value = tokens.astype(F32)
    value = value - jnp.mean(value, axis=-1, keepdims=True)
    spread = jnp.mean(value * value, axis=-1, keepdims=True)
    return (value * lax.rsqrt(spread + epsilon)).astype(BF)


def lift(joined, normed, keys, values):
    width = joined.shape[0]
    rows = normed[...]
    keys[...] = dot(rows, joined[:, :width]).astype(BF)
    lifted = dot(rows, joined[:, width:]).astype(BF)
    for start in range(0, width, 128):
        values[:, 2 * start : 2 * start + 128] = lifted[:, start : start + 128]
        values[:, 2 * start + 128 : 2 * start + 256] = jnp.ones((rows.shape[0], 128), BF)


def collect(sources, target, sems):
    copies = []
    for index, (ref, base, column, align) in enumerate(sources):
        if not isinstance(base, int):
            base = pl.multiple_of(base, align)
        copies.append(
            pltpu.make_async_copy(
                ref.at[:, pl.ds(column, target.shape[1])],
                target.at[pl.ds(base, ref.shape[0]), :],
                sems.at[index],
            )
        )
        copies[-1].start()
    return copies


def place_of(slot, swap):
    position = lax.axis_index("seq")
    return position ^ slot if swap else slot


def prepare_kernel(order_ref, *refs, pieces, chunks, swap):
    kv_refs = refs[:pieces]
    chunk_refs = refs[pieces : pieces + chunks]
    joined, normed, keys, values, perm_ref, sems = refs[pieces + chunks :]
    width = joined.shape[0]
    if pieces > 1:
        own, beside, near, far, near_corner, far_corner = kv_refs
        depth, half = own.shape[0], near.shape[0]
        group = lax.axis_index("groups")
        sources = [
            (own, block_of(True, 0) * depth, width, depth),
            (beside, block_of(True, 1) * depth, width, depth),
        ]
        for flip, first, second in ((2, near, far), (3, near_corner, far_corner)):
            base = block_of(True, flip) * depth
            sources.append((first, base + group * half, 0, half))
            sources.append((second, base + (group ^ 1) * half, 0, half))
    else:
        sources = [(kv_refs[0], 0, width, 1)]
    copies = collect(sources, joined, sems)
    shards, count = order_ref.shape
    square = iota((count, count), 0) == iota((count, count), 1)
    lane = iota((1, count), 1)
    labels = jnp.concatenate([lane + place_of(slot, swap) * count for slot in range(shards)], axis=1)
    labels = labels.astype(F32)
    for slot in range(shards):
        row = order_ref[pl.ds(place_of(slot, swap), 1), :].astype(F32)
        across = jnp.broadcast_to(row, (count, count))
        down = jnp.sum(jnp.where(square, across, 0.0), axis=1, keepdims=True)
        perm_ref[slot * count : (slot + 1) * count, :] = one_hot(labels == down)
    for slot, ref in enumerate(chunk_refs):
        normed[slot * count : (slot + 1) * count, :] = normal(tokens_of(ref))
    for copy in copies:
        copy.wait()
    lift(joined, normed, keys, values)


def extend_kernel(perm_ref, joined, normed0, *refs, pieces, chunks, early, swap):
    chunk_refs = refs[:chunks]
    query_refs = refs[chunks : chunks + pieces]
    query, keys1, values1, token_ref, picked_ref, on_ref, normed1, sems = refs[chunks + pieces :]
    count = token_ref.shape[0]
    copies = collect(weight_rows(query_refs), query, sems)
    for slot, ref in enumerate(chunk_refs[early:]):
        normed1[slot * count : (slot + 1) * count, :] = normal(tokens_of(ref))
    lift(joined, normed1, keys1, values1)
    own = own_rows(perm_ref, count, swap)
    near, far = early * count, chunks * count
    picked_ref[...] = dot(own[:, :near], normed0[...]) + dot(own[:, near:far], normed1[...])
    on, token = flags_and_tokens(perm_ref, own, chunk_refs, 0)
    on_ref[...] = on
    token_ref[...] = token
    for copy in copies:
        copy.wait()


def gather_kernel(*refs):
    output, sems = refs[-2:]
    for copy in collect(weight_rows(refs[:-2]), output, sems):
        copy.wait()


def weight_rows(refs):
    sources = []
    for piece, ref in enumerate(refs):
        depth = ref.shape[0]
        sources.append((ref, block_of(len(refs) > 1, piece) * depth, 0, depth))
    return sources


def own_rows(perm_ref, count, swap):
    slot = 0 if swap else lax.axis_index("seq")
    return perm_ref[pl.ds(pl.multiple_of(slot * count, count), count), :]


def flags_and_tokens(perm_ref, own, chunk_refs, first):
    count = own.shape[0]
    on = token = 0.0
    for slot, ref in enumerate(chunk_refs):
        here = slice((first + slot) * count, (first + slot + 1) * count)
        on += dot(flags_of(ref), perm_ref[here, :])
        token += dot(own[:, here], tokens_of(ref))
    return on, token


def finish_kernel(
    perm_ref, joined, keys0, values0, keys1, values1, query, output, token_ref, picked_ref, on_ref,
    *refs, chunks, swap
):
    chunk_refs = refs[:chunks]
    out_ref, normed2, keys2, values2, cap, mixed = refs[chunks:]
    count, width = token_ref.shape
    first = perm_ref.shape[0] // count - chunks
    for slot, ref in enumerate(chunk_refs):
        normed2[slot * count : (slot + 1) * count, :] = normal(tokens_of(ref))
    lift(joined, normed2, keys2, values2)
    own = own_rows(perm_ref, count, swap)
    picked = (picked_ref[...] + dot(own[:, first * count :], normed2[...])).astype(BF)
    head = width // HEADS
    queries = (dot(picked, query[...]) * head ** (-0.5)).astype(BF)
    on, token = flags_and_tokens(perm_ref, own, chunk_refs, first)
    on += on_ref[...]
    token += token_ref[...]
    allowed = (own.astype(F32) + jnp.broadcast_to(on[:1], own.shape)) > 0.5
    cap[...] = jnp.where(allowed, largest, masked_score)
    low = iota((count, 2 * head), 1) < head
    groups = ((keys0, values0), (keys1, values1), (keys2, values2))
    for pair in range(HEADS // 2):
        here = slice(pair * 2 * head, (pair + 1) * 2 * head)
        part_query = queries[:, here]
        zero = jnp.zeros_like(part_query)
        both = [jnp.where(low, part_query, zero), jnp.where(low, zero, part_query)]
        both = jnp.concatenate(both, axis=0)
        scores = jnp.concatenate([dot(both, keys[:, here], 1, 1) for keys, _ in groups], axis=1)
        weights = []
        for half in range(2):
            score = jnp.minimum(scores[half * count : (half + 1) * count], cap[...])
            weights.append(jnp.exp((score - jnp.max(score, axis=-1, keepdims=True)).astype(BF)))
        weights = jnp.concatenate(weights, axis=0)
        part, start = 0.0, 0
        there = slice(2 * pair * 2 * head, 2 * (pair + 1) * 2 * head)
        for keys, values in groups:
            part += dot(weights[:, start : start + keys.shape[0]], values[:, there])
            start += keys.shape[0]
        part = part[:, : 2 * head] / part[:, 2 * head :]
        mixed[:, here] = jnp.where(low, part[:count], part[count:]).astype(BF)
    out_ref[...] = (token + dot(mixed[...], output[...])).astype(BF)


def vmem():
    return pl.BlockSpec(memory_space=pltpu.VMEM)


def hbm():
    return pl.BlockSpec(memory_space=pl.ANY)


def fixed():
    return pl.BlockSpec(memory_space=pltpu.HBM)


def params(mib):
    return pltpu.CompilerParams(vmem_limit_bytes=mib * 1024 * 1024)


def array(shape, dtype=BF):
    return jax.ShapeDtypeStruct(shape, dtype)


def front(rows, k1, k2, wires, weights):
    channels = rows.shape[0] // wires
    middle = k1.shape[1]
    length = rows.shape[1] // 2
    outs = [array((2 * channels + middle, length)), array(rows.shape), array(k1.shape), array(k2.shape)]
    if weights:
        depth, width = weights[0].shape
        outs += [array((depth // 2, width // 3 * 2)), array((depth, width // 3))]
    operands = [pltpu.with_memory_space_constraint(v, pltpu.HBM) for v in (rows, k1, k2, *weights)]
    return pl.pallas_call(
        functools.partial(
            front_kernel, wires=wires, channels=channels, middle=middle, paired=len(weights) > 0
        ),
        out_shape=outs,
        in_specs=[fixed()] * len(operands),
        out_specs=[vmem()] * len(outs),
        scratch_shapes=[
            pltpu.VMEM((9 * channels, length), BF),
            pltpu.SemaphoreType.DMA((channels * wires // 256 + 4,)),
        ],
        compiler_params=params(8),
        name="front",
    )(*operands)


def central(msg, rows, k1, k2, wires, count):
    middle, outer = k1.shape[1], k2.shape[1]
    channels = k1.shape[0] // 9
    length = msg.shape[1]
    return pl.pallas_call(
        functools.partial(central_kernel, wires=wires, channels=channels, middle=middle),
        out_shape=(
            array((middle, length), F32),
            array((outer, length // 2), F32),
            array((2 * outer, count)),
        ),
        in_specs=[vmem()] * 4,
        out_specs=[vmem()] * 3,
        scratch_shapes=[
            pltpu.VMEM(((wires - 2) * 3 * channels, length), BF),
            pltpu.VMEM(((wires // 2 - 1) * 3 * middle, length // 2), BF),
        ],
        compiler_params=params(10),
        name="central",
    )(msg, rows, k1, k2)


def mix(patch, embeds):
    width = embeds[0].shape[1]
    return pl.pallas_call(
        functools.partial(mix_kernel, pieces=len(embeds)),
        out_shape=(array((patch.shape[1], width), F32), array((patch.shape[0], width))),
        in_specs=[vmem()] * (1 + len(embeds)),
        out_specs=[vmem()] * 2,
        scratch_shapes=[pltpu.VMEM((patch.shape[0], width), BF)],
        compiler_params=params(8),
        name="mix",
    )(patch, *embeds)


def blend(patch, token, embed):
    return pl.pallas_call(
        blend_kernel,
        out_shape=(array(token.shape, F32), array((embed.shape[0] // 2, embed.shape[1]))),
        in_specs=[vmem()] * 3,
        out_specs=[vmem()] * 2,
        compiler_params=params(6),
        name="blend",
    )(patch, token, embed)


def back(got, k1, k2, active, *parts):
    middle = k1.shape[1]
    channels = k1.shape[0] // 9
    length = got.shape[1]
    count = active.shape[1]
    width = parts[2].shape[1]
    return pl.pallas_call(
        functools.partial(back_kernel, channels=channels, middle=middle),
        out_shape=array((width + EXTRA, count)),
        in_specs=[vmem()] * (4 + len(parts)),
        out_specs=vmem(),
        scratch_shapes=[
            pltpu.VMEM((3 * channels, length), BF),
            pltpu.VMEM((6 * middle, length // 2), BF),
            pltpu.VMEM((2 * k2.shape[1], count), BF),
        ],
        compiler_params=params(8),
        name="back",
    )(got, k1, k2, active, *parts)


def prepare(order, weights, chunks, swap):
    shards, count = order.shape
    width = chunks[0].shape[0] - EXTRA
    size, near = shards * count, len(chunks) * count
    return pl.pallas_call(
        functools.partial(prepare_kernel, pieces=len(weights), chunks=len(chunks), swap=swap),
        out_shape=(array((width, 2 * width)),) + (array((near, width)),) * 2 + (array((near, 2 * width)), array((size, size))),
        in_specs=[vmem()] + [fixed()] + [hbm()] * (len(weights) - 1) + [vmem()] * len(chunks),
        out_specs=[vmem()] * 5,
        scratch_shapes=[pltpu.SemaphoreType.DMA((len(weights),))],
        compiler_params=params(8 + size // 128),
        name="prepare",
    )(order, *weights, *chunks)


def extend(ready, chunks, weights, early, swap):
    joined, normed, _, _, perm = ready
    width = joined.shape[0]
    size = perm.shape[0]
    count = chunks[0].shape[1]
    far = (len(chunks) - early) * count
    pieces = len(weights)
    return pl.pallas_call(
        functools.partial(extend_kernel, pieces=pieces, chunks=len(chunks), early=early, swap=swap),
        out_shape=(
            array((width, width)),
            array((far, width)),
            array((far, 2 * width)),
            array((count, width), F32),
            array((count, width), F32),
            array((EXTRA, size), F32),
        ),
        in_specs=[vmem()] * (3 + len(chunks)) + [fixed()] + [hbm()] * (pieces - 1),
        out_specs=[vmem()] * 6,
        scratch_shapes=[pltpu.VMEM((far, width), BF), pltpu.SemaphoreType.DMA((pieces,))],
        compiler_params=params(8 + size // 128),
        name="extend",
    )(perm, joined, normed, *chunks, *weights)


def gather(weights):
    width = weights[0].shape[1]
    return pl.pallas_call(
        gather_kernel,
        out_shape=array((width, width)),
        in_specs=[fixed()] + [hbm()] * (len(weights) - 1),
        out_specs=vmem(),
        scratch_shapes=[pltpu.SemaphoreType.DMA((len(weights),))],
        compiler_params=params(4),
        name="gather",
    )(*weights)


def finish(ready, extra, output, chunks, swap):
    joined, _, keys, values, perm = ready
    query, keys1, values1, token, picked, on = extra
    width = joined.shape[0]
    size = perm.shape[0]
    count = token.shape[0]
    far = len(chunks) * count
    return pl.pallas_call(
        functools.partial(finish_kernel, chunks=len(chunks), swap=swap),
        out_shape=array((count, width)),
        in_specs=[vmem()] * (11 + len(chunks)),
        out_specs=vmem(),
        scratch_shapes=[
            pltpu.VMEM((far, width), BF),
            pltpu.VMEM((far, width), BF),
            pltpu.VMEM((far, 2 * width), BF),
            pltpu.VMEM((count, size), F32),
            pltpu.VMEM((count, width), BF),
        ],
        compiler_params=params(8 + size // 64),
        name="finish",
    )(perm, joined, keys, values, keys1, values1, query, output, token, picked, on, *chunks)


def exchanged(value, axis, flip):
    count = lax.axis_size(axis)
    return lax.ppermute(value, axis, [(i, i ^ flip) for i in range(count)])


def layer(
    readout, first_kernel, second_kernel, embed_weight, project_weight, output_weight, order, active
):
    shards = lax.axis_size("seq")
    paired = lax.axis_size("mp") == 2 and lax.axis_size("section") == 2 and lax.axis_size("groups") == 2
    swap = shards == 4
    channels, wires, ticks = readout.shape[1:]
    k1 = first_kernel.reshape(-1, first_kernel.shape[-1])
    k2 = second_kernel.reshape(-1, second_kernel.shape[-1])
    order = order.reshape(shards, -1)
    count = order.shape[1]
    rows = readout.reshape(channels * wires, ticks)
    if paired:
        embed_across = exchanged(embed_weight, "mp", 1)
        embed_beside = exchanged(embed_weight, "section", 1)
        embed_corner = exchanged(embed_across, "section", 1)
        embeds = [embed_weight, embed_beside, embed_across]
        msg, rows, k1, k2, near, query = front(rows, k1, k2, wires, (project_weight,))
    else:
        embeds = [lax.all_gather(embed_weight, ("mp", "section"), axis=0, tiled=True)]
        msg, rows, k1, k2 = front(rows, k1, k2, wires, ())
    got = lax.ppermute(msg, "seq", [(i, (i + 1) % shards) for i in range(shards)])
    first, second, patch = central(msg, rows, k1, k2, wires, count)
    token, low = mix(patch, embeds)
    parts = [first, second, token, low]
    if paired:
        parts[2], corner_low = blend(patch, token, embed_corner)
        parts.append(corner_low)
    tokens = back(got, k1, k2, active, *parts)
    if swap:
        chunks = [tokens] + [exchanged(tokens, "seq", flip) for flip in (1, 2)]
        chunks.append(exchanged(chunks[2], "seq", 1))
    else:
        everyone = lax.all_gather(tokens, "seq", axis=0, tiled=True)
        each = everyone.shape[0] // shards
        chunks = [everyone[i * each : (i + 1) * each] for i in range(shards)]
    if paired:
        project_beside = exchanged(project_weight, "section", 1)
        output_beside = exchanged(output_weight, "section", 1)
        near = exchanged(near, "mp", 1)
        far = exchanged(near, "groups", 1)
        query = exchanged(query, "mp", 1)
        output_across = exchanged(output_weight, "mp", 1)
        kv_weights = [project_weight, project_beside, near, far]
        kv_weights.append(exchanged(near, "section", 1))
        kv_weights.append(exchanged(far, "section", 1))
        query_weights = [project_weight, project_beside, query]
        query_weights.append(exchanged(query, "section", 1))
        output_weights = [output_weight, output_beside, output_across]
        output_weights.append(exchanged(output_across, "section", 1))
    else:
        kv_weights = [lax.all_gather(project_weight, ("mp", "section"), axis=0, tiled=True)]
        query_weights = kv_weights
        output_weights = [lax.all_gather(output_weight, ("mp", "section"), axis=0, tiled=True)]
    early, later = shards // 2, shards // 2 + shards // 4
    ready = prepare(order, kv_weights, chunks[:early], swap)
    extra = extend(ready, chunks[:later], query_weights, early, swap)
    output = gather(output_weights)
    result = finish(ready, extra, output, chunks[later:], swap)
    return result[None]


def solution(mesh):
    in_specs = (
        P(("groups", "mp", "section"), None, "seq", None),
        P(),
        P(),
        P(("mp", "section"), None),
        P(("mp", "section"), None),
        P(("mp", "section"), None),
        P(("groups", "mp", "section"), None),
        P(("groups", "mp", "section"), "seq"),
    )
    out_specs = P(("groups", "mp", "section"), "seq", None)
    return jax.shard_map(layer, mesh=mesh, in_specs=in_specs, out_specs=out_specs, check_vma=False)
```
